32 devices in a mesh: dp: 4 (over y, x), sp: 8 (over z, core).
Axes of the slice: x: 2, y: 2, z: 4, core: 2. Of those that a mesh axis runs over, the one named last changes fastest.
Arguments:
- first_layer_input: bfloat16 [8, 1024, 1024], P('dp', 'sp'), may hold values from -6 to 6
- cotangent: bfloat16 [8, 1024, 1024], P('dp', 'sp'), may hold values from -6 to 6
- document_begin: int32 [8, 1024], P('dp'), may hold values from 0 to 1023, as said below
- query_key_value_weight: bfloat16 [2, 1024, 3072], P(None, 'dp'), may hold values from -0.1875 to 0.1875
- attention_out_weight: bfloat16 [2, 1024, 1024], P(None, 'dp'), may hold values from -0.5 to 0.5
- feedforward_in_weight: bfloat16 [2, 1024, 4096], P(None, 'dp'), may hold values from -0.1875 to 0.1875
- feedforward_out_weight: bfloat16 [2, 4096, 1024], P(None, 'dp'), may hold values from -0.09375 to 0.09375
- query_value_bias: float32 [2, 2, 1024], replicated, may hold values from -3 to 3
- attention_out_bias: float32 [2, 1024], replicated, may hold values from -2 to 2
- feedforward_in_bias: float32 [2, 4096], replicated, may hold values from -2 to 2
- feedforward_out_bias: float32 [2, 1024], replicated, may hold values from -2 to 2
- layernorm_gain: float32 [2, 2, 1024], replicated, may hold values from 0.25 to 1.75
- layernorm_bias: float32 [2, 2, 1024], replicated, may hold values from -2 to 2
- adapter_down_maps: float32 [2, 2, 4, 1024], replicated, may hold values from -0.1875 to 0.1875
- adapter_up_maps: float32 [2, 2, 4, 1024], replicated, may hold values from -0.3 to 0.3
Outputs:
- output: float32 [8, 1024, 1024], P('dp', 'sp')
- input_grad: float32 [8, 1024, 1024], P('dp', 'sp')
- grad_down: float32 [2, 2, 4, 1024], replicated
- grad_up: float32 [2, 2, 4, 1024], replicated
The draws below stay inside these ranges and needn't reach their ends.
Inputs may be any that keep to these rules, and one draw needn't show every extreme that they name: document_begin[s, t] is the first position of the document that holds token t of slot s: 0 at t = 0, never falling along a slot, equal to t where a document begins and constant inside a document. Of every aligned group of 2 slots, one is a single document; in every other slot the last token is a document of its own.
All inputs are finite; a program needn't handle non-finite values.
Results may differ from the reference program's by a relative error of at most 0.014.
Values may be sent and summed in bfloat16 or wider, within the bound.
A program may use at most 192 MiB of HBM per device.

```python
import math
import jax
import jax.numpy as jnp
from jax import lax

MODEL_DIM = 1024
HEAD_SIZE = 64
FF = 4096
ADAPTER_RANK = 4
LAYER_COUNT = 2
SEQ = 1024
SLOT_DEV = 2
SLOTS = 8
TOKENS = 8192


def draw_document_begin(key, part):
    mark_key, pick_key = jax.random.split(key)
    start_rate = max(SEQ // 8, 2)
    boundary = jax.random.randint(mark_key, (SLOTS, SEQ), 0, start_rate) == 0
    group_count = SLOTS // SLOT_DEV
    chosen = jax.random.randint(pick_key, (group_count, 1), 0, SLOT_DEV)
    member = jnp.arange(SLOT_DEV)[None, :] == chosen
    single = member.reshape(SLOTS, 1)
    places = jnp.arange(SEQ).astype(jnp.int32)[None, :]
    several = jnp.logical_not(single)
    boundary = (boundary | (places == SEQ - 1)) & several | (places == 0)
    document_starts = jnp.where(boundary, places, 0).astype(jnp.int32)
    return lax.cummax(document_starts, axis=1).astype(jnp.int32)


def shard_levels(key, extent, shards, smallest, top_value):
    loudness, own = 1.0, jax.random.fold_in(key, 6)
    for axis_at, shards_of in shards:
        heights = jnp.exp(jax.random.uniform(jax.random.fold_in(own, axis_at), (shards_of,), jnp.float32, smallest / len(shards), top_value / len(shards)))
        loudness = loudness * jnp.repeat(heights, extent[axis_at] // shards_of).reshape([-1 if axis == axis_at else 1 for axis in range(len(extent))])
    return loudness


def bell_draw(own_key, dims, scale, bound, cuts=(), kind=jnp.bfloat16):
    values = jax.random.normal(own_key, dims, jnp.float32) * scale
    if len(cuts) > 0:
        values = shard_levels(own_key, dims, cuts, -0.22, 0.18) * values
    return jnp.clip(values, min=-bound, max=bound).astype(kind)


def setup_inputs(seed: int = 0) -> dict:
    streams_of = jax.random.split(jax.random.key(seed), 16)
    return {
        "first_layer_input": bell_draw(streams_of[0], (SLOTS, SEQ, MODEL_DIM), 1.0, 6.0, ((0, 4), (1, 8))),
        "cotangent": bell_draw(streams_of[1], (SLOTS, SEQ, MODEL_DIM), 1.0, 6.0, ((0, 4), (1, 8))),
        "document_begin": draw_document_begin(jax.random.fold_in(streams_of[15], 71), 0),
        "query_key_value_weight": bell_draw(streams_of[3], (LAYER_COUNT, MODEL_DIM, 3 * MODEL_DIM), MODEL_DIM ** -0.5, 0.1875, ((1, 4),)),
        "attention_out_weight": bell_draw(streams_of[4], (LAYER_COUNT, MODEL_DIM, MODEL_DIM), (MODEL_DIM // 8) ** -0.5, 0.5, ((1, 4),)),
        "feedforward_in_weight": bell_draw(streams_of[5], (LAYER_COUNT, MODEL_DIM, FF), MODEL_DIM ** -0.5, 0.1875, ((1, 4),)),
        "feedforward_out_weight": bell_draw(streams_of[6], (LAYER_COUNT, FF, MODEL_DIM), FF ** -0.5, 0.09375, ((1, 4),)),
        "query_value_bias": bell_draw(streams_of[7], (LAYER_COUNT, 2, MODEL_DIM), 0.5, 3.0, (), jnp.float32),
        "attention_out_bias": bell_draw(streams_of[8], (LAYER_COUNT, MODEL_DIM), 0.3, 2.0, (), jnp.float32),
        "feedforward_in_bias": bell_draw(streams_of[9], (LAYER_COUNT, FF), 0.3, 2.0, (), jnp.float32),
        "feedforward_out_bias": bell_draw(streams_of[10], (LAYER_COUNT, MODEL_DIM), 0.3, 2.0, (), jnp.float32),
        "layernorm_gain": jnp.clip(1.0 + 0.15 * jax.random.normal(streams_of[11], (LAYER_COUNT, 2, MODEL_DIM), jnp.float32), 0.25, 1.75),
        "layernorm_bias": bell_draw(streams_of[12], (LAYER_COUNT, 2, MODEL_DIM), 0.3, 2.0, (), jnp.float32),
        "adapter_down_maps": bell_draw(streams_of[13], (LAYER_COUNT, 2, ADAPTER_RANK, MODEL_DIM), MODEL_DIM ** -0.5, 0.1875, (), jnp.float32),
        "adapter_up_maps": bell_draw(streams_of[14], (LAYER_COUNT, 2, ADAPTER_RANK, MODEL_DIM), 0.05, 0.3, (), jnp.float32),
    }


EPSILON = 1e-05
ADAPTER_ALPHA = 32.0
EXACT_PRECISION = lax.Precision.HIGHEST
MASKED = -1e+30

@jax.custom_vjp
def reduced_rank(v):
    return lax.optimization_barrier(v.astype(jnp.bfloat16)).astype(jnp.float32)

@jax.custom_vjp
def reduced_rank_back(v):
    return v

def low_keep(v):
    return (reduced_rank(v), None)

def low_pass(kept, grad):
    return (grad,)

def back_keep(v):
    return (v, None)

def back_low(kept, grad):
    return (reduced_rank(grad),)
reduced_rank.defvjp(low_keep, low_pass)
reduced_rank_back.defvjp(back_keep, back_low)

def layer_norm(tensor, gains, shifts):
    row_mean = lax.optimization_barrier(jnp.mean(tensor, -1, keepdims=True))
    centred = tensor - row_mean
    spread = lax.optimization_barrier(jnp.mean(centred * centred, -1, keepdims=True))
    return centred * lax.rsqrt(spread + EPSILON) * gains + shifts

def matrix_product(spec, left, right):
    return jnp.einsum(spec, left, right, precision=EXACT_PRECISION)

def slot_attention(slot_items):
    query_rows, key_rows, value_rows, document_starts = slot_items
    length = query_rows.shape[0]
    heads_q = query_rows.reshape(length, -1, HEAD_SIZE)
    heads_k = key_rows.reshape(length, -1, HEAD_SIZE)
    heads_v = value_rows.reshape(length, -1, HEAD_SIZE)
    scores = reduced_rank_back(matrix_product('qhd,khd->hqk', heads_q, heads_k))
    places = jnp.arange(length)
    allowed = (document_starts[:, None] == document_starts[None, :]) & (places[None, :] <= places[:, None])
    scores = jnp.where(allowed[None], scores, MASKED)
    row_max = lax.optimization_barrier(jnp.max(scores, -1, keepdims=True))
    exponents = jnp.exp(scores - row_max)
    probability = reduced_rank(exponents / lax.optimization_barrier(jnp.sum(exponents, -1, keepdims=True)))
    mixture = matrix_product('hqk,khd->qhd', probability, heads_v)
    return mixture.reshape(length, -1)

def layer_block(hidden_state, document_starts, weight_set, extra_items, down_projection, up_projection):
    query_key_value_weight, attention_out_weight, feedforward_in_weight, feedforward_out_weight = weight_set
    query_value_bias, attention_out_bias, feedforward_in_bias, feedforward_out_bias, gains, shifts = extra_items
    model_dimension = hidden_state.shape[-1]
    normed = reduced_rank(layer_norm(hidden_state, gains[0], shifts[0]))
    projected_rows = matrix_product('gsd,de->gse', normed, query_key_value_weight)
    adapter_scale = ADAPTER_ALPHA / down_projection.shape[1]
    query_row_block = matrix_product('gsd,rd->gsr', normed, down_projection[0])
    value_row_block = matrix_product('gsd,rd->gsr', normed, down_projection[1])
    query_rows = (projected_rows[..., :model_dimension] + query_value_bias[0] + adapter_scale * matrix_product('exc,ch->exh', query_row_block, up_projection[0])) * HEAD_SIZE ** (-0.5)
    query_rows = reduced_rank(reduced_rank_back(query_rows))
    key_rows = reduced_rank(reduced_rank_back(projected_rows[..., model_dimension:2 * model_dimension]))
    value_rows = reduced_rank(reduced_rank_back(projected_rows[..., 2 * model_dimension:] + query_value_bias[1] + adapter_scale * matrix_product('exc,ch->exh', value_row_block, up_projection[1])))
    mixture = lax.map(jax.checkpoint(slot_attention), (query_rows, key_rows, value_rows, document_starts))
    mixture = reduced_rank(reduced_rank_back(mixture))
    attended = hidden_state + reduced_rank_back(matrix_product('gsd,de->gse', mixture, attention_out_weight) + attention_out_bias)
    normed_mlp = reduced_rank(layer_norm(attended, gains[1], shifts[1]))
    pre_act = reduced_rank_back(matrix_product('gsd,df->gsf', normed_mlp, feedforward_in_weight) + feedforward_in_bias)
    activation = reduced_rank(jax.nn.gelu(pre_act, approximate=True))
    return attended + reduced_rank_back(matrix_product('gsf,fd->gsd', activation, feedforward_out_weight) + feedforward_out_bias)

def forward_pass(hidden_state, adapter_down_maps, adapter_up_maps, document_starts, frozen_params, extra_items):
    for layer_number in range(LAYER_COUNT):
        weight_set = tuple((matrix[layer_number] for matrix in frozen_params))
        layer_extra_items = tuple((table[layer_number] for table in extra_items))
        hidden_state = layer_block(hidden_state, document_starts, weight_set, layer_extra_items, adapter_down_maps[layer_number], adapter_up_maps[layer_number])
    return hidden_state

def reference(first_layer_input, cotangent, document_begin, query_key_value_weight, attention_out_weight, feedforward_in_weight, feedforward_out_weight, query_value_bias, attention_out_bias, feedforward_in_bias, feedforward_out_bias, layernorm_gain, layernorm_bias, adapter_down_maps, adapter_up_maps):
    frozen_params = (query_key_value_weight.astype(jnp.float32), attention_out_weight.astype(jnp.float32), feedforward_in_weight.astype(jnp.float32), feedforward_out_weight.astype(jnp.float32))
    extra_items = (query_value_bias, attention_out_bias, feedforward_in_bias, feedforward_out_bias, layernorm_gain, layernorm_bias)
    slot_group = math.gcd(SLOTS, 4)
    group_count = SLOTS // slot_group
    hidden_groups = first_layer_input.astype(jnp.float32).reshape(group_count, slot_group, SEQ, MODEL_DIM)
    cot_groups = cotangent.astype(jnp.float32).reshape(group_count, slot_group, SEQ, MODEL_DIM)
    start_groups = document_begin.reshape(group_count, slot_group, SEQ)

    def step(carry, group_items):
        hidden_portion, cot_part, start_part = group_items

        def run_model(hidden_x, down_x, up_x):
            return forward_pass(hidden_x, down_x, up_x, start_part, frozen_params, extra_items)
        final_result, pullback_function = jax.vjp(run_model, hidden_portion, adapter_down_maps, adapter_up_maps)
        grad_hidden, grad_d, grad_u = pullback_function(cot_part)
        return ((carry[0] + grad_d, carry[1] + grad_u), (final_result, grad_hidden))
    zero_fill = (jnp.zeros(adapter_down_maps.shape, jnp.float32), jnp.zeros(adapter_up_maps.shape, jnp.float32))
    sums, stacked = lax.scan(step, zero_fill, (hidden_groups, cot_groups, start_groups))
    token_scale = 1.0 / math.sqrt(TOKENS)
    return (stacked[0].reshape(SLOTS, SEQ, MODEL_DIM), stacked[1].reshape(SLOTS, SEQ, MODEL_DIM), sums[0] * token_scale, sums[1] * token_scale)
```

```python
from functools import partial
import math

import jax
import jax.numpy as jnp
from jax import lax
from jax.experimental import pallas as pl
from jax.experimental.pallas import tpu as pltpu
from jax.sharding import Mesh, PartitionSpec as P

HEAD_SIZE = 64


EPSILON = 1e-05
ADAPTER_ALPHA = 32.0
EXACT_PRECISION = lax.Precision.HIGHEST
MASKED = -1e30
SP = ("z", "core")


def layer_norm(tensor, gains, shifts):
    row_mean = jnp.mean(tensor, -1, keepdims=True)
    centred = tensor - row_mean
    spread = jnp.mean(centred * centred, -1, keepdims=True)
    return centred * lax.rsqrt(spread + EPSILON) * gains + shifts


def fetch_weights(
    query_key_value_weight,
    attention_out_weight,
    feedforward_in_weight,
    feedforward_out_weight,
    layer_number,
):
    core = lax.axis_index("core")

    def fetch(shards):
        half = shards.shape[1] // 2
        part = lax.dynamic_slice_in_dim(shards[layer_number], core * half, half, 0)
        return lax.all_gather(part, ("dp", "core"), axis=0, tiled=True)

    return (
        fetch(query_key_value_weight),
        fetch(attention_out_weight),
        fetch(feedforward_in_weight),
        fetch(feedforward_out_weight),
    )


def sum_kernel(sizes, terms_ref, out_ref, landing, send_sem, recv_sem, send_sem2, recv_sem2):
    count = math.prod(sizes)
    me = [lax.axis_index(name) for name in ("dp", "z", "core")]
    mine = (me[0] * sizes[1] + me[1]) * sizes[2] + me[2]

    def place(step):
        other = lax.rem(mine + step, count)
        return other, (
            other // (sizes[1] * sizes[2]),
            lax.rem(other // sizes[2], sizes[1]),
            lax.rem(other, sizes[2]),
        )

    barrier = pltpu.get_barrier_semaphore()
    for step in range(1, count):
        pl.semaphore_signal(
            barrier, inc=1, device_id=place(step)[1], device_id_type=pl.DeviceIdType.MESH
        )
    pl.semaphore_wait(barrier, count - 1)

    def scatter(step):
        other, device = place(step)
        return pltpu.make_async_remote_copy(
            src_ref=terms_ref.at[other],
            dst_ref=landing.at[step],
            send_sem=send_sem.at[step],
            recv_sem=recv_sem.at[step],
            device_id=device,
            device_id_type=pl.DeviceIdType.MESH,
        )

    def spread(step):
        other, device = place(step)
        return pltpu.make_async_remote_copy(
            src_ref=out_ref.at[mine],
            dst_ref=out_ref.at[mine],
            send_sem=send_sem2.at[step],
            recv_sem=recv_sem2.at[step],
            device_id=device,
            device_id_type=pl.DeviceIdType.MESH,
        )

    for step in range(1, count):
        scatter(step).start()
    landing[0] = terms_ref[mine]
    for step in range(1, count):
        scatter(step).wait()
    out_ref[mine] = jnp.sum(landing[...], axis=0)
    for step in range(1, count):
        spread(step).start()
    for step in range(1, count):
        spread(step).wait()


def sum_adapters(down_terms, up_terms):
    sizes = [lax.axis_size(name) for name in ("dp", "z", "core")]
    count = math.prod(sizes)
    packed = jnp.stack([down_terms, up_terms])
    if count > 64 or packed.size % (count * 1024) != 0:
        return lax.psum((down_terms, up_terms), ("dp", "z", "core"))
    pieces = packed.reshape(count, -1, 128)
    vmem = pl.BlockSpec(memory_space=pltpu.VMEM)
    summed = pl.pallas_call(
        partial(sum_kernel, sizes),
        out_shape=jax.ShapeDtypeStruct(pieces.shape, jnp.float32),
        in_specs=[vmem],
        out_specs=vmem,
        scratch_shapes=[pltpu.VMEM(pieces.shape, jnp.float32)]
        + [pltpu.SemaphoreType.DMA((count,))] * 4,
        name="adapter_sum",
        compiler_params=pltpu.CompilerParams(collective_id=0, has_side_effects=True),
    )(pieces)
    summed = summed.reshape(packed.shape)
    return summed[0], summed[1]


def slot_scores(query_rows, key_rows, document_starts):
    length = query_rows.shape[0]
    heads_q = query_rows.reshape(length, -1, HEAD_SIZE)
    heads_k = key_rows.reshape(length, -1, HEAD_SIZE)
    scores = jnp.einsum("qhd,khd->hqk", heads_q, heads_k, preferred_element_type=jnp.float32)
    places = jnp.arange(length)
    allowed = (document_starts[:, None] == document_starts[None, :]) & (
        places[None, :] <= places[:, None]
    )
    return jnp.where(allowed[None], scores, MASKED)


def slot_forward(slot_items):
    query_rows, key_rows, value_rows, document_starts = slot_items
    length = query_rows.shape[0]
    scores = slot_scores(query_rows, key_rows, document_starts)
    row_max = jnp.max(scores, -1, keepdims=True)
    row_total = jnp.sum(jnp.exp(scores - row_max), -1, keepdims=True)
    log_total = row_max + jnp.log(row_total)
    probability = jnp.exp(scores - log_total).astype(jnp.bfloat16)
    mixture = jnp.einsum(
        "hqk,khd->qhd",
        probability,
        value_rows.reshape(length, -1, HEAD_SIZE),
        preferred_element_type=jnp.float32,
    )
    return (mixture.reshape(length, -1).astype(jnp.bfloat16), log_total[..., 0])


def slot_backward(slot_items):
    query_rows, key_rows, value_rows, document_starts, log_total, grad_mixture = slot_items
    length = query_rows.shape[0]
    scores = slot_scores(query_rows, key_rows, document_starts)
    probability = jnp.exp(scores - log_total[..., None])
    low_probability = probability.astype(jnp.bfloat16)
    grad_heads = grad_mixture.reshape(length, -1, HEAD_SIZE)
    value_heads = value_rows.reshape(length, -1, HEAD_SIZE)
    grad_values = jnp.einsum(
        "hqk,qhd->khd", low_probability, grad_heads, preferred_element_type=jnp.float32
    )
    grad_prob = jnp.einsum(
        "qhd,khd->hqk", grad_heads, value_heads, preferred_element_type=jnp.float32
    )
    grad_scores = probability * (grad_prob - jnp.sum(probability * grad_prob, -1, keepdims=True))
    low_scores = grad_scores.astype(jnp.bfloat16)
    grad_queries = jnp.einsum(
        "hqk,khd->qhd",
        low_scores,
        key_rows.reshape(length, -1, HEAD_SIZE),
        preferred_element_type=jnp.float32,
    )
    grad_keys = jnp.einsum(
        "hqk,qhd->khd",
        low_scores,
        query_rows.reshape(length, -1, HEAD_SIZE),
        preferred_element_type=jnp.float32,
    )
    return (
        grad_queries.reshape(length, -1).astype(jnp.bfloat16),
        grad_keys.reshape(length, -1).astype(jnp.bfloat16),
        grad_values.reshape(length, -1).astype(jnp.bfloat16),
    )


def layer_forward(hidden_state, weight_set, params, document_begin):
    query_key_value_weight, attention_out_weight, feedforward_in_weight, feedforward_out_weight = (
        weight_set
    )
    (
        query_value_bias,
        attention_out_bias,
        feedforward_in_bias,
        feedforward_out_bias,
        gains,
        shifts,
        down_projection,
        up_projection,
    ) = params
    model_dimension = hidden_state.shape[-1]
    normed = layer_norm(hidden_state, gains[0], shifts[0]).astype(jnp.bfloat16)
    projected_rows = jnp.einsum(
        "std,de->ste", normed, query_key_value_weight, preferred_element_type=jnp.float32
    )
    widened = normed.astype(jnp.float32)
    adapter_scale = ADAPTER_ALPHA / down_projection.shape[1]
    query_row_block = jnp.einsum(
        "nyh,lh->nyl", widened, down_projection[0], precision=EXACT_PRECISION
    )
    value_row_block = jnp.einsum(
        "nyh,lh->nyl", widened, down_projection[1], precision=EXACT_PRECISION
    )
    query_rows = (
        (
            projected_rows[..., :model_dimension]
            + query_value_bias[0]
            + adapter_scale
            * jnp.einsum(
                "wah,hp->wap", query_row_block, up_projection[0], precision=EXACT_PRECISION
            )
        )
        * HEAD_SIZE ** (-0.5)
    ).astype(jnp.bfloat16)
    key_rows = projected_rows[..., model_dimension : 2 * model_dimension].astype(jnp.bfloat16)
    value_rows = (
        projected_rows[..., 2 * model_dimension :]
        + query_value_bias[1]
        + adapter_scale
        * jnp.einsum("wah,hp->wap", value_row_block, up_projection[1], precision=EXACT_PRECISION)
    ).astype(jnp.bfloat16)
    queries_h, keys_h, values_h = lax.all_to_all(
        jnp.stack([query_rows, key_rows, value_rows]), SP, split_axis=3, concat_axis=2, tiled=True
    )
    mixture_h, log_total = lax.map(slot_forward, (queries_h, keys_h, values_h, document_begin))
    mixture = lax.all_to_all(mixture_h, SP, split_axis=1, concat_axis=2, tiled=True)
    attended = hidden_state + (
        jnp.einsum("std,de->ste", mixture, attention_out_weight, preferred_element_type=jnp.float32)
        + attention_out_bias
    )
    normed_mlp = layer_norm(attended, gains[1], shifts[1]).astype(jnp.bfloat16)
    pre_act = (
        jnp.einsum(
            "std,df->stf", normed_mlp, feedforward_in_weight, preferred_element_type=jnp.float32
        )
        + feedforward_in_bias
    )
    activation = jax.nn.gelu(pre_act, approximate=True).astype(jnp.bfloat16)
    final_result = attended + (
        jnp.einsum(
            "stf,fd->std", activation, feedforward_out_weight, preferred_element_type=jnp.float32
        )
        + feedforward_out_bias
    )
    saved_state = (
        normed,
        query_row_block,
        value_row_block,
        queries_h,
        keys_h,
        values_h,
        log_total,
        attended,
        pre_act,
    )
    return (final_result, saved_state)


def layer_backward(hidden_state, gradient, weight_set, params, document_begin, saved_state):
    query_key_value_weight, attention_out_weight, feedforward_in_weight, feedforward_out_weight = (
        weight_set
    )
    (
        query_value_bias,
        attention_out_bias,
        feedforward_in_bias,
        feedforward_out_bias,
        gains,
        shifts,
        down_projection,
        up_projection,
    ) = params
    (
        normed,
        query_row_block,
        value_row_block,
        queries_h,
        keys_h,
        values_h,
        log_total,
        attended,
        pre_act,
    ) = saved_state
    grad_act = jnp.einsum(
        "std,fd->stf",
        gradient.astype(jnp.bfloat16),
        feedforward_out_weight,
        preferred_element_type=jnp.float32,
    )
    unused_act, gelu_back = jax.vjp(partial(jax.nn.gelu, approximate=True), pre_act)
    grad_pre = gelu_back(grad_act)[0].astype(jnp.bfloat16)
    grad_normed_mlp = jnp.einsum(
        "stf,df->std", grad_pre, feedforward_in_weight, preferred_element_type=jnp.float32
    )
    unused_norm, second_back = jax.vjp(
        lambda tensor: layer_norm(tensor, gains[1], shifts[1]), attended
    )
    grad_attended = gradient + second_back(grad_normed_mlp)[0]
    grad_mixture = jnp.einsum(
        "ste,de->std",
        grad_attended.astype(jnp.bfloat16),
        attention_out_weight,
        preferred_element_type=jnp.float32,
    ).astype(jnp.bfloat16)
    grad_mixture_h = lax.all_to_all(grad_mixture, SP, split_axis=2, concat_axis=1, tiled=True)
    grad_q_h, grad_k_h, grad_v_h = lax.map(
        slot_backward, (queries_h, keys_h, values_h, document_begin, log_total, grad_mixture_h)
    )
    grad_queries, grad_keys, grad_values = lax.all_to_all(
        jnp.stack([grad_q_h, grad_k_h, grad_v_h]), SP, split_axis=2, concat_axis=3, tiled=True
    )
    grad_queries = grad_queries * jnp.asarray(HEAD_SIZE ** (-0.5), jnp.bfloat16)
    stacked = jnp.concatenate([grad_queries, grad_keys, grad_values], -1)
    grad_normed = jnp.einsum(
        "ste,de->std", stacked, query_key_value_weight, preferred_element_type=jnp.float32
    )
    adapter_scale = ADAPTER_ALPHA / down_projection.shape[1]
    widened = normed.astype(jnp.float32)
    query_widened = grad_queries.astype(jnp.float32)
    value_widened = grad_values.astype(jnp.float32)
    query_row_gradient = adapter_scale * jnp.einsum(
        "nyh,lh->nyl", query_widened, up_projection[0], precision=EXACT_PRECISION
    )
    value_row_gradient = adapter_scale * jnp.einsum(
        "nyh,lh->nyl", value_widened, up_projection[1], precision=EXACT_PRECISION
    )
    query_up_weight = adapter_scale * jnp.einsum(
        "fkp,fkz->pz", query_row_block, query_widened, precision=EXACT_PRECISION
    )
    value_up_weight = adapter_scale * jnp.einsum(
        "fkp,fkz->pz", value_row_block, value_widened, precision=EXACT_PRECISION
    )
    down_q = jnp.einsum("fkp,fkz->pz", query_row_gradient, widened, precision=EXACT_PRECISION)
    down_v = jnp.einsum("fkp,fkz->pz", value_row_gradient, widened, precision=EXACT_PRECISION)
    grad_normed = (
        grad_normed
        + jnp.einsum(
            "wah,hp->wap", query_row_gradient, down_projection[0], precision=EXACT_PRECISION
        )
        + jnp.einsum(
            "wah,hp->wap", value_row_gradient, down_projection[1], precision=EXACT_PRECISION
        )
    )
    unused_first, first_back = jax.vjp(
        lambda tensor: layer_norm(tensor, gains[0], shifts[0]), hidden_state
    )
    grad_hidden = grad_attended + first_back(grad_normed)[0]
    return (grad_hidden, jnp.stack([down_q, down_v]), jnp.stack([query_up_weight, value_up_weight]))


def body(
    first_layer_input,
    cotangent,
    document_begin,
    query_key_value_weight,
    attention_out_weight,
    feedforward_in_weight,
    feedforward_out_weight,
    query_value_bias,
    attention_out_bias,
    feedforward_in_bias,
    feedforward_out_bias,
    layernorm_gain,
    layernorm_bias,
    adapter_down_maps,
    adapter_up_maps,
):
    layers = query_key_value_weight.shape[0]

    def params_of(layer_number):
        return (
            query_value_bias[layer_number],
            attention_out_bias[layer_number],
            feedforward_in_bias[layer_number],
            feedforward_out_bias[layer_number],
            layernorm_gain[layer_number],
            layernorm_bias[layer_number],
            adapter_down_maps[layer_number],
            adapter_up_maps[layer_number],
        )

    hidden_state = first_layer_input.astype(jnp.float32)
    inputs = []
    gathered = []
    kept = []
    for layer_number in range(layers):
        weight_set = fetch_weights(
            query_key_value_weight,
            attention_out_weight,
            feedforward_in_weight,
            feedforward_out_weight,
            layer_number,
        )
        inputs.append(hidden_state)
        gathered.append(weight_set)
        hidden_state, saved_state = layer_forward(
            hidden_state, weight_set, params_of(layer_number), document_begin
        )
        kept.append(saved_state)
    gradient = cotangent.astype(jnp.float32)
    down_parts = [None] * layers
    up_parts = [None] * layers
    for layer_number in reversed(range(layers)):
        gradient, down_terms, up_terms = layer_backward(
            inputs[layer_number],
            gradient,
            gathered[layer_number],
            params_of(layer_number),
            document_begin,
            kept[layer_number],
        )
        down_parts[layer_number] = down_terms
        up_parts[layer_number] = up_terms
    grad_down = jnp.stack(down_parts)
    grad_up = jnp.stack(up_parts)
    grad_down, grad_up = sum_adapters(grad_down, grad_up)
    tokens = (
        first_layer_input.shape[0]
        * first_layer_input.shape[1]
        * lax.axis_size("dp")
        * lax.axis_size("z")
        * lax.axis_size("core")
    )
    token_scale = 1.0 / math.sqrt(tokens)
    return (hidden_state, gradient, grad_down * token_scale, grad_up * token_scale)


def solution(mesh):
    rows, columns = mesh.devices.shape
    mesh = Mesh(mesh.devices.reshape(rows, columns // 2, 2), ("dp",) + SP)
    placed = (
        P("dp", SP, None),
        P("dp", SP, None),
        P("dp", None),
        P(None, "dp", None),
        P(None, "dp", None),
        P(None, "dp", None),
        P(None, "dp", None),
        P(),
        P(),
        P(),
        P(),
        P(),
        P(),
        P(),
        P(),
    )
    return jax.shard_map(
        body,
        mesh=mesh,
        in_specs=placed,
        out_specs=(P("dp", SP, None), P("dp", SP, None), P(), P()),
        check_vma=False,
    )
```

```python
from functools import partial
import math

import jax
import jax.numpy as jnp
from jax import lax
from jax.experimental import pallas as pl
from jax.experimental.pallas import tpu as pltpu
from jax.sharding import Mesh, PartitionSpec as P

HEAD_SIZE = 64


EPSILON = 1e-05
ADAPTER_ALPHA = 32.0
EXACT_PRECISION = lax.Precision.HIGHEST
MASKED = -1e30
SP = ("z", "core")


def layer_norm(tensor, gains, shifts):
    row_mean = jnp.mean(tensor, -1, keepdims=True)
    centred = tensor - row_mean
    spread = jnp.mean(centred * centred, -1, keepdims=True)
    return centred * lax.rsqrt(spread + EPSILON) * gains + shifts


def fetch_weights(
    query_key_value_weight,
    attention_out_weight,
    feedforward_in_weight,
    feedforward_out_weight,
    layer_number,
):
    core = lax.axis_index("core")

    def fetch(shards):
        half = shards.shape[1] // 2
        part = lax.dynamic_slice_in_dim(shards[layer_number], core * half, half, 0)
        return lax.all_gather(part, ("dp", "core"), axis=0, tiled=True)

    return (
        fetch(query_key_value_weight),
        fetch(attention_out_weight),
        fetch(feedforward_in_weight),
        fetch(feedforward_out_weight),
    )


def sum_kernel(sizes, terms_ref, out_ref, landing, send_sem, recv_sem, send_sem2, recv_sem2):
    count = math.prod(sizes)
    me = [lax.axis_index(name) for name in ("dp", "z", "core")]
    mine = (me[0] * sizes[1] + me[1]) * sizes[2] + me[2]

    def place(step):
        other = lax.rem(mine + step, count)
        return other, (
            other // (sizes[1] * sizes[2]),
            lax.rem(other // sizes[2], sizes[1]),
            lax.rem(other, sizes[2]),
        )

    barrier = pltpu.get_barrier_semaphore()
    for step in range(1, count):
        pl.semaphore_signal(
            barrier, inc=1, device_id=place(step)[1], device_id_type=pl.DeviceIdType.MESH
        )
    pl.semaphore_wait(barrier, count - 1)

    def scatter(step):
        other, device = place(step)
        return pltpu.make_async_remote_copy(
            src_ref=terms_ref.at[other],
            dst_ref=landing.at[step],
            send_sem=send_sem.at[step],
            recv_sem=recv_sem.at[step],
            device_id=device,
            device_id_type=pl.DeviceIdType.MESH,
        )

    def spread(step):
        other, device = place(step)
        return pltpu.make_async_remote_copy(
            src_ref=out_ref.at[mine],
            dst_ref=out_ref.at[mine],
            send_sem=send_sem2.at[step],
            recv_sem=recv_sem2.at[step],
            device_id=device,
            device_id_type=pl.DeviceIdType.MESH,
        )

    for step in range(1, count):
        scatter(step).start()
    landing[0] = terms_ref[mine]
    for step in range(1, count):
        scatter(step).wait()
    out_ref[mine] = jnp.sum(landing[...], axis=0)
    for step in range(1, count):
        spread(step).start()
    for step in range(1, count):
        spread(step).wait()


def sum_adapters(down_terms, up_terms):
    sizes = [lax.axis_size(name) for name in ("dp", "z", "core")]
    count = math.prod(sizes)
    packed = jnp.stack([down_terms, up_terms])
    if count > 64 or packed.size % (count * 1024) != 0:
        return lax.psum((down_terms, up_terms), ("dp", "z", "core"))
    pieces = packed.reshape(count, -1, 128)
    vmem = pl.BlockSpec(memory_space=pltpu.VMEM)
    summed = pl.pallas_call(
        partial(sum_kernel, sizes),
        out_shape=jax.ShapeDtypeStruct(pieces.shape, jnp.float32),
        in_specs=[vmem],
        out_specs=vmem,
        scratch_shapes=[pltpu.VMEM(pieces.shape, jnp.float32)]
        + [pltpu.SemaphoreType.DMA((count,))] * 4,
        name="adapter_sum",
        compiler_params=pltpu.CompilerParams(collective_id=0, has_side_effects=True),
    )(pieces)
    summed = summed.reshape(packed.shape)
    return summed[0], summed[1]


def slot_scores(query_rows, key_rows, document_starts):
    length = query_rows.shape[0]
    heads_q = query_rows.reshape(length, -1, HEAD_SIZE)
    heads_k = key_rows.reshape(length, -1, HEAD_SIZE)
    scores = jnp.einsum("qhd,khd->hqk", heads_q, heads_k, preferred_element_type=jnp.float32)
    places = jnp.arange(length)
    allowed = (document_starts[:, None] == document_starts[None, :]) & (
        places[None, :] <= places[:, None]
    )
    return jnp.where(allowed[None], scores, MASKED)


def slot_forward(slot_items):
    query_rows, key_rows, value_rows, document_starts = slot_items
    length = query_rows.shape[0]
    scores = slot_scores(query_rows, key_rows, document_starts)
    row_max = jnp.max(scores, -1, keepdims=True)
    row_total = jnp.sum(jnp.exp(scores - row_max), -1, keepdims=True)
    log_total = row_max + jnp.log(row_total)
    probability = jnp.exp(scores - log_total).astype(jnp.bfloat16)
    mixture = jnp.einsum(
        "hqk,khd->qhd",
        probability,
        value_rows.reshape(length, -1, HEAD_SIZE),
        preferred_element_type=jnp.float32,
    )
    return (mixture.reshape(length, -1).astype(jnp.bfloat16), log_total[..., 0])


def slot_backward(slot_items):
    query_rows, key_rows, value_rows, document_starts, log_total, grad_mixture = slot_items
    length = query_rows.shape[0]
    scores = slot_scores(query_rows, key_rows, document_starts)
    probability = jnp.exp(scores - log_total[..., None])
    low_probability = probability.astype(jnp.bfloat16)
    grad_heads = grad_mixture.reshape(length, -1, HEAD_SIZE)
    value_heads = value_rows.reshape(length, -1, HEAD_SIZE)
    grad_values = jnp.einsum(
        "hqk,qhd->khd", low_probability, grad_heads, preferred_element_type=jnp.float32
    )
    grad_prob = jnp.einsum(
        "qhd,khd->hqk", grad_heads, value_heads, preferred_element_type=jnp.float32
    )
    grad_scores = probability * (grad_prob - jnp.sum(probability * grad_prob, -1, keepdims=True))
    low_scores = grad_scores.astype(jnp.bfloat16)
    grad_queries = jnp.einsum(
        "hqk,khd->qhd",
        low_scores,
        key_rows.reshape(length, -1, HEAD_SIZE),
        preferred_element_type=jnp.float32,
    )
    grad_keys = jnp.einsum(
        "hqk,qhd->khd",
        low_scores,
        query_rows.reshape(length, -1, HEAD_SIZE),
        preferred_element_type=jnp.float32,
    )
    return (
        grad_queries.reshape(length, -1).astype(jnp.bfloat16),
        grad_keys.reshape(length, -1).astype(jnp.bfloat16),
        grad_values.reshape(length, -1).astype(jnp.bfloat16),
    )


def layer_forward(hidden_state, weight_set, params, document_begin):
    query_key_value_weight, attention_out_weight, feedforward_in_weight, feedforward_out_weight = (
        weight_set
    )
    (
        query_value_bias,
        attention_out_bias,
        feedforward_in_bias,
        feedforward_out_bias,
        gains,
        shifts,
        down_projection,
        up_projection,
    ) = params
    model_dimension = hidden_state.shape[-1]
    normed = layer_norm(hidden_state, gains[0], shifts[0]).astype(jnp.bfloat16)
    projected_rows = jnp.einsum(
        "std,de->ste", normed, query_key_value_weight, preferred_element_type=jnp.float32
    )
    widened = normed.astype(jnp.float32)
    adapter_scale = ADAPTER_ALPHA / down_projection.shape[1]
    query_row_block = jnp.einsum(
        "nyh,lh->nyl", widened, down_projection[0], precision=EXACT_PRECISION
    )
    value_row_block = jnp.einsum(
        "nyh,lh->nyl", widened, down_projection[1], precision=EXACT_PRECISION
    )
    query_rows = (
        (
            projected_rows[..., :model_dimension]
            + query_value_bias[0]
            + adapter_scale
            * jnp.einsum(
                "wah,hp->wap", query_row_block, up_projection[0], precision=EXACT_PRECISION
            )
        )
        * HEAD_SIZE ** (-0.5)
    ).astype(jnp.bfloat16)
    key_rows = projected_rows[..., model_dimension : 2 * model_dimension].astype(jnp.bfloat16)
    value_rows = (
        projected_rows[..., 2 * model_dimension :]
        + query_value_bias[1]
        + adapter_scale
        * jnp.einsum("wah,hp->wap", value_row_block, up_projection[1], precision=EXACT_PRECISION)
    ).astype(jnp.bfloat16)
    queries_h, keys_h, values_h = lax.all_to_all(
        jnp.stack([query_rows, key_rows, value_rows]), SP, split_axis=3, concat_axis=2, tiled=True
    )
    mixture_h, log_total = lax.map(slot_forward, (queries_h, keys_h, values_h, document_begin))
    mixture = lax.all_to_all(mixture_h, SP, split_axis=1, concat_axis=2, tiled=True)
    attended = hidden_state + (
        jnp.einsum("std,de->ste", mixture, attention_out_weight, preferred_element_type=jnp.float32)
        + attention_out_bias
    )
    normed_mlp = layer_norm(attended, gains[1], shifts[1]).astype(jnp.bfloat16)
    pre_act = (
        jnp.einsum(
            "std,df->stf", normed_mlp, feedforward_in_weight, preferred_element_type=jnp.float32
        )
        + feedforward_in_bias
    )
    activation = jax.nn.gelu(pre_act, approximate=True).astype(jnp.bfloat16)
    final_result = attended + (
        jnp.einsum(
            "stf,fd->std", activation, feedforward_out_weight, preferred_element_type=jnp.float32
        )
        + feedforward_out_bias
    )
    saved_state = (
        normed,
        query_row_block,
        value_row_block,
        queries_h,
        keys_h,
        values_h,
        log_total,
        attended,
        pre_act,
    )
    return (final_result, saved_state)


def layer_backward(hidden_state, gradient, weight_set, params, document_begin, saved_state):
    query_key_value_weight, attention_out_weight, feedforward_in_weight, feedforward_out_weight = (
        weight_set
    )
    (
        query_value_bias,
        attention_out_bias,
        feedforward_in_bias,
        feedforward_out_bias,
        gains,
        shifts,
        down_projection,
        up_projection,
    ) = params
    (
        normed,
        query_row_block,
        value_row_block,
        queries_h,
        keys_h,
        values_h,
        log_total,
        attended,
        pre_act,
    ) = saved_state
    grad_act = jnp.einsum(
        "std,fd->stf",
        gradient.astype(jnp.bfloat16),
        feedforward_out_weight,
        preferred_element_type=jnp.float32,
    )
    unused_act, gelu_back = jax.vjp(partial(jax.nn.gelu, approximate=True), pre_act)
    grad_pre = gelu_back(grad_act)[0].astype(jnp.bfloat16)
    grad_normed_mlp = jnp.einsum(
        "stf,df->std", grad_pre, feedforward_in_weight, preferred_element_type=jnp.float32
    )
    unused_norm, second_back = jax.vjp(
        lambda tensor: layer_norm(tensor, gains[1], shifts[1]), attended
    )
    grad_attended = gradient + second_back(grad_normed_mlp)[0]
    grad_mixture = jnp.einsum(
        "ste,de->std",
        grad_attended.astype(jnp.bfloat16),
        attention_out_weight,
        preferred_element_type=jnp.float32,
    ).astype(jnp.bfloat16)
    grad_mixture_h = lax.all_to_all(grad_mixture, SP, split_axis=2, concat_axis=1, tiled=True)
    grad_q_h, grad_k_h, grad_v_h = lax.map(
        slot_backward, (queries_h, keys_h, values_h, document_begin, log_total, grad_mixture_h)
    )
    grad_queries, grad_keys, grad_values = lax.all_to_all(
        jnp.stack([grad_q_h, grad_k_h, grad_v_h]), SP, split_axis=2, concat_axis=3, tiled=True
    )
    grad_queries = grad_queries * jnp.asarray(HEAD_SIZE ** (-0.5), jnp.bfloat16)
    stacked = jnp.concatenate([grad_queries, grad_keys, grad_values], -1)
    grad_normed = jnp.einsum(
        "ste,de->std", stacked, query_key_value_weight, preferred_element_type=jnp.float32
    )
    adapter_scale = ADAPTER_ALPHA / down_projection.shape[1]
    widened = normed.astype(jnp.float32)
    query_widened = grad_queries.astype(jnp.float32)
    value_widened = grad_values.astype(jnp.float32)
    query_row_gradient = adapter_scale * jnp.einsum(
        "nyh,lh->nyl", query_widened, up_projection[0], precision=EXACT_PRECISION
    )
    value_row_gradient = adapter_scale * jnp.einsum(
        "nyh,lh->nyl", value_widened, up_projection[1], precision=EXACT_PRECISION
    )
    query_up_weight = adapter_scale * jnp.einsum(
        "fkp,fkz->pz", query_row_block, query_widened, precision=EXACT_PRECISION
    )
    value_up_weight = adapter_scale * jnp.einsum(
        "fkp,fkz->pz", value_row_block, value_widened, precision=EXACT_PRECISION
    )
    down_q = jnp.einsum("fkp,fkz->pz", query_row_gradient, widened, precision=EXACT_PRECISION)
    down_v = jnp.einsum("fkp,fkz->pz", value_row_gradient, widened, precision=EXACT_PRECISION)
    grad_normed = (
        grad_normed
        + jnp.einsum(
            "wah,hp->wap", query_row_gradient, down_projection[0], precision=EXACT_PRECISION
        )
        + jnp.einsum(
            "wah,hp->wap", value_row_gradient, down_projection[1], precision=EXACT_PRECISION
        )
    )
    unused_first, first_back = jax.vjp(
        lambda tensor: layer_norm(tensor, gains[0], shifts[0]), hidden_state
    )
    grad_hidden = grad_attended + first_back(grad_normed)[0]
    return (grad_hidden, jnp.stack([down_q, down_v]), jnp.stack([query_up_weight, value_up_weight]))


def body(
    first_layer_input,
    cotangent,
    document_begin,
    query_key_value_weight,
    attention_out_weight,
    feedforward_in_weight,
    feedforward_out_weight,
    query_value_bias,
    attention_out_bias,
    feedforward_in_bias,
    feedforward_out_bias,
    layernorm_gain,
    layernorm_bias,
    adapter_down_maps,
    adapter_up_maps,
):
    layers = query_key_value_weight.shape[0]

    def params_of(layer_number):
        return (
            query_value_bias[layer_number],
            attention_out_bias[layer_number],
            feedforward_in_bias[layer_number],
            feedforward_out_bias[layer_number],
            layernorm_gain[layer_number],
            layernorm_bias[layer_number],
            adapter_down_maps[layer_number],
            adapter_up_maps[layer_number],
        )

    hidden_state = first_layer_input.astype(jnp.float32)
    inputs = []
    gathered = []
    kept = []
    for layer_number in range(layers):
        weight_set = fetch_weights(
            query_key_value_weight,
            attention_out_weight,
            feedforward_in_weight,
            feedforward_out_weight,
            layer_number,
        )
        inputs.append(hidden_state)
        gathered.append(weight_set)
        hidden_state, saved_state = layer_forward(
            hidden_state, weight_set, params_of(layer_number), document_begin
        )
        kept.append(saved_state)
    gradient = cotangent.astype(jnp.float32)
    down_parts = [None] * layers
    up_parts = [None] * layers
    for layer_number in reversed(range(layers)):
        gradient, down_terms, up_terms = layer_backward(
            inputs[layer_number],
            gradient,
            gathered[layer_number],
            params_of(layer_number),
            document_begin,
            kept[layer_number],
        )
        down_parts[layer_number] = down_terms
        up_parts[layer_number] = up_terms
    grad_down = jnp.stack(down_parts)
    grad_up = jnp.stack(up_parts)
    grad_down, grad_up = sum_adapters(grad_down, grad_up)
    tokens = (
        first_layer_input.shape[0]
        * first_layer_input.shape[1]
        * lax.axis_size("dp")
        * lax.axis_size("z")
        * lax.axis_size("core")
    )
    token_scale = 1.0 / math.sqrt(tokens)
    return (hidden_state, gradient, grad_down * token_scale, grad_up * token_scale)


MESH = pl.DeviceIdType.MESH
BLOCK = 256
TILE = 512
VMEM_LIMIT = 60 * 1024 * 1024


def dot_nn(left, right):
    return jnp.dot(left, right, preferred_element_type=jnp.float32)


def dot_nt(left, right):
    return lax.dot_general(
        left, right, (((1,), (1,)), ((), ())), preferred_element_type=jnp.float32
    )


def dot_tn(left, right):
    return lax.dot_general(
        left, right, (((0,), (0,)), ((), ())), preferred_element_type=jnp.float32
    )


def normalize(tensor):
    centred = tensor - jnp.mean(tensor, -1, keepdims=True)
    spread = jnp.mean(centred * centred, -1, keepdims=True)
    scale = lax.rsqrt(spread + EPSILON)
    return centred * scale, scale


def norm_backward(tensor, gains, gradient):
    unit, scale = normalize(tensor)
    weighted = gradient * gains
    first = jnp.mean(weighted, -1, keepdims=True)
    second = jnp.mean(weighted * unit, -1, keepdims=True)
    return scale * (weighted - first - unit * second)


GELU_INNER = math.sqrt(2.0 / math.pi)
GELU_CUBE = 0.044715


def gelu(value):
    inner = GELU_INNER * (value + GELU_CUBE * (value * value * value))
    return 0.5 * value * (1.0 + jnp.tanh(inner))


def gelu_slope(value):
    square = value * value
    bend = jnp.tanh(GELU_INNER * (value + GELU_CUBE * (square * value)))
    climb = GELU_INNER * (1.0 + 3.0 * GELU_CUBE * square)
    return 0.5 * (1.0 + bend) + 0.5 * value * (1.0 - bend * bend) * climb


def split_heads(rows):
    heads = rows.shape[1] // HEAD_SIZE
    owner = lax.broadcasted_iota(jnp.int32, rows.shape, 1) // HEAD_SIZE
    return jnp.concatenate(
        [jnp.where(owner == head, rows, jnp.zeros_like(rows)) for head in range(heads)], 0
    )


def join_heads(stacked, length):
    heads = stacked.shape[1] // HEAD_SIZE
    owner = lax.broadcasted_iota(jnp.int32, (length, stacked.shape[1]), 1) // HEAD_SIZE
    joined = stacked[:length]
    for head in range(1, heads):
        joined = jnp.where(owner == head, stacked[head * length : (head + 1) * length], joined)
    return joined


def allowed_pairs(key_block, query_block, begin_row, heads):
    shape = (BLOCK, heads * BLOCK)
    key_place = key_block * BLOCK + lax.broadcasted_iota(jnp.int32, shape, 0)
    column = lax.broadcasted_iota(jnp.int32, (1, heads * BLOCK), 1)
    query_place = query_block * BLOCK + lax.rem(column, BLOCK)
    return (key_place >= begin_row) & (key_place <= query_place)


def greet(peers):
    barrier = pltpu.get_barrier_semaphore()
    for peer in peers:
        pl.semaphore_signal(barrier, inc=1, device_id=peer, device_id_type=MESH)
    pl.semaphore_wait(barrier, len(peers))


def remote(source, target, send_sem, recv_sem, device):
    return pltpu.make_async_remote_copy(
        src_ref=source,
        dst_ref=target,
        send_sem=send_sem,
        recv_sem=recv_sem,
        device_id=device,
        device_id_type=MESH,
    )


def stream(count, copies, body):
    for copy in copies(0, 0):
        copy.start()

    def step(index, carry):
        slot = lax.rem(index, 2)

        @pl.when(index + 1 < count)
        def _():
            for copy in copies(index + 1, 1 - slot):
                copy.start()

        for copy in copies(index, slot):
            copy.wait()
        body(index, slot)
        return carry

    lax.fori_loop(0, count, step, 0)


def at_columns(index, size):
    return pl.ds(pl.multiple_of(index * size, size), size)


class Gather:
    def __init__(self, shard, full, shards, chip, lane, sems):
        self.shard, self.full = shard, full
        self.rows = shard.shape[0]
        self.chip, self.core = chip, lax.rem(lane, 2)
        self.next_x = chip + 1 - 2 * lax.rem(chip, 2)
        self.next_y = lax.rem(chip + 2, shards)
        self.far = shards - 1 - chip
        self.to_x, self.to_y = (self.next_x, lane), (self.next_y, lane)
        self.to_core = (chip, lane + 1 - 2 * self.core)
        self.send_sem, self.recv_sem, self.core_send, self.core_recv, self.own_sem = sems

    def quarter(self, owner, part):
        size = self.rows // 4
        start = self.core * (2 * size) + part * size
        if owner is None:
            return self.shard.at[pl.ds(pl.multiple_of(start, size), size)]
        return self.full.at[pl.ds(pl.multiple_of(owner * self.rows + start, size), size)]

    def hop(self, index):
        source, owner, part, device = (
            (None, self.chip, 0, self.to_x),
            (None, self.chip, 1, self.to_y),
            (None, self.chip, 0, self.to_y),
            (None, self.chip, 1, self.to_x),
            (self.next_x, self.next_x, 0, self.to_y),
            (self.next_y, self.next_y, 1, self.to_x),
        )[index]
        return remote(
            self.quarter(source, part),
            self.quarter(owner, part),
            self.send_sem.at[index],
            self.recv_sem.at[index],
            device,
        )

    def across(self, index):
        owner = (self.next_x, self.next_y, self.far)[index]
        size = self.rows // 2
        start = pl.multiple_of(owner * self.rows + self.core * size, size)
        half = self.full.at[pl.ds(start, size)]
        return remote(
            half, half, self.core_send.at[index], self.core_recv.at[index], self.to_core
        )

    def own(self):
        start = pl.multiple_of(self.chip * self.rows, self.rows)
        return pltpu.make_async_copy(
            self.shard, self.full.at[pl.ds(start, self.rows)], self.own_sem
        )

    def begin(self):
        for index in range(4):
            self.hop(index).start()

    def pass_on(self):
        self.hop(0).wait_recv()
        self.hop(4).start()
        self.hop(1).wait_recv()
        self.hop(5).start()

    def cross(self):
        self.hop(3).wait_recv()
        self.across(0).start()
        self.hop(2).wait_recv()
        self.across(1).start()
        self.hop(4).wait_recv()
        self.hop(5).wait_recv()
        self.across(2).start()

    def arrive(self):
        for index in range(3):
            self.across(index).wait_recv()
        self.own().wait()

    def drain(self):
        for index in range(6):
            self.hop(index).wait_send()
        for index in range(3):
            self.across(index).wait_send()


def forward_kernel(
    layer,
    sizes,
    hidden,
    begin,
    shard_qkv,
    shard_out,
    shard_in,
    shard_back,
    qkv_bias,
    out_bias,
    in_bias,
    back_bias,
    gains,
    shifts,
    down,
    up,
    result,
    normed,
    low_rank,
    heads_in,
    mixed,
    log_total,
    attended,
    pre_act,
    full_qkv,
    full_out,
    full_in,
    full_back,
    tile_in,
    tile_back,
    out_weight,
    heads_out,
    mixture,
    scores,
    activation,
    total,
    tile_sem,
    out_sem,
    heads_send,
    heads_recv,
    mix_send,
    mix_recv,
    hop_send,
    hop_recv,
    core_send,
    core_recv,
    own_sem,
):
    chips, lanes = sizes
    chip, lane = lax.axis_index("dp"), lax.axis_index("sp")
    slots, length, width = heads_in.shape[2:]
    heads = width // HEAD_SIZE
    rows, model = hidden.shape
    hidden_units = in_bias.shape[1]
    blocks = lanes * length // BLOCK
    per_block = BLOCK // length

    def others():
        return [lax.rem(lane + step, lanes) for step in range(1, lanes)]

    gathers = [
        Gather(
            shard.at[layer],
            full,
            chips,
            chip,
            lane,
            (
                hop_send.at[index],
                hop_recv.at[index],
                core_send.at[index],
                core_recv.at[index],
                own_sem.at[index],
            ),
        )
        for index, (shard, full) in enumerate(
            (
                (shard_qkv, full_qkv),
                (shard_out, full_out),
                (shard_in, full_in),
                (shard_back, full_back),
            )
        )
    ]
    get_qkv, get_out, get_in, get_back = gathers
    greet([(chip, other) for other in others()] + [get_qkv.to_x, get_qkv.to_y])
    get_qkv.begin()
    for gather in gathers:
        gather.own().start()

    unit, _ = normalize(hidden[...])
    normed[...] = (unit * gains[0:1] + shifts[0:1]).astype(jnp.bfloat16)
    low_rank[...] = dot_nt(normed[...], down[...])
    get_qkv.pass_on()
    get_out.begin()
    get_in.begin()
    get_qkv.cross()
    get_qkv.arrive()

    def qkv_tile(index, slot):
        return [
            pltpu.make_async_copy(
                full_qkv.at[:, at_columns(index, TILE)], tile_in.at[slot], tile_sem.at[0, slot]
            )
        ]

    per_tile = TILE // width
    tiles_each = model // TILE

    def qkv_body(index, slot):
        columns = at_columns(index, TILE)
        value = dot_nn(normed[...], tile_in[slot])
        value += dot_nn(low_rank[...].astype(jnp.bfloat16), up[:, columns])
        value += qkv_bias[0:1, columns]
        value = (value * qkv_bias[1:2, columns]).astype(jnp.bfloat16)
        kind = index // tiles_each
        first = lax.rem(index, tiles_each) * per_tile
        for step in range(per_tile):
            part = value[:, step * width : (step + 1) * width]
            for slot_at in range(slots):
                heads_out[slot_at, first + step, kind] = part[
                    slot_at * length : (slot_at + 1) * length
                ]

    stream(3 * tiles_each, qkv_tile, qkv_body)

    def send_heads(slot_at, other):
        return remote(
            heads_out.at[slot_at, other],
            heads_in.at[lane, :, slot_at],
            heads_send.at[slot_at, other],
            heads_recv.at[slot_at, lane],
            (chip, other),
        )

    def take_heads(slot_at, other):
        return remote(
            heads_out.at[slot_at, other],
            heads_in.at[other, :, slot_at],
            heads_send.at[slot_at, other],
            heads_recv.at[slot_at, other],
            (chip, other),
        )

    for slot_at in range(slots):
        for other in others():
            send_heads(slot_at, other).start()
        heads_in[lane, :, slot_at] = heads_out[slot_at, lane]

    get_out.pass_on()
    get_in.pass_on()
    get_back.begin()

    def send_mixed(slot_at, other):
        return remote(
            mixed.at[slot_at, other],
            mixture.at[lane, slot_at],
            mix_send.at[slot_at, other],
            mix_recv.at[slot_at, lane],
            (chip, other),
        )

    def take_mixed(slot_at, other):
        return remote(
            mixed.at[slot_at, other],
            mixture.at[other, slot_at],
            mix_send.at[slot_at, other],
            mix_recv.at[slot_at, other],
            (chip, other),
        )

    def attend(slot_at):
        def token_rows(kind, block):
            return heads_in[pl.ds(block * per_block, per_block), kind, slot_at].reshape(
                BLOCK, width
            )

        def query_step(query_block, carry):
            queries = split_heads(token_rows(0, query_block))
            begin_row = begin[slot_at, query_block]

            def score_step(key_block, best):
                found = dot_nt(token_rows(1, key_block), queries)
                open_pairs = allowed_pairs(key_block, query_block, begin_row, heads)
                found = jnp.where(open_pairs, found, MASKED)
                scores[key_block] = found
                return jnp.maximum(best, jnp.max(found, 0, keepdims=True))

            best = lax.fori_loop(
                0, query_block + 1, score_step, jnp.full((1, heads * BLOCK), MASKED, jnp.float32)
            )

            def exp_step(key_block, sums):
                raised = jnp.exp(scores[key_block] - best)
                scores[key_block] = raised
                return sums + jnp.sum(raised, 0, keepdims=True)

            sums = lax.fori_loop(
                0, query_block + 1, exp_step, jnp.zeros((1, heads * BLOCK), jnp.float32)
            )
            log_total[slot_at, query_block] = best + jnp.log(sums)
            inverse = 1.0 / sums

            def mix_step(key_block, mix):
                weights = (scores[key_block] * inverse).astype(jnp.bfloat16)
                return mix + dot_tn(weights, token_rows(2, key_block))

            mix = lax.fori_loop(
                0, query_block + 1, mix_step, jnp.zeros((heads * BLOCK, width), jnp.float32)
            )
            out = join_heads(mix, BLOCK).astype(jnp.bfloat16)
            for part in range(per_block):
                other = query_block * per_block + part
                mixed[slot_at, other] = out[part * length : (part + 1) * length]

                @pl.when(other != lane)
                def _():
                    send_mixed(slot_at, other).start()

            return carry

        lax.fori_loop(0, blocks, query_step, 0)

    for slot_at in range(slots):
        for other in others():
            take_heads(slot_at, other).wait_recv()
        attend(slot_at)
        mixture[lane, slot_at] = mixed[slot_at, lane]
        if slot_at == 0:
            get_out.cross()
            get_out.arrive()
            pltpu.make_async_copy(full_out, out_weight, out_sem).start()

    pltpu.make_async_copy(full_out, out_weight, out_sem).wait()
    for slot_at in range(slots):
        for other in others():
            take_mixed(slot_at, other).wait_recv()
    total[...] = hidden[...] + out_bias[...]

    def out_body(index, carry):
        part = jnp.concatenate(
            [mixture[2 * index].reshape(rows, width), mixture[2 * index + 1].reshape(rows, width)],
            1,
        )
        start = pl.multiple_of(index * 2 * width, 2 * width)
        total[...] += dot_nn(part, out_weight[pl.ds(start, 2 * width)])
        return carry

    lax.fori_loop(0, lanes // 2, out_body, 0)
    attended[...] = total[...]
    unit, _ = normalize(total[...])
    second = (unit * gains[1:2] + shifts[1:2]).astype(jnp.bfloat16)
    get_in.cross()
    get_in.arrive()

    def in_tile(index, slot):
        return [
            pltpu.make_async_copy(
                full_in.at[:, at_columns(index, TILE)], tile_in.at[slot], tile_sem.at[0, slot]
            )
        ]

    def in_body(index, slot):
        columns = at_columns(index, TILE)
        value = dot_nn(second, tile_in[slot]) + in_bias[:, columns]
        pre_act[:, columns] = value.astype(jnp.bfloat16)
        activation[index] = gelu(value).astype(jnp.bfloat16)

    get_back.pass_on()
    stream(hidden_units // TILE, in_tile, in_body)
    get_back.cross()
    get_back.arrive()
    total[...] += back_bias[...]

    def back_tile(index, slot):
        return [
            pltpu.make_async_copy(
                full_back.at[at_columns(index, TILE)], tile_back.at[slot], tile_sem.at[1, slot]
            )
        ]

    def back_body(index, slot):
        total[...] += dot_nn(activation[index], tile_back[slot])

    stream(hidden_units // TILE, back_tile, back_body)
    result[...] = total[...]
    for gather in gathers:
        gather.drain()
    for slot_at in range(slots):
        for other in others():
            send_heads(slot_at, other).wait_send()
            send_mixed(slot_at, other).wait_send()


def backward_kernel(
    sizes,
    gradient,
    hidden,
    begin,
    gains,
    down,
    up,
    normed,
    low_rank,
    heads_in,
    mixed,
    log_total,
    attended,
    pre_act,
    full_qkv,
    full_out,
    full_in,
    full_back,
    result,
    adapters,
    tile_in,
    tile_back,
    out_weight,
    qkv_weight,
    total,
    grad_attended,
    mix_out,
    mix_in,
    queries,
    mix_heads,
    delta,
    query_sum,
    key_sum,
    value_sum,
    heads_out,
    grads_in,
    grads_flat,
    tile_sem,
    load_sem,
    mix_send,
    mix_recv,
    heads_send,
    heads_recv,
):
    chips, lanes = sizes
    chip, lane = lax.axis_index("dp"), lax.axis_index("sp")
    slots, length, width = heads_in.shape[2:]
    heads = width // HEAD_SIZE
    rows, model = hidden.shape
    hidden_units = pre_act.shape[1]
    blocks = lanes * length // BLOCK
    per_block = BLOCK // length

    def others():
        return [lax.rem(lane + step, lanes) for step in range(1, lanes)]

    greet([(chip, other) for other in others()])
    load_out = pltpu.make_async_copy(full_out, out_weight, load_sem.at[0])
    load_qkv = pltpu.make_async_copy(full_qkv, qkv_weight, load_sem.at[1])

    low_gradient = gradient[...].astype(jnp.bfloat16)
    total[...] = jnp.zeros_like(total)

    def tiles(index, slot):
        part = at_columns(index, TILE)
        return [
            pltpu.make_async_copy(full_in.at[:, part], tile_in.at[slot], tile_sem.at[0, slot]),
            pltpu.make_async_copy(full_back.at[part], tile_back.at[slot], tile_sem.at[1, slot]),
        ]

    def forward_tile(index, slot):
        columns = at_columns(index, TILE)
        grad_act = dot_nt(low_gradient, tile_back[slot])
        slope = gelu_slope(pre_act[:, columns].astype(jnp.float32))
        grad_pre = (slope * grad_act).astype(jnp.bfloat16)
        total[...] += dot_nt(grad_pre, tile_in[slot])

    stream(hidden_units // TILE, tiles, forward_tile)
    load_out.start()
    load_qkv.start()
    grad_attended[...] = gradient[...] + norm_backward(attended[...], gains[1:2], total[...])
    low_attended = grad_attended[...].astype(jnp.bfloat16)
    load_out.wait()

    def send_mix(slot_at, other):
        return remote(
            mix_out.at[slot_at, other],
            mix_in.at[lane, slot_at],
            mix_send.at[slot_at, other],
            mix_recv.at[slot_at, lane],
            (chip, other),
        )

    def take_mix(slot_at, other):
        return remote(
            mix_out.at[slot_at, other],
            mix_in.at[other, slot_at],
            mix_send.at[slot_at, other],
            mix_recv.at[slot_at, other],
            (chip, other),
        )

    def mix_body(index, carry):
        start = pl.multiple_of(index * 2 * width, 2 * width)
        value = dot_nt(low_attended, out_weight[pl.ds(start, 2 * width)]).astype(jnp.bfloat16)
        for step in range(2):
            part = value[:, step * width : (step + 1) * width]
            for slot_at in range(slots):
                mix_out[slot_at, 2 * index + step] = part[
                    slot_at * length : (slot_at + 1) * length
                ]
        return carry

    lax.fori_loop(0, lanes // 2, mix_body, 0)
    for slot_at in range(slots):
        for other in others():
            send_mix(slot_at, other).start()
        mix_in[lane, slot_at] = mix_out[slot_at, lane]

    def send_heads(slot_at, other):
        return remote(
            heads_out.at[slot_at, other],
            grads_in.at[lane, slot_at],
            heads_send.at[slot_at, other],
            heads_recv.at[slot_at, lane],
            (chip, other),
        )

    def take_heads(slot_at, other):
        return remote(
            heads_out.at[slot_at, other],
            grads_in.at[other, slot_at],
            heads_send.at[slot_at, other],
            heads_recv.at[slot_at, other],
            (chip, other),
        )

    def attend(slot_at):
        def token_rows(kind, block):
            return heads_in[pl.ds(block * per_block, per_block), kind, slot_at].reshape(
                BLOCK, width
            )

        def prepare(block, carry):
            queries[block] = split_heads(token_rows(0, block))
            grads = mix_in[pl.ds(block * per_block, per_block), slot_at].reshape(BLOCK, width)
            grads = split_heads(grads)
            mix_heads[block] = grads
            mix = mixed[slot_at, pl.ds(block * per_block, per_block)].reshape(BLOCK, width)
            mix = jnp.concatenate([mix] * heads, 0).astype(jnp.float32)
            product = grads.astype(jnp.float32) * mix
            delta[block] = jnp.sum(product.T, 0, keepdims=True)
            query_sum[block] = jnp.zeros_like(query_sum[block])
            return carry

        lax.fori_loop(0, blocks, prepare, 0)

        def key_step(key_block, carry):
            keys = token_rows(1, key_block)
            values = token_rows(2, key_block)
            key_sum[...] = jnp.zeros_like(key_sum)
            value_sum[...] = jnp.zeros_like(value_sum)

            def query_step(query_block, inner):
                query_heads = queries[query_block]
                grad_heads = mix_heads[query_block]
                found = dot_nt(keys, query_heads)
                open_pairs = allowed_pairs(
                    key_block, query_block, begin[slot_at, query_block], heads
                )
                weights = jnp.where(
                    open_pairs, jnp.exp(found - log_total[slot_at, query_block]), 0.0
                )
                value_sum[...] += dot_nn(weights.astype(jnp.bfloat16), grad_heads)
                grad_weights = dot_nt(values, grad_heads)
                grad_scores = (weights * (grad_weights - delta[query_block])).astype(jnp.bfloat16)
                key_sum[...] += dot_nn(grad_scores, query_heads)
                query_sum[query_block] += dot_tn(grad_scores, keys)
                return inner

            lax.fori_loop(key_block, blocks, query_step, 0)
            for kind, sums in ((1, key_sum), (2, value_sum)):
                for part in range(per_block):
                    heads_out[slot_at, key_block * per_block + part, kind] = sums[
                        part * length : (part + 1) * length
                    ].astype(jnp.bfloat16)
            return carry

        lax.fori_loop(0, blocks, key_step, 0)

        def finish(block, carry):
            out = join_heads(query_sum[block], BLOCK).astype(jnp.bfloat16)
            out = out * jnp.asarray(HEAD_SIZE ** (-0.5), jnp.bfloat16)
            for part in range(per_block):
                heads_out[slot_at, block * per_block + part, 0] = out[
                    part * length : (part + 1) * length
                ]
            return carry

        lax.fori_loop(0, blocks, finish, 0)

    for slot_at in range(slots):
        for other in others():
            take_mix(slot_at, other).wait_recv()
        attend(slot_at)
        for other in others():
            send_heads(slot_at, other).start()
        grads_in[lane, slot_at] = heads_out[slot_at, lane]

    load_qkv.wait()
    for slot_at in range(slots):
        for other in others():
            take_heads(slot_at, other).wait_recv()
    for other in range(lanes):
        for kind in range(3):
            for slot_at in range(slots):
                start = kind * model + other * width
                grads_flat[slot_at * length : (slot_at + 1) * length, start : start + width] = (
                    grads_in[other, slot_at, kind]
                )

    grad_low = dot_nt(grads_flat[...], up[...])
    grad_low = grad_low.astype(jnp.bfloat16)
    total[...] = dot_nn(grad_low, down[...])

    def qkv_body(index, carry):
        columns = at_columns(index, TILE)
        total[...] += dot_nt(grads_flat[:, columns], qkv_weight[:, columns])
        return carry

    lax.fori_loop(0, 3 * model // TILE, qkv_body, 0)
    result[...] = grad_attended[...] + norm_backward(hidden[...], gains[0:1], total[...])
    ranks = down.shape[0]
    adapters[0:ranks] = dot_tn(grad_low, normed[...])
    scale = ADAPTER_ALPHA / (ranks // 2)
    low_values = (low_rank[...] * scale).astype(jnp.bfloat16)
    owner = lax.broadcasted_iota(jnp.int32, (ranks, model), 0)
    up_query = dot_tn(low_values, grads_flat[:, :model])
    up_value = dot_tn(low_values, grads_flat[:, 2 * model :])
    adapters[ranks : 2 * ranks] = jnp.where(owner < ranks // 2, up_query, up_value)
    for slot_at in range(slots):
        for other in others():
            send_mix(slot_at, other).wait_send()
            send_heads(slot_at, other).wait_send()


def fast_sum(sizes, terms):
    count = math.prod(sizes)
    pieces = terms.reshape(count, -1, 128)
    vmem = pl.BlockSpec(memory_space=pltpu.VMEM)
    summed = pl.pallas_call(
        partial(fast_sum_kernel, sizes),
        out_shape=jax.ShapeDtypeStruct(pieces.shape, jnp.float32),
        in_specs=[vmem],
        out_specs=vmem,
        scratch_shapes=[pltpu.VMEM(pieces.shape, jnp.float32)]
        + [pltpu.SemaphoreType.DMA((count,))] * 4,
        name="adapter_sum",
        compiler_params=pltpu.CompilerParams(collective_id=0, has_side_effects=True),
    )(pieces)
    return summed.reshape(terms.shape)


def fast_sum_kernel(sizes, terms, total, landing, send_sem, recv_sem, spread_send, spread_recv):
    chips, lanes = sizes
    count = chips * lanes
    mine = lax.axis_index("dp") * lanes + lax.axis_index("sp")

    def place(step):
        other = lax.rem(mine + step, count)
        return other, (other // lanes, lax.rem(other, lanes))

    def scatter(step):
        other, device = place(step)
        return remote(
            terms.at[other], landing.at[step], send_sem.at[step], recv_sem.at[step], device
        )

    def spread(step):
        _, device = place(step)
        return remote(
            total.at[mine], total.at[mine], spread_send.at[step], spread_recv.at[step], device
        )

    greet([place(step)[1] for step in range(1, count)])
    for step in range(1, count):
        scatter(step).start()
    landing[0] = terms[mine]
    for step in range(1, count):
        scatter(step).wait()
    total[mine] = jnp.sum(landing[...], axis=0)
    for step in range(1, count):
        spread(step).start()
    for step in range(1, count):
        spread(step).wait()


def forward_call(layer, sizes, hidden, begin, shards, extras):
    chips, lanes = sizes
    rows, model = hidden.shape
    slots, blocks = begin.shape[:2]
    length = rows // slots
    width = model // lanes
    heads = width // HEAD_SIZE
    hidden_units = shards[2].shape[2]
    vmem = pl.BlockSpec(memory_space=pltpu.VMEM)
    anywhere = pl.BlockSpec(memory_space=pl.ANY)
    low, full = jnp.bfloat16, jnp.float32
    shape = jax.ShapeDtypeStruct
    dma = pltpu.SemaphoreType.DMA
    return pl.pallas_call(
        partial(forward_kernel, layer, sizes),
        out_shape=(
            shape((rows, model), full),
            shape((rows, model), low),
            shape((rows, extras[-2].shape[0]), full),
            shape((lanes, 3, slots, length, width), low),
            shape((slots, lanes, length, width), low),
            shape((slots, blocks, 1, heads * BLOCK), full),
            shape((rows, model), full),
            shape((rows, hidden_units), low),
        )
        + tuple(shape((chips * shard.shape[1], shard.shape[2]), low) for shard in shards),
        in_specs=[vmem] * 2 + [anywhere] * 4 + [vmem] * len(extras),
        out_specs=(vmem,) * 8 + (anywhere,) * 4,
        scratch_shapes=[
            pltpu.VMEM((2, model, TILE), low),
            pltpu.VMEM((2, TILE, model), low),
            pltpu.VMEM((model, model), low),
            pltpu.VMEM((slots, lanes, 3, length, width), low),
            pltpu.VMEM((lanes, slots, length, width), low),
            pltpu.VMEM((blocks, BLOCK, heads * BLOCK), full),
            pltpu.VMEM((hidden_units // TILE, rows, TILE), low),
            pltpu.VMEM((rows, model), full),
            dma((2, 2)),
            dma,
            dma((slots, lanes)),
            dma((slots, lanes)),
            dma((slots, lanes)),
            dma((slots, lanes)),
            dma((4, 6)),
            dma((4, 6)),
            dma((4, 3)),
            dma((4, 3)),
            dma((4,)),
        ],
        name="layer_forward",
        compiler_params=pltpu.CompilerParams(
            collective_id=1 + layer, has_side_effects=True, vmem_limit_bytes=VMEM_LIMIT
        ),
    )(hidden, begin, *shards, *extras)


def backward_call(layer, sizes, gradient, hidden, begin, extras, kept):
    chips, lanes = sizes
    rows, model = hidden.shape
    slots, blocks = begin.shape[:2]
    length = rows // slots
    width = model // lanes
    heads = width // HEAD_SIZE
    vmem = pl.BlockSpec(memory_space=pltpu.VMEM)
    anywhere = pl.BlockSpec(memory_space=pl.ANY)
    low, full = jnp.bfloat16, jnp.float32
    shape = jax.ShapeDtypeStruct
    dma = pltpu.SemaphoreType.DMA
    ranks = extras[1].shape[0]
    return pl.pallas_call(
        partial(backward_kernel, sizes),
        out_shape=(shape((rows, model), full), shape((2 * ranks, model), full)),
        in_specs=[vmem] * (3 + len(extras) + 7) + [anywhere] * 4,
        out_specs=(vmem, vmem),
        scratch_shapes=[
            pltpu.VMEM((2, model, TILE), low),
            pltpu.VMEM((2, TILE, model), low),
            pltpu.VMEM((model, model), low),
            pltpu.VMEM((model, 3 * model), low),
            pltpu.VMEM((rows, model), full),
            pltpu.VMEM((rows, model), full),
            pltpu.VMEM((slots, lanes, length, width), low),
            pltpu.VMEM((lanes, slots, length, width), low),
            pltpu.VMEM((blocks, heads * BLOCK, width), low),
            pltpu.VMEM((blocks, heads * BLOCK, width), low),
            pltpu.VMEM((blocks, 1, heads * BLOCK), full),
            pltpu.VMEM((blocks, heads * BLOCK, width), full),
            pltpu.VMEM((BLOCK, width), full),
            pltpu.VMEM((BLOCK, width), full),
            pltpu.VMEM((slots, lanes, 3, length, width), low),
            pltpu.VMEM((lanes, slots, 3, length, width), low),
            pltpu.VMEM((rows, 3 * model), low),
            dma((2, 2)),
            dma((2,)),
            dma((slots, lanes)),
            dma((slots, lanes)),
            dma((slots, lanes)),
            dma((slots, lanes)),
        ],
        name="layer_backward",
        compiler_params=pltpu.CompilerParams(
            collective_id=8 + layer, has_side_effects=True, vmem_limit_bytes=VMEM_LIMIT
        ),
    )(gradient, hidden, begin, *extras, *kept)


def fast_body(
    sizes,
    first_layer_input,
    cotangent,
    document_begin,
    query_key_value_weight,
    attention_out_weight,
    feedforward_in_weight,
    feedforward_out_weight,
    query_value_bias,
    attention_out_bias,
    feedforward_in_bias,
    feedforward_out_bias,
    layernorm_gain,
    layernorm_bias,
    adapter_down_maps,
    adapter_up_maps,
):
    chips, lanes = sizes
    slots, length, model = first_layer_input.shape
    layers, _, rank, _ = adapter_down_maps.shape
    heads = model // lanes // HEAD_SIZE
    blocks = lanes * length // BLOCK
    begin = document_begin.reshape(slots, blocks, 1, BLOCK)
    begin = jnp.concatenate([begin] * heads, -1)
    shards = (
        query_key_value_weight,
        attention_out_weight,
        feedforward_in_weight,
        feedforward_out_weight,
    )
    adapter_scale = ADAPTER_ALPHA / rank
    blank = jnp.zeros((rank, model), jnp.bfloat16)
    plain = jnp.ones((2 * model,), jnp.float32)

    def extras_of(layer):
        down = adapter_down_maps[layer].reshape(2 * rank, model).astype(jnp.bfloat16)
        ups = (adapter_scale * adapter_up_maps[layer]).astype(jnp.bfloat16)
        up = jnp.concatenate(
            [
                jnp.concatenate([ups[0], blank, blank], 1),
                jnp.concatenate([blank, blank, ups[1]], 1),
            ],
            0,
        )
        bias = query_value_bias[layer]
        qkv_bias = jnp.stack(
            [
                jnp.concatenate([bias[0], jnp.zeros_like(bias[0]), bias[1]]),
                jnp.concatenate([jnp.full((model,), HEAD_SIZE ** (-0.5), jnp.float32), plain]),
            ]
        )
        return (
            qkv_bias,
            attention_out_bias[layer][None],
            feedforward_in_bias[layer][None],
            feedforward_out_bias[layer][None],
            layernorm_gain[layer],
            layernorm_bias[layer],
            down,
            up,
        )

    hidden = first_layer_input.astype(jnp.float32).reshape(slots * length, model)
    inputs, kept = [], []
    for layer in range(layers):
        inputs.append(hidden)
        hidden, *state = forward_call(layer, sizes, hidden, begin, shards, extras_of(layer))
        kept.append(state)
    gradient = cotangent.astype(jnp.float32).reshape(slots * length, model)
    terms = [None] * layers
    for layer in reversed(range(layers)):
        extras = extras_of(layer)
        gradient, terms[layer] = backward_call(
            layer, sizes, gradient, inputs[layer], begin, (extras[4], *extras[6:]), kept[layer]
        )
    summed = fast_sum(sizes, jnp.stack(terms))
    summed = summed * (1.0 / math.sqrt(slots * chips * length * lanes))
    summed = summed.reshape(layers, 2, 2, rank, model)
    shape = first_layer_input.shape
    return hidden.reshape(shape), gradient.reshape(shape), summed[:, 0], summed[:, 1]


def solution(mesh):
    chips, lanes = sizes = tuple(mesh.devices.shape)
    fast = sizes == (4, 8)
    token_axes = "sp" if fast else SP
    if not fast:
        mesh = Mesh(mesh.devices.reshape(chips, lanes // 2, 2), ("dp",) + SP)
    tokens = P("dp", token_axes, None)
    weights = P(None, "dp", None)
    return jax.shard_map(
        partial(fast_body, sizes) if fast else body,
        mesh=mesh,
        in_specs=(tokens, tokens, P("dp", None)) + (weights,) * 4 + (P(),) * 8,
        out_specs=(tokens, tokens, P(), P()),
        check_vma=False,
    )
```

```python
from functools import partial
import math

import jax
import jax.numpy as jnp
from jax import lax
from jax.experimental import pallas as pl
from jax.experimental.pallas import tpu as pltpu
from jax.sharding import Mesh, PartitionSpec as P

HEAD_SIZE = 64


EPSILON = 1e-05
ADAPTER_ALPHA = 32.0
EXACT_PRECISION = lax.Precision.HIGHEST
MASKED = -1e30
SP = ("z", "core")


def layer_norm(tensor, gains, shifts):
    row_mean = jnp.mean(tensor, -1, keepdims=True)
    centred = tensor - row_mean
    spread = jnp.mean(centred * centred, -1, keepdims=True)
    return centred * lax.rsqrt(spread + EPSILON) * gains + shifts


def fetch_weights(
    query_key_value_weight,
    attention_out_weight,
    feedforward_in_weight,
    feedforward_out_weight,
    layer_number,
):
    core = lax.axis_index("core")

    def fetch(shards):
        half = shards.shape[1] // 2
        part = lax.dynamic_slice_in_dim(shards[layer_number], core * half, half, 0)
        return lax.all_gather(part, ("dp", "core"), axis=0, tiled=True)

    return (
        fetch(query_key_value_weight),
        fetch(attention_out_weight),
        fetch(feedforward_in_weight),
        fetch(feedforward_out_weight),
    )


def sum_kernel(sizes, terms_ref, out_ref, landing, send_sem, recv_sem, send_sem2, recv_sem2):
    count = math.prod(sizes)
    me = [lax.axis_index(name) for name in ("dp", "z", "core")]
    mine = (me[0] * sizes[1] + me[1]) * sizes[2] + me[2]

    def place(step):
        other = lax.rem(mine + step, count)
        return other, (
            other // (sizes[1] * sizes[2]),
            lax.rem(other // sizes[2], sizes[1]),
            lax.rem(other, sizes[2]),
        )

    barrier = pltpu.get_barrier_semaphore()
    for step in range(1, count):
        pl.semaphore_signal(
            barrier, inc=1, device_id=place(step)[1], device_id_type=pl.DeviceIdType.MESH
        )
    pl.semaphore_wait(barrier, count - 1)

    def scatter(step):
        other, device = place(step)
        return pltpu.make_async_remote_copy(
            src_ref=terms_ref.at[other],
            dst_ref=landing.at[step],
            send_sem=send_sem.at[step],
            recv_sem=recv_sem.at[step],
            device_id=device,
            device_id_type=pl.DeviceIdType.MESH,
        )

    def spread(step):
        other, device = place(step)
        return pltpu.make_async_remote_copy(
            src_ref=out_ref.at[mine],
            dst_ref=out_ref.at[mine],
            send_sem=send_sem2.at[step],
            recv_sem=recv_sem2.at[step],
            device_id=device,
            device_id_type=pl.DeviceIdType.MESH,
        )

    for step in range(1, count):
        scatter(step).start()
    landing[0] = terms_ref[mine]
    for step in range(1, count):
        scatter(step).wait()
    out_ref[mine] = jnp.sum(landing[...], axis=0)
    for step in range(1, count):
        spread(step).start()
    for step in range(1, count):
        spread(step).wait()


def sum_adapters(down_terms, up_terms):
    sizes = [lax.axis_size(name) for name in ("dp", "z", "core")]
    count = math.prod(sizes)
    packed = jnp.stack([down_terms, up_terms])
    if count > 64 or packed.size % (count * 1024) != 0:
        return lax.psum((down_terms, up_terms), ("dp", "z", "core"))
    pieces = packed.reshape(count, -1, 128)
    vmem = pl.BlockSpec(memory_space=pltpu.VMEM)
    summed = pl.pallas_call(
        partial(sum_kernel, sizes),
        out_shape=jax.ShapeDtypeStruct(pieces.shape, jnp.float32),
        in_specs=[vmem],
        out_specs=vmem,
        scratch_shapes=[pltpu.VMEM(pieces.shape, jnp.float32)]
        + [pltpu.SemaphoreType.DMA((count,))] * 4,
        name="adapter_sum",
        compiler_params=pltpu.CompilerParams(collective_id=0, has_side_effects=True),
    )(pieces)
    summed = summed.reshape(packed.shape)
    return summed[0], summed[1]


def slot_scores(query_rows, key_rows, document_starts):
    length = query_rows.shape[0]
    heads_q = query_rows.reshape(length, -1, HEAD_SIZE)
    heads_k = key_rows.reshape(length, -1, HEAD_SIZE)
    scores = jnp.einsum("qhd,khd->hqk", heads_q, heads_k, preferred_element_type=jnp.float32)
    places = jnp.arange(length)
    allowed = (document_starts[:, None] == document_starts[None, :]) & (
        places[None, :] <= places[:, None]
    )
    return jnp.where(allowed[None], scores, MASKED)


def slot_forward(slot_items):
    query_rows, key_rows, value_rows, document_starts = slot_items
    length = query_rows.shape[0]
    scores = slot_scores(query_rows, key_rows, document_starts)
    row_max = jnp.max(scores, -1, keepdims=True)
    row_total = jnp.sum(jnp.exp(scores - row_max), -1, keepdims=True)
    log_total = row_max + jnp.log(row_total)
    probability = jnp.exp(scores - log_total).astype(jnp.bfloat16)
    mixture = jnp.einsum(
        "hqk,khd->qhd",
        probability,
        value_rows.reshape(length, -1, HEAD_SIZE),
        preferred_element_type=jnp.float32,
    )
    return (mixture.reshape(length, -1).astype(jnp.bfloat16), log_total[..., 0])


def slot_backward(slot_items):
    query_rows, key_rows, value_rows, document_starts, log_total, grad_mixture = slot_items
    length = query_rows.shape[0]
    scores = slot_scores(query_rows, key_rows, document_starts)
    probability = jnp.exp(scores - log_total[..., None])
    low_probability = probability.astype(jnp.bfloat16)
    grad_heads = grad_mixture.reshape(length, -1, HEAD_SIZE)
    value_heads = value_rows.reshape(length, -1, HEAD_SIZE)
    grad_values = jnp.einsum(
        "hqk,qhd->khd", low_probability, grad_heads, preferred_element_type=jnp.float32
    )
    grad_prob = jnp.einsum(
        "qhd,khd->hqk", grad_heads, value_heads, preferred_element_type=jnp.float32
    )
    grad_scores = probability * (grad_prob - jnp.sum(probability * grad_prob, -1, keepdims=True))
    low_scores = grad_scores.astype(jnp.bfloat16)
    grad_queries = jnp.einsum(
        "hqk,khd->qhd",
        low_scores,
        key_rows.reshape(length, -1, HEAD_SIZE),
        preferred_element_type=jnp.float32,
    )
    grad_keys = jnp.einsum(
        "hqk,qhd->khd",
        low_scores,
        query_rows.reshape(length, -1, HEAD_SIZE),
        preferred_element_type=jnp.float32,
    )
    return (
        grad_queries.reshape(length, -1).astype(jnp.bfloat16),
        grad_keys.reshape(length, -1).astype(jnp.bfloat16),
        grad_values.reshape(length, -1).astype(jnp.bfloat16),
    )


def layer_forward(hidden_state, weight_set, params, document_begin):
    query_key_value_weight, attention_out_weight, feedforward_in_weight, feedforward_out_weight = (
        weight_set
    )
    (
        query_value_bias,
        attention_out_bias,
        feedforward_in_bias,
        feedforward_out_bias,
        gains,
        shifts,
        down_projection,
        up_projection,
    ) = params
    model_dimension = hidden_state.shape[-1]
    normed = layer_norm(hidden_state, gains[0], shifts[0]).astype(jnp.bfloat16)
    projected_rows = jnp.einsum(
        "std,de->ste", normed, query_key_value_weight, preferred_element_type=jnp.float32
    )
    widened = normed.astype(jnp.float32)
    adapter_scale = ADAPTER_ALPHA / down_projection.shape[1]
    query_row_block = jnp.einsum(
        "nyh,lh->nyl", widened, down_projection[0], precision=EXACT_PRECISION
    )
    value_row_block = jnp.einsum(
        "nyh,lh->nyl", widened, down_projection[1], precision=EXACT_PRECISION
    )
    query_rows = (
        (
            projected_rows[..., :model_dimension]
            + query_value_bias[0]
            + adapter_scale
            * jnp.einsum(
                "wah,hp->wap", query_row_block, up_projection[0], precision=EXACT_PRECISION
            )
        )
        * HEAD_SIZE ** (-0.5)
    ).astype(jnp.bfloat16)
    key_rows = projected_rows[..., model_dimension : 2 * model_dimension].astype(jnp.bfloat16)
    value_rows = (
        projected_rows[..., 2 * model_dimension :]
        + query_value_bias[1]
        + adapter_scale
        * jnp.einsum("wah,hp->wap", value_row_block, up_projection[1], precision=EXACT_PRECISION)
    ).astype(jnp.bfloat16)
    queries_h, keys_h, values_h = lax.all_to_all(
        jnp.stack([query_rows, key_rows, value_rows]), SP, split_axis=3, concat_axis=2, tiled=True
    )
    mixture_h, log_total = lax.map(slot_forward, (queries_h, keys_h, values_h, document_begin))
    mixture = lax.all_to_all(mixture_h, SP, split_axis=1, concat_axis=2, tiled=True)
    attended = hidden_state + (
        jnp.einsum("std,de->ste", mixture, attention_out_weight, preferred_element_type=jnp.float32)
        + attention_out_bias
    )
    normed_mlp = layer_norm(attended, gains[1], shifts[1]).astype(jnp.bfloat16)
    pre_act = (
        jnp.einsum(
            "std,df->stf", normed_mlp, feedforward_in_weight, preferred_element_type=jnp.float32
        )
        + feedforward_in_bias
    )
    activation = jax.nn.gelu(pre_act, approximate=True).astype(jnp.bfloat16)
    final_result = attended + (
        jnp.einsum(
            "stf,fd->std", activation, feedforward_out_weight, preferred_element_type=jnp.float32
        )
        + feedforward_out_bias
    )
    saved_state = (
        normed,
        query_row_block,
        value_row_block,
        queries_h,
        keys_h,
        values_h,
        log_total,
        attended,
        pre_act,
    )
    return (final_result, saved_state)


def layer_backward(hidden_state, gradient, weight_set, params, document_begin, saved_state):
    query_key_value_weight, attention_out_weight, feedforward_in_weight, feedforward_out_weight = (
        weight_set
    )
    (
        query_value_bias,
        attention_out_bias,
        feedforward_in_bias,
        feedforward_out_bias,
        gains,
        shifts,
        down_projection,
        up_projection,
    ) = params
    (
        normed,
        query_row_block,
        value_row_block,
        queries_h,
        keys_h,
        values_h,
        log_total,
        attended,
        pre_act,
    ) = saved_state
    grad_act = jnp.einsum(
        "std,fd->stf",
        gradient.astype(jnp.bfloat16),
        feedforward_out_weight,
        preferred_element_type=jnp.float32,
    )
    unused_act, gelu_back = jax.vjp(partial(jax.nn.gelu, approximate=True), pre_act)
    grad_pre = gelu_back(grad_act)[0].astype(jnp.bfloat16)
    grad_normed_mlp = jnp.einsum(
        "stf,df->std", grad_pre, feedforward_in_weight, preferred_element_type=jnp.float32
    )
    unused_norm, second_back = jax.vjp(
        lambda tensor: layer_norm(tensor, gains[1], shifts[1]), attended
    )
    grad_attended = gradient + second_back(grad_normed_mlp)[0]
    grad_mixture = jnp.einsum(
        "ste,de->std",
        grad_attended.astype(jnp.bfloat16),
        attention_out_weight,
        preferred_element_type=jnp.float32,
    ).astype(jnp.bfloat16)
    grad_mixture_h = lax.all_to_all(grad_mixture, SP, split_axis=2, concat_axis=1, tiled=True)
    grad_q_h, grad_k_h, grad_v_h = lax.map(
        slot_backward, (queries_h, keys_h, values_h, document_begin, log_total, grad_mixture_h)
    )
    grad_queries, grad_keys, grad_values = lax.all_to_all(
        jnp.stack([grad_q_h, grad_k_h, grad_v_h]), SP, split_axis=2, concat_axis=3, tiled=True
    )
    grad_queries = grad_queries * jnp.asarray(HEAD_SIZE ** (-0.5), jnp.bfloat16)
    stacked = jnp.concatenate([grad_queries, grad_keys, grad_values], -1)
    grad_normed = jnp.einsum(
        "ste,de->std", stacked, query_key_value_weight, preferred_element_type=jnp.float32
    )
    adapter_scale = ADAPTER_ALPHA / down_projection.shape[1]
    widened = normed.astype(jnp.float32)
    query_widened = grad_queries.astype(jnp.float32)
    value_widened = grad_values.astype(jnp.float32)
    query_row_gradient = adapter_scale * jnp.einsum(
        "nyh,lh->nyl", query_widened, up_projection[0], precision=EXACT_PRECISION
    )
    value_row_gradient = adapter_scale * jnp.einsum(
        "nyh,lh->nyl", value_widened, up_projection[1], precision=EXACT_PRECISION
    )
    query_up_weight = adapter_scale * jnp.einsum(
        "fkp,fkz->pz", query_row_block, query_widened, precision=EXACT_PRECISION
    )
    value_up_weight = adapter_scale * jnp.einsum(
        "fkp,fkz->pz", value_row_block, value_widened, precision=EXACT_PRECISION
    )
    down_q = jnp.einsum("fkp,fkz->pz", query_row_gradient, widened, precision=EXACT_PRECISION)
    down_v = jnp.einsum("fkp,fkz->pz", value_row_gradient, widened, precision=EXACT_PRECISION)
    grad_normed = (
        grad_normed
        + jnp.einsum(
            "wah,hp->wap", query_row_gradient, down_projection[0], precision=EXACT_PRECISION
        )
        + jnp.einsum(
            "wah,hp->wap", value_row_gradient, down_projection[1], precision=EXACT_PRECISION
        )
    )
    unused_first, first_back = jax.vjp(
        lambda tensor: layer_norm(tensor, gains[0], shifts[0]), hidden_state
    )
    grad_hidden = grad_attended + first_back(grad_normed)[0]
    return (grad_hidden, jnp.stack([down_q, down_v]), jnp.stack([query_up_weight, value_up_weight]))


def body(
    first_layer_input,
    cotangent,
    document_begin,
    query_key_value_weight,
    attention_out_weight,
    feedforward_in_weight,
    feedforward_out_weight,
    query_value_bias,
    attention_out_bias,
    feedforward_in_bias,
    feedforward_out_bias,
    layernorm_gain,
    layernorm_bias,
    adapter_down_maps,
    adapter_up_maps,
):
    layers = query_key_value_weight.shape[0]

    def params_of(layer_number):
        return (
            query_value_bias[layer_number],
            attention_out_bias[layer_number],
            feedforward_in_bias[layer_number],
            feedforward_out_bias[layer_number],
            layernorm_gain[layer_number],
            layernorm_bias[layer_number],
            adapter_down_maps[layer_number],
            adapter_up_maps[layer_number],
        )

    hidden_state = first_layer_input.astype(jnp.float32)
    inputs = []
    gathered = []
    kept = []
    for layer_number in range(layers):
        weight_set = fetch_weights(
            query_key_value_weight,
            attention_out_weight,
            feedforward_in_weight,
            feedforward_out_weight,
            layer_number,
        )
        inputs.append(hidden_state)
        gathered.append(weight_set)
        hidden_state, saved_state = layer_forward(
            hidden_state, weight_set, params_of(layer_number), document_begin
        )
        kept.append(saved_state)
    gradient = cotangent.astype(jnp.float32)
    down_parts = [None] * layers
    up_parts = [None] * layers
    for layer_number in reversed(range(layers)):
        gradient, down_terms, up_terms = layer_backward(
            inputs[layer_number],
            gradient,
            gathered[layer_number],
            params_of(layer_number),
            document_begin,
            kept[layer_number],
        )
        down_parts[layer_number] = down_terms
        up_parts[layer_number] = up_terms
    grad_down = jnp.stack(down_parts)
    grad_up = jnp.stack(up_parts)
    grad_down, grad_up = sum_adapters(grad_down, grad_up)
    tokens = (
        first_layer_input.shape[0]
        * first_layer_input.shape[1]
        * lax.axis_size("dp")
        * lax.axis_size("z")
        * lax.axis_size("core")
    )
    token_scale = 1.0 / math.sqrt(tokens)
    return (hidden_state, gradient, grad_down * token_scale, grad_up * token_scale)


MESH = pl.DeviceIdType.MESH
TILE = 512
LANES = 128
DEPTH = 4
VMEM_LIMIT = 60 * 1024 * 1024
LOW, FULL = jnp.bfloat16, jnp.float32


def dot_nn(left, right):
    return jnp.dot(left, right, preferred_element_type=FULL)


def dot_nt(left, right):
    return lax.dot_general(left, right, (((1,), (1,)), ((), ())), preferred_element_type=FULL)


def dot_tn(left, right):
    return lax.dot_general(left, right, (((0,), (0,)), ((), ())), preferred_element_type=FULL)


def normalize(tensor):
    centred = tensor - jnp.mean(tensor, -1, keepdims=True)
    spread = jnp.mean(centred * centred, -1, keepdims=True)
    scale = lax.rsqrt(spread + EPSILON)
    return centred * scale, scale


def norm_backward(tensor, gains, gradient):
    unit, scale = normalize(tensor)
    weighted = gradient * gains
    first = jnp.mean(weighted, -1, keepdims=True)
    second = jnp.mean(weighted * unit, -1, keepdims=True)
    return scale * (weighted - first - unit * second)


GELU_INNER = math.sqrt(2.0 / math.pi)
GELU_CUBE = 0.044715


def gelu(value):
    inner = GELU_INNER * (value + GELU_CUBE * (value * value * value))
    return 0.5 * value * (1.0 + jnp.tanh(inner))


def gelu_slope(value):
    square = value * value
    bend = jnp.tanh(GELU_INNER * (value + GELU_CUBE * (square * value)))
    climb = GELU_INNER * (1.0 + 3.0 * GELU_CUBE * square)
    return 0.5 * (1.0 + bend) + 0.5 * value * (1.0 - bend * bend) * climb


def split_heads(rows):
    heads = rows.shape[1] // HEAD_SIZE
    owner = lax.broadcasted_iota(jnp.int32, rows.shape, 1) // HEAD_SIZE
    return jnp.concatenate(
        [jnp.where(owner == head, rows, jnp.zeros_like(rows)) for head in range(heads)], 0
    )


def join_heads(stacked, length):
    heads = stacked.shape[0] // HEAD_SIZE
    joined = [
        stacked[head * HEAD_SIZE : (head + 1) * HEAD_SIZE, head * length : (head + 1) * length]
        for head in range(heads)
    ]
    return jnp.concatenate(joined, 0).T


def remote(source, target, send_sem, recv_sem, device):
    return pltpu.make_async_remote_copy(
        src_ref=source,
        dst_ref=target,
        send_sem=send_sem,
        recv_sem=recv_sem,
        device_id=device,
        device_id_type=MESH,
    )


def prime(count, copies):
    for index in range(min(count, DEPTH)):
        for copy in copies(index, index):
            copy.start()


def stream(count, copies, body):
    def step(index, carry):
        slot = lax.rem(index, DEPTH)
        for copy in copies(index, slot):
            copy.wait()
        body(index, slot)

        @pl.when(index + DEPTH < count)
        def _():
            for copy in copies(index + DEPTH, slot):
                copy.start()

        return carry

    lax.fori_loop(0, count, step, 0)


def at_columns(index, size):
    return pl.ds(pl.multiple_of(index * size, size), size)


class Gather:
    def __init__(self, shard, full, stride, offset, columns, place, sems):
        self.shard, self.full = shard, full
        self.stride, self.offset, self.columns = stride, offset, columns
        self.rows = shard.shape[0]
        self.unit = self.rows // 16
        chips, chip, lane = place
        self.chip, self.core, self.side = chip, lax.rem(lane, 2), lax.rem(lane // 2, 2)
        self.next_x = chip + 1 - 2 * lax.rem(chip, 2)
        self.next_y = lax.rem(chip + 2, chips)
        self.far = chips - 1 - chip
        self.to_x, self.to_y = (self.next_x, lane), (self.next_y, lane)
        self.to_z = (chip, lane + 2 - 4 * self.side)
        self.to_core = (chip, lane + 1 - 2 * self.core)
        self.send_sem, self.recv_sem = sems

    def whole(self, owner, start, count):
        first = owner * self.stride + self.offset + start
        return self.full.at[pl.ds(pl.multiple_of(first, 16), count), self.columns]

    def units(self, owner, first, count, own=False):
        start = (self.core * 8 + first) * self.unit
        size = count * self.unit
        if own:
            return self.shard.at[pl.ds(pl.multiple_of(start, 16), size), self.columns]
        return self.whole(owner, start, size)

    def hop(self, index):
        side = self.side
        owner, first, count, device = (
            (self.chip, 4 * side, 4, self.to_x),
            (self.chip, 4 * side, 4, self.to_y),
            (self.chip, 4 - 4 * side, 4, self.to_x),
            (self.chip, 4 - 4 * side, 4, self.to_y),
            (self.next_x, 4 * side, 2, self.to_y),
            (self.next_y, 4 * side + 2, 2, self.to_x),
            (self.far, 4 * side, 4, self.to_z),
            (self.next_x, 0, 8, self.to_core),
            (self.next_y, 0, 8, self.to_core),
            (self.far, 0, 8, self.to_core),
        )[index]
        return remote(
            self.units(owner, first, count, own=index < 4),
            self.units(owner, first, count),
            self.send_sem.at[index],
            self.recv_sem.at[index],
            device,
        )

    def own(self):
        return remote(
            self.shard.at[:, self.columns],
            self.whole(self.chip, 0, self.rows),
            self.send_sem.at[10],
            self.recv_sem.at[10],
            self.to_core,
        )

    def begin(self):
        for index in range(4):
            self.hop(index).start()
        self.own().start()

    def pass_on(self):
        for arrived, onward in ((0, 4), (1, 5)):
            self.hop(arrived).wait_recv()
            self.hop(onward).start()

    def trade(self):
        self.hop(4).wait_recv()
        self.hop(5).wait_recv()
        self.hop(6).start()
        for arrived, onward in ((2, 7), (3, 8)):
            self.hop(arrived).wait_recv()
            self.hop(onward).start()

    def cross(self):
        self.hop(6).wait_recv()
        self.hop(9).start()

    def arrive(self):
        for index in range(7, 10):
            self.hop(index).wait_recv()
        self.own().wait_recv()

    def drain(self):
        for index in range(10):
            self.hop(index).wait_send()
        self.own().wait_send()


def train_kernel(
    sizes,
    tokens_in,
    cotangent_in,
    begin,
    shard_qkv,
    shard_out,
    shard_in,
    shard_back,
    qv_bias,
    out_bias,
    in_bias,
    back_bias,
    gains,
    shifts,
    down_maps,
    up_maps,
    output,
    input_grad,
    grad_down,
    grad_up,
    full_qkv,
    full_out,
    full_in,
    full_back,
    hidden,
    tokens_low,
    cotangent_low,
    normed,
    low_rank,
    heads_in,
    mixed,
    log_total,
    attended,
    pre_act,
    tile_in,
    tile_back,
    out_weight,
    qkv_weight,
    heads_out,
    mixture,
    scores,
    activation,
    total,
    gradient,
    grad_attended,
    mix_out,
    mix_in,
    queries,
    mix_heads,
    delta,
    query_sum,
    key_sum,
    value_sum,
    grads_in,
    grads_flat,
    qkv_bias,
    up_low,
    down_low,
    return_out,
    result_low,
    terms,
    landing,
    landing_chips,
    summed,
    tile_sem,
    load_sem,
    heads_send,
    heads_recv,
    mix_send,
    mix_recv,
    move_send,
    move_recv,
    sum_send,
    sum_recv,
    gather_send,
    gather_recv,
):
    chips, lanes = sizes
    chip, lane = lax.axis_index("dp"), lax.axis_index("sp")
    slots, length, model = tokens_in.shape
    layers, rows, hidden_units = pre_act.shape
    ranks = down_low.shape[0]
    group = lanes // slots
    half, seat = lane // group, lax.rem(lane, group)
    parts = model // group // LANES
    heads = LANES // HEAD_SIZE
    per_tile = TILE // LANES
    tiles_each = model // TILE
    shares = hidden_units // TILE

    def gathers_of(layer):
        model_half, unit_half = 3 * model // 2, hidden_units // 2
        back_rows = shard_back.shape[1]
        back_half = back_rows // 2
        everything = pl.ds(0, model)
        plans = (
            (shard_qkv.at[layer], full_qkv, shard_qkv.shape[1], 0, pl.ds(0, model_half)),
            (shard_qkv.at[layer], full_qkv, shard_qkv.shape[1], 0, pl.ds(model_half, model_half)),
            (shard_out.at[layer], full_out, shard_out.shape[1], 0, everything),
            (shard_in.at[layer], full_in, shard_in.shape[1], 0, pl.ds(0, unit_half)),
            (shard_in.at[layer], full_in, shard_in.shape[1], 0, pl.ds(unit_half, unit_half)),
            (shard_back.at[layer, pl.ds(0, back_half)], full_back, back_rows, 0, everything),
            (
                shard_back.at[layer, pl.ds(back_half, back_half)],
                full_back,
                back_rows,
                back_half,
                everything,
            ),
        )
        return [
            Gather(
                shard,
                full.at[layer],
                stride,
                offset,
                columns,
                (chips, chip, lane),
                (gather_send.at[layer, index], gather_recv.at[layer, index]),
            )
            for index, (shard, full, stride, offset, columns) in enumerate(plans)
        ]

    gathers = [gathers_of(layer) for layer in range(layers)]

    def mates():
        return [lax.rem(seat + step, group) for step in range(1, group)]

    def device(mate):
        return (chip, half * group + mate)

    def lane_of(slot):
        return slot * group + lane // 2

    def move_in(kind, source, target):
        def copy(slot):
            return remote(
                source.at[slot],
                target.at[pl.ds(pl.multiple_of(lax.rem(lane, 2) * length, length), length)],
                move_send.at[kind, slot],
                move_recv.at[kind, lax.rem(lane, 2)],
                (chip, lane_of(slot)),
            )

        for slot in range(slots):

            @pl.when(lane_of(slot) != lane)
            def _():
                copy(slot).start()

            @pl.when(lane_of(slot) == lane)
            def _():
                start = pl.multiple_of(lax.rem(lane, 2) * length, length)
                target[pl.ds(start, length)] = source[slot]

    def move_in_wait(kind, source, target, sent):
        for step in range(2):
            sender = 2 * seat + step
            copy = remote(
                source.at[0],
                target.at[pl.ds(step * length, length)],
                move_send.at[kind, step],
                move_recv.at[kind, step],
                (chip, lane_of(step)),
            )
            if sent:

                @pl.when(lane_of(step) != lane)
                def _():
                    copy.wait_send()

            else:

                @pl.when(sender != lane)
                def _():
                    copy.wait_recv()

    def move_out(kind, source, target):
        for step in range(2):
            owner = 2 * seat + step
            part = pl.ds(step * length, length)

            @pl.when(owner != lane)
            def _():
                remote(
                    source.at[part],
                    target.at[half],
                    move_send.at[kind, step],
                    move_recv.at[kind, half],
                    (chip, owner),
                ).start()

            @pl.when(owner == lane)
            def _():
                target[half] = source[part]

    def move_out_wait(kind, source, target, sent):
        for step in range(2):
            owner = 2 * seat + step
            copy = remote(
                source.at[pl.ds(step * length, length)],
                target.at[step],
                move_send.at[kind, step],
                move_recv.at[kind, step],
                (chip, owner),
            )
            if sent:

                @pl.when(owner != lane)
                def _():
                    copy.wait_send()

            else:

                @pl.when(lane_of(step) != lane)
                def _():
                    copy.wait_recv()

    def heads_copy(part, mate, target, owner):
        return remote(
            heads_out.at[mate, part],
            target.at[owner, part],
            heads_send.at[part, mate],
            heads_recv.at[part, owner],
            device(mate),
        )

    def mix_copy(part, mate, source, target, owner):
        return remote(
            source.at[part, mate],
            target.at[owner, part],
            mix_send.at[part, mate],
            mix_recv.at[part, owner],
            device(mate),
        )

    def allowed_pairs(key_block, query_block, diagonal):
        place = lax.broadcasted_iota(jnp.int32, (rows, heads * rows), 0)
        begin_row = begin[pl.ds(half, 1), at_columns(query_block, rows)]
        begin_row = jnp.concatenate([begin_row] * heads, 1) - key_block * rows
        allowed = place >= begin_row
        if diagonal:
            column = lax.broadcasted_iota(jnp.int32, (1, heads * rows), 1)
            allowed = allowed & (place <= lax.rem(column, rows))
        return allowed

    def load_params(layer):
        scale = ADAPTER_ALPHA / (ranks // 2)
        down = jnp.concatenate([down_maps[layer, 0], down_maps[layer, 1]], 0)
        down_low[...] = down.astype(LOW)
        blank = jnp.zeros((ranks // 2, model), FULL)
        up_query = jnp.concatenate([scale * up_maps[layer, 0], blank], 0)
        up_value = jnp.concatenate([blank, scale * up_maps[layer, 1]], 0)
        up_low[:, :model] = up_query.astype(LOW)
        up_low[:, model : 2 * model] = jnp.zeros((ranks, model), LOW)
        up_low[:, 2 * model :] = up_value.astype(LOW)

    def forward(layer, following):
        get_qkv_a, get_qkv_b, get_out, get_in_a, get_in_b, get_back_a, get_back_b = gathers[layer]
        if layer == 0:
            get_qkv_a.begin()
            move_in(0, tokens_in, tokens_low)
            get_qkv_a.pass_on()
            get_qkv_b.begin()
        load_params(layer)
        qkv_bias[0:1, :model] = qv_bias[layer, 0:1]
        qkv_bias[0:1, model : 2 * model] = jnp.zeros((1, model), FULL)
        qkv_bias[0:1, 2 * model :] = qv_bias[layer, 1:2]
        qkv_bias[1:2, :model] = jnp.full((1, model), HEAD_SIZE ** (-0.5), FULL)
        qkv_bias[1:2, model:] = jnp.ones((1, 2 * model), FULL)
        if layer == 0:
            get_qkv_a.trade()
            move_in_wait(0, tokens_in, tokens_low, False)
            hidden[0] = tokens_low[...].astype(FULL)
        unit, _ = normalize(hidden[layer])
        normed[layer] = (unit * gains[layer, 0:1] + shifts[layer, 0:1]).astype(LOW)
        low_rank[layer] = dot_nt(normed[layer], down_low[...])
        if layer > 0:
            for part in range(parts):
                for mate in mates():
                    heads_copy(part, mate, heads_in.at[layer - 1], seat).wait_send()
        get_qkv_b.pass_on()
        get_out.begin()
        get_in_a.begin()
        get_qkv_a.cross()

        def qkv_run(first_tile, count):
            def copies(index, slot):
                columns = at_columns(first_tile + index, TILE)
                return [
                    pltpu.make_async_copy(
                        full_qkv.at[layer, :, columns], tile_in.at[slot], tile_sem.at[0, slot]
                    )
                ]

            def body(index, slot):
                tile = first_tile + index
                columns = at_columns(tile, TILE)
                value = dot_nn(normed[layer], tile_in[slot])
                value += dot_nn(low_rank[layer].astype(LOW), up_low[:, columns])
                value += qkv_bias[0:1, columns]
                value = (value * qkv_bias[1:2, columns]).astype(LOW)
                kind = tile // tiles_each
                first = lax.rem(tile, tiles_each) * (per_tile // parts)
                for step in range(per_tile):
                    heads_out[first + step // parts, step % parts, kind] = value[
                        :, step * LANES : (step + 1) * LANES
                    ]

            prime(count, copies)
            stream(count, copies, body)

        tile_count = 3 * tiles_each
        get_qkv_a.arrive()
        qkv_run(0, tile_count // 2)
        get_qkv_b.trade()
        get_qkv_b.cross()
        get_qkv_b.arrive()
        qkv_run(tile_count // 2, tile_count // 2)
        arrivals = heads_in.at[layer]
        for part in range(parts):
            for mate in mates():
                heads_copy(part, mate, arrivals, seat).start()
            heads_in[layer, seat, part] = heads_out[seat, part]
        get_out.pass_on()
        get_in_a.pass_on()
        get_in_b.begin()

        def attend(part):
            def query_step(query_block, carry):
                query_heads = split_heads(heads_in[layer, query_block, part, 0])

                def score_step(key_block, best, diagonal=False):
                    found = dot_nt(heads_in[layer, key_block, part, 1], query_heads)
                    allowed = allowed_pairs(key_block, query_block, diagonal)
                    found = jnp.where(allowed, found, MASKED)
                    scores[key_block] = found
                    return jnp.maximum(best, jnp.max(found, 0, keepdims=True))

                lowest = jnp.full((1, heads * rows), MASKED, FULL)
                best = lax.fori_loop(0, query_block, score_step, lowest)
                best = score_step(query_block, best, True)

                def mix_step(key_block, carried):
                    sums, mix = carried
                    raised = jnp.exp(scores[key_block] - best)
                    sums = sums + jnp.sum(raised, 0, keepdims=True)
                    return sums, mix + dot_tn(heads_in[layer, key_block, part, 2], raised.astype(LOW))

                nothing = jnp.zeros((1, heads * rows), FULL), jnp.zeros((LANES, heads * rows), FULL)
                sums, mix = lax.fori_loop(0, query_block + 1, mix_step, nothing)
                log_total[layer, part, query_block] = best + jnp.log(sums)
                mixed[layer, part, query_block] = join_heads(mix * (1.0 / sums), rows).astype(LOW)

                @pl.when(query_block != seat)
                def _():
                    mix_copy(part, query_block, mixed.at[layer], mixture, seat).start()

                return carry

            lax.fori_loop(0, group, query_step, 0)
            mixture[seat, part] = mixed[layer, part, seat]

        load = pltpu.make_async_copy(full_out.at[layer], out_weight, load_sem.at[0])
        for part in range(parts):
            for mate in mates():
                heads_copy(part, mate, arrivals, mate).wait_recv()
            attend(part)
            if part == 0:
                get_out.trade()
                get_in_b.pass_on()
                get_back_a.begin()
                get_in_a.trade()
        get_back_a.pass_on()
        get_back_b.begin()
        get_out.cross()
        get_out.arrive()
        load.start()
        get_in_b.trade()
        get_in_a.cross()

        for part in range(parts):
            for mate in mates():
                mix_copy(part, mate, mixed.at[layer], mixture, mate).wait_recv()
        load.wait()
        total[...] = hidden[layer] + out_bias[layer : layer + 1]

        def out_body(index, carry):
            joined = jnp.concatenate([mixture[index, part] for part in range(parts)], 1)
            start = pl.multiple_of(index * parts * LANES, parts * LANES)
            total[...] += dot_nn(joined, out_weight[pl.ds(start, parts * LANES)])
            return carry

        lax.fori_loop(0, group, out_body, 0)
        attended[layer] = total[...]
        unit, _ = normalize(total[...])
        second = (unit * gains[layer, 1:2] + shifts[layer, 1:2]).astype(LOW)

        def in_run(first_tile, count):
            def copies(index, slot):
                columns = at_columns(first_tile + index, TILE)
                return [
                    pltpu.make_async_copy(
                        full_in.at[layer, :, columns], tile_in.at[slot], tile_sem.at[0, slot]
                    )
                ]

            def body(index, slot):
                tile = first_tile + index
                columns = at_columns(tile, TILE)
                value = dot_nn(second, tile_in[slot]) + in_bias[layer : layer + 1, columns]
                pre_act[layer, :, columns] = value.astype(LOW)
                activation[tile] = gelu(value).astype(LOW)

            prime(count, copies)
            stream(count, copies, body)

        get_back_a.trade()
        get_in_a.arrive()
        in_run(0, shares // 2)
        get_back_b.pass_on()
        if following is not None:
            following[0].begin()
        get_in_b.cross()
        get_in_b.arrive()
        in_run(shares // 2, shares // 2)
        if following is not None:
            move_in(1, cotangent_in, cotangent_low)
        get_back_a.cross()
        for part in range(parts):
            for mate in mates():
                mix_copy(part, mate, mixed.at[layer], mixture, seat).wait_send()

    def back_run(layer, first_tile, ready=False):
        def copies(index, slot):
            return [
                pltpu.make_async_copy(
                    full_back.at[layer, at_columns(2 * index + first_tile, TILE)],
                    tile_back.at[slot],
                    tile_sem.at[1, slot],
                )
            ]

        def body(index, slot):
            total[...] += dot_nn(activation[2 * index + first_tile], tile_back[slot])

        prime(shares // 2, copies)
        stream(shares // 2, copies, body)

    def grad_tile(index):
        pairs = shares // 2
        return 2 * lax.rem(index, pairs) + index // pairs

    def grad_copies(layer, first):
        def copies(index, slot):
            columns = at_columns(grad_tile(first + index), TILE)
            return [
                pltpu.make_async_copy(
                    full_in.at[layer, :, columns], tile_in.at[slot], tile_sem.at[0, slot]
                ),
                pltpu.make_async_copy(
                    full_back.at[layer, columns], tile_back.at[slot], tile_sem.at[1, slot]
                ),
            ]

        return copies

    def grad_run(layer, low_gradient, first, count):
        def body(index, slot):
            columns = at_columns(grad_tile(first + index), TILE)
            grad_act = dot_nt(low_gradient, tile_back[slot])
            slope = gelu_slope(pre_act[layer, :, columns].astype(FULL))
            grad_pre = (slope * grad_act).astype(LOW)
            total[...] += dot_nt(grad_pre, tile_in[slot])

        stream(count, grad_copies(layer, first), body)

    def backward(layer, last):
        load_out = pltpu.make_async_copy(full_out.at[layer], out_weight, load_sem.at[0])
        load_qkv = pltpu.make_async_copy(full_qkv.at[layer], qkv_weight, load_sem.at[1])
        if last:
            load_out.start()
        load_qkv.start()
        load_params(layer)
        low_gradient = gradient[...].astype(LOW)
        total[...] = jnp.zeros_like(total)
        if last:
            get_back_a, get_back_b = gathers[layer][5:7]
            get_back_b.trade()
            get_back_a.arrive()
            prime(shares // 2, grad_copies(layer, 0))
            grad_run(layer, low_gradient, 0, shares // 2)
            get_back_b.cross()
            get_back_b.arrive()
            prime(shares // 2, grad_copies(layer, shares // 2))
            grad_run(layer, low_gradient, shares // 2, shares // 2)
        else:
            grad_run(layer, low_gradient, 0, shares)
        grad_attended[...] = gradient[...] + norm_backward(
            attended[layer], gains[layer, 1:2], total[...]
        )
        low_attended = grad_attended[...].astype(LOW)
        load_out.wait()
        if not last:
            for part in range(parts):
                for mate in mates():
                    mix_copy(part, mate, mix_out, mix_in, seat).wait_send()

        def mix_body(index, carry):
            start = pl.multiple_of(index * parts * LANES, parts * LANES)
            value = dot_nt(low_attended, out_weight[pl.ds(start, parts * LANES)]).astype(LOW)
            for part in range(parts):
                mix_out[part, index] = value[:, part * LANES : (part + 1) * LANES]
            return carry

        lax.fori_loop(0, group, mix_body, 0)
        for part in range(parts):
            for mate in mates():
                mix_copy(part, mate, mix_out, mix_in, seat).start()
            mix_in[seat, part] = mix_out[part, seat]
            for mate in mates():
                heads_copy(part, mate, grads_in, seat).wait_send()
        if last:
            total[...] = attended[layer] + back_bias[layer : layer + 1]
            back_run(layer, 0)
            back_run(layer, 1)
            result_low[...] = total[...].astype(LOW)
        if layer > 0:
            pltpu.make_async_copy(full_out.at[layer - 1], out_weight, load_sem.at[0]).start()
            prime(shares, grad_copies(layer - 1, 0))

        def attend(part):
            def prepare(block, carry):
                queries[block] = split_heads(heads_in[layer, block, part, 0])
                grads = split_heads(mix_in[block, part])
                mix_heads[block] = grads
                mix = jnp.concatenate([mixed[layer, part, block]] * heads, 0)
                product = grads.astype(FULL) * mix.astype(FULL)
                delta[block] = jnp.sum(product.T, 0, keepdims=True)
                query_sum[block] = jnp.zeros_like(query_sum[block])
                return carry

            lax.fori_loop(0, group, prepare, 0)

            def key_step(key_block, carry):
                keys = heads_in[layer, key_block, part, 1]
                values = heads_in[layer, key_block, part, 2]
                key_sum[...] = jnp.zeros_like(key_sum)
                value_sum[...] = jnp.zeros_like(value_sum)

                def query_step(query_block, inner, diagonal=False):
                    query_heads = queries[query_block]
                    grad_heads = mix_heads[query_block]
                    found = dot_nt(keys, query_heads)
                    raised = jnp.exp(found - log_total[layer, part, query_block])
                    allowed = allowed_pairs(key_block, query_block, diagonal)
                    weights = jnp.where(allowed, raised, 0.0)
                    value_sum[...] += dot_nn(weights.astype(LOW), grad_heads)
                    grad_weights = dot_nt(values, grad_heads)
                    grad_scores = weights * (grad_weights - delta[query_block])
                    grad_scores = grad_scores.astype(LOW)
                    key_sum[...] += dot_nn(grad_scores, query_heads)
                    query_sum[query_block] += dot_tn(keys, grad_scores)
                    return inner

                query_step(key_block, 0, True)
                lax.fori_loop(key_block + 1, group, query_step, 0)
                out = join_heads(query_sum[key_block], rows).astype(LOW)
                heads_out[key_block, part, 0] = out * jnp.asarray(HEAD_SIZE ** (-0.5), LOW)
                heads_out[key_block, part, 1] = key_sum[...].astype(LOW)
                heads_out[key_block, part, 2] = value_sum[...].astype(LOW)

                @pl.when(key_block != seat)
                def _():
                    heads_copy(part, key_block, grads_in, seat).start()

                return carry

            lax.fori_loop(0, group, key_step, 0)
            grads_in[seat, part] = heads_out[seat, part]

        for part in range(parts):
            for mate in mates():
                mix_copy(part, mate, mix_out, mix_in, mate).wait_recv()
            attend(part)

        load_qkv.wait()
        for part in range(parts):
            for mate in mates():
                heads_copy(part, mate, grads_in, mate).wait_recv()
            for owner in range(group):
                for kind in range(3):
                    start = kind * model + (owner * parts + part) * LANES
                    grads_flat[:, start : start + LANES] = grads_in[owner, part, kind]

        grad_low = dot_nt(grads_flat[...], up_low[...]).astype(LOW)
        scale = ADAPTER_ALPHA / (ranks // 2)
        low_values = (low_rank[layer] * scale).astype(LOW)
        rank = ranks // 2
        down_terms = dot_tn(grad_low, normed[layer])
        terms[4 * layer] = down_terms[:rank]
        terms[4 * layer + 1] = down_terms[rank:]
        terms[4 * layer + 2] = dot_tn(low_values, grads_flat[:, :model])[:rank]
        terms[4 * layer + 3] = dot_tn(low_values, grads_flat[:, 2 * model :])[rank:]
        if not last:
            sum_begin()
        total[...] = dot_nn(grad_low, down_low[...])

        def qkv_body(index, carry):
            columns = at_columns(index, TILE)
            total[...] += dot_nt(grads_flat[:, columns], qkv_weight[:, columns])
            return carry

        lax.fori_loop(0, 3 * tiles_each, qkv_body, 0)
        gradient[...] = grad_attended[...] + norm_backward(
            hidden[layer], gains[layer, 0:1], total[...]
        )

    def sum_lanes():
        return [
            remote(
                terms.at[lax.rem(lane + step, lanes)],
                landing.at[lane],
                sum_send.at[0, step],
                sum_recv.at[0, step],
                (chip, lax.rem(lane + step, lanes)),
            )
            for step in range(1, lanes)
        ]

    def sum_spread():
        return [
            remote(
                summed.at[lane],
                summed.at[lane],
                sum_send.at[1, step],
                sum_recv.at[1, step],
                (chip, lax.rem(lane + step, lanes)),
            )
            for step in range(1, lanes)
        ]

    def sum_chips():
        return [
            remote(
                summed,
                landing_chips.at[chip],
                sum_send.at[2, step],
                sum_recv.at[2, step],
                (lax.rem(chip + step, chips), lane),
            )
            for step in range(1, chips)
        ]

    def sum_begin():
        for copy in sum_lanes():
            copy.start()
        landing[lane] = terms[lane]

    def sum_lanes_finish():
        for copy in sum_lanes():
            copy.wait()
        summed[lane] = jnp.sum(landing[...], axis=0)
        for copy in sum_spread():
            copy.start()

    def sum_finish():
        for copy in sum_spread():
            copy.wait()
        for copy in sum_chips():
            copy.start()
        landing_chips[chip] = summed[...]
        for copy in sum_chips():
            copy.wait()
        scale = 1.0 / math.sqrt(slots * chips * length * lanes)
        for layer in range(layers):
            for kind in range(2):
                for grads, entry in ((grad_down, kind), (grad_up, 2 + kind)):
                    terms_of = landing_chips[:, 4 * layer + entry]
                    grads[layer, kind] = jnp.sum(terms_of, axis=0) * scale

    barrier = pltpu.get_barrier_semaphore()
    friends = [(chip, lax.rem(lane + step, lanes)) for step in range(1, lanes)]
    friends += [(lax.rem(chip + step, chips), lane) for step in range(1, chips)]
    for friend in friends:
        pl.semaphore_signal(barrier, inc=1, device_id=friend, device_id_type=MESH)
    pl.semaphore_wait(barrier, len(friends))

    for layer in range(layers):
        last = layer + 1 == layers
        forward(layer, None if last else gathers[layer + 1])
        if not last:
            total[...] = attended[layer] + back_bias[layer : layer + 1]
            get_back_a, get_back_b = gathers[layer][5:7]
            get_back_a.arrive()
            back_run(layer, 0)
            gathers[layer + 1][0].pass_on()
            gathers[layer + 1][1].begin()
            get_back_b.trade()
            get_back_b.cross()
            get_back_b.arrive()
            back_run(layer, 1)
            hidden[layer + 1] = total[...]
            gathers[layer + 1][0].trade()
    move_in_wait(1, cotangent_in, cotangent_low, False)
    gradient[...] = cotangent_low[...].astype(FULL)
    for layer in reversed(range(layers)):
        last = layer + 1 == layers
        backward(layer, last)
        if last:
            move_out(2, result_low, output)
    return_out[...] = gradient[...].astype(LOW)
    sum_lanes_finish()
    move_out(3, return_out, input_grad)
    sum_finish()
    move_out_wait(2, result_low, output, False)
    move_out_wait(3, return_out, input_grad, False)

    move_in_wait(0, tokens_in, tokens_low, True)
    move_in_wait(1, cotangent_in, cotangent_low, True)
    move_out_wait(2, result_low, output, True)
    move_out_wait(3, return_out, input_grad, True)
    for layer_gathers in gathers:
        for gather in layer_gathers:
            gather.drain()
    for part in range(parts):
        for mate in mates():
            mix_copy(part, mate, mix_out, mix_in, seat).wait_send()
            heads_copy(part, mate, grads_in, seat).wait_send()


def fast_body(sizes, *arrays):
    chips, lanes = sizes
    tokens, _, _, *shards = arrays[:7]
    slots, length, model = tokens.shape
    layers, kinds, rank, _ = arrays[-1].shape
    hidden_units = shards[2].shape[2]
    group = lanes // slots
    rows, ranks = slots * length, kinds * rank
    parts, heads = model // group // LANES, LANES // HEAD_SIZE
    vmem = pl.BlockSpec(memory_space=pltpu.VMEM)
    anywhere = pl.BlockSpec(memory_space=pl.ANY)
    shape, dma = jax.ShapeDtypeStruct, pltpu.SemaphoreType.DMA
    scratch = [
        ((layers, rows, model), FULL),
        ((rows, model), LOW),
        ((rows, model), LOW),
        ((layers, rows, model), LOW),
        ((layers, rows, ranks), FULL),
        ((layers, group, parts, 3, rows, LANES), LOW),
        ((layers, parts, group, rows, LANES), LOW),
        ((layers, parts, group, 1, heads * rows), FULL),
        ((layers, rows, model), FULL),
        ((layers, rows, hidden_units), LOW),
        ((DEPTH, model, TILE), LOW),
        ((DEPTH, TILE, model), LOW),
        ((model, model), LOW),
        ((model, 3 * model), LOW),
        ((group, parts, 3, rows, LANES), LOW),
        ((group, parts, rows, LANES), LOW),
        ((group, rows, heads * rows), FULL),
        ((hidden_units // TILE, rows, TILE), LOW),
        ((rows, model), FULL),
        ((rows, model), FULL),
        ((rows, model), FULL),
        ((parts, group, rows, LANES), LOW),
        ((group, parts, rows, LANES), LOW),
        ((group, heads * rows, LANES), LOW),
        ((group, heads * rows, LANES), LOW),
        ((group, 1, heads * rows), FULL),
        ((group, LANES, heads * rows), FULL),
        ((rows, LANES), FULL),
        ((rows, LANES), FULL),
        ((group, parts, 3, rows, LANES), LOW),
        ((rows, 3 * model), LOW),
        ((2, 3 * model), FULL),
        ((ranks, 3 * model), LOW),
        ((ranks, model), LOW),
        ((rows, model), LOW),
        ((rows, model), LOW),
        ((lanes, rank, model), FULL),
        ((lanes, rank, model), FULL),
        ((chips, lanes, rank, model), FULL),
        ((lanes, rank, model), FULL),
    ]
    semaphores = [
        (2, DEPTH),
        (2,),
        (parts, group),
        (parts, group),
        (parts, group),
        (parts, group),
        (4, 2),
        (4, 2),
        (3, lanes),
        (3, lanes),
        (layers, 7, 11),
        (layers, 7, 11),
    ]
    results = pl.pallas_call(
        partial(train_kernel, sizes),
        out_shape=(
            shape((slots, length, model), LOW),
            shape((slots, length, model), LOW),
            shape((layers, kinds, rank, model), FULL),
            shape((layers, kinds, rank, model), FULL),
        )
        + tuple(shape((layers, chips * part.shape[1], part.shape[2]), LOW) for part in shards),
        in_specs=[vmem] * 3 + [anywhere] * 4 + [vmem] * 8,
        out_specs=(vmem,) * 4 + (anywhere,) * 4,
        scratch_shapes=[pltpu.VMEM(*entry) for entry in scratch]
        + [dma(entry) for entry in semaphores],
        name="train",
        compiler_params=pltpu.CompilerParams(
            collective_id=0, has_side_effects=True, vmem_limit_bytes=VMEM_LIMIT
        ),
    )(*arrays)
    output, input_grad, grad_down, grad_up = results[:4]
    return output.astype(FULL), input_grad.astype(FULL), grad_down, grad_up


def solution(mesh):
    chips, lanes = sizes = tuple(mesh.devices.shape)
    fast = sizes == (4, 8)
    token_axes = "sp" if fast else SP
    if not fast:
        mesh = Mesh(mesh.devices.reshape(chips, lanes // 2, 2), ("dp",) + SP)
    tokens = P("dp", token_axes, None)
    weights = P(None, "dp", None)
    return jax.shard_map(
        partial(fast_body, sizes) if fast else body,
        mesh=mesh,
        in_specs=(tokens, tokens, P("dp", None)) + (weights,) * 4 + (P(),) * 8,
        out_specs=(tokens, tokens, P(), P()),
        check_vma=False,
    )
```

```python
from functools import partial
import math

import jax
import jax.numpy as jnp
from jax import lax
from jax.experimental import pallas as pl
from jax.experimental.pallas import tpu as pltpu
from jax.sharding import Mesh, PartitionSpec as P

HEAD_SIZE = 64


EPSILON = 1e-05
ADAPTER_ALPHA = 32.0
EXACT_PRECISION = lax.Precision.HIGHEST
MASKED = -1e30
SP = ("z", "core")


def layer_norm(tensor, gains, shifts):
    row_mean = jnp.mean(tensor, -1, keepdims=True)
    centred = tensor - row_mean
    spread = jnp.mean(centred * centred, -1, keepdims=True)
    return centred * lax.rsqrt(spread + EPSILON) * gains + shifts


def fetch_weights(
    query_key_value_weight,
    attention_out_weight,
    feedforward_in_weight,
    feedforward_out_weight,
    layer_number,
):
    core = lax.axis_index("core")

    def fetch(shards):
        half = shards.shape[1] // 2
        part = lax.dynamic_slice_in_dim(shards[layer_number], core * half, half, 0)
        return lax.all_gather(part, ("dp", "core"), axis=0, tiled=True)

    return (
        fetch(query_key_value_weight),
        fetch(attention_out_weight),
        fetch(feedforward_in_weight),
        fetch(feedforward_out_weight),
    )


def sum_kernel(sizes, terms_ref, out_ref, landing, send_sem, recv_sem, send_sem2, recv_sem2):
    count = math.prod(sizes)
    me = [lax.axis_index(name) for name in ("dp", "z", "core")]
    mine = (me[0] * sizes[1] + me[1]) * sizes[2] + me[2]

    def place(step):
        other = lax.rem(mine + step, count)
        return other, (
            other // (sizes[1] * sizes[2]),
            lax.rem(other // sizes[2], sizes[1]),
            lax.rem(other, sizes[2]),
        )

    barrier = pltpu.get_barrier_semaphore()
    for step in range(1, count):
        pl.semaphore_signal(
            barrier, inc=1, device_id=place(step)[1], device_id_type=pl.DeviceIdType.MESH
        )
    pl.semaphore_wait(barrier, count - 1)

    def scatter(step):
        other, device = place(step)
        return pltpu.make_async_remote_copy(
            src_ref=terms_ref.at[other],
            dst_ref=landing.at[step],
            send_sem=send_sem.at[step],
            recv_sem=recv_sem.at[step],
            device_id=device,
            device_id_type=pl.DeviceIdType.MESH,
        )

    def spread(step):
        other, device = place(step)
        return pltpu.make_async_remote_copy(
            src_ref=out_ref.at[mine],
            dst_ref=out_ref.at[mine],
            send_sem=send_sem2.at[step],
            recv_sem=recv_sem2.at[step],
            device_id=device,
            device_id_type=pl.DeviceIdType.MESH,
        )

    for step in range(1, count):
        scatter(step).start()
    landing[0] = terms_ref[mine]
    for step in range(1, count):
        scatter(step).wait()
    out_ref[mine] = jnp.sum(landing[...], axis=0)
    for step in range(1, count):
        spread(step).start()
    for step in range(1, count):
        spread(step).wait()


def sum_adapters(down_terms, up_terms):
    sizes = [lax.axis_size(name) for name in ("dp", "z", "core")]
    count = math.prod(sizes)
    packed = jnp.stack([down_terms, up_terms])
    if count > 64 or packed.size % (count * 1024) != 0:
        return lax.psum((down_terms, up_terms), ("dp", "z", "core"))
    pieces = packed.reshape(count, -1, 128)
    vmem = pl.BlockSpec(memory_space=pltpu.VMEM)
    summed = pl.pallas_call(
        partial(sum_kernel, sizes),
        out_shape=jax.ShapeDtypeStruct(pieces.shape, jnp.float32),
        in_specs=[vmem],
        out_specs=vmem,
        scratch_shapes=[pltpu.VMEM(pieces.shape, jnp.float32)]
        + [pltpu.SemaphoreType.DMA((count,))] * 4,
        name="adapter_sum",
        compiler_params=pltpu.CompilerParams(collective_id=0, has_side_effects=True),
    )(pieces)
    summed = summed.reshape(packed.shape)
    return summed[0], summed[1]


def slot_scores(query_rows, key_rows, document_starts):
    length = query_rows.shape[0]
    heads_q = query_rows.reshape(length, -1, HEAD_SIZE)
    heads_k = key_rows.reshape(length, -1, HEAD_SIZE)
    scores = jnp.einsum("qhd,khd->hqk", heads_q, heads_k, preferred_element_type=jnp.float32)
    places = jnp.arange(length)
    allowed = (document_starts[:, None] == document_starts[None, :]) & (
        places[None, :] <= places[:, None]
    )
    return jnp.where(allowed[None], scores, MASKED)


def slot_forward(slot_items):
    query_rows, key_rows, value_rows, document_starts = slot_items
    length = query_rows.shape[0]
    scores = slot_scores(query_rows, key_rows, document_starts)
    row_max = jnp.max(scores, -1, keepdims=True)
    row_total = jnp.sum(jnp.exp(scores - row_max), -1, keepdims=True)
    log_total = row_max + jnp.log(row_total)
    probability = jnp.exp(scores - log_total).astype(jnp.bfloat16)
    mixture = jnp.einsum(
        "hqk,khd->qhd",
        probability,
        value_rows.reshape(length, -1, HEAD_SIZE),
        preferred_element_type=jnp.float32,
    )
    return (mixture.reshape(length, -1).astype(jnp.bfloat16), log_total[..., 0])


def slot_backward(slot_items):
    query_rows, key_rows, value_rows, document_starts, log_total, grad_mixture = slot_items
    length = query_rows.shape[0]
    scores = slot_scores(query_rows, key_rows, document_starts)
    probability = jnp.exp(scores - log_total[..., None])
    low_probability = probability.astype(jnp.bfloat16)
    grad_heads = grad_mixture.reshape(length, -1, HEAD_SIZE)
    value_heads = value_rows.reshape(length, -1, HEAD_SIZE)
    grad_values = jnp.einsum(
        "hqk,qhd->khd", low_probability, grad_heads, preferred_element_type=jnp.float32
    )
    grad_prob = jnp.einsum(
        "qhd,khd->hqk", grad_heads, value_heads, preferred_element_type=jnp.float32
    )
    grad_scores = probability * (grad_prob - jnp.sum(probability * grad_prob, -1, keepdims=True))
    low_scores = grad_scores.astype(jnp.bfloat16)
    grad_queries = jnp.einsum(
        "hqk,khd->qhd",
        low_scores,
        key_rows.reshape(length, -1, HEAD_SIZE),
        preferred_element_type=jnp.float32,
    )
    grad_keys = jnp.einsum(
        "hqk,qhd->khd",
        low_scores,
        query_rows.reshape(length, -1, HEAD_SIZE),
        preferred_element_type=jnp.float32,
    )
    return (
        grad_queries.reshape(length, -1).astype(jnp.bfloat16),
        grad_keys.reshape(length, -1).astype(jnp.bfloat16),
        grad_values.reshape(length, -1).astype(jnp.bfloat16),
    )


def layer_forward(hidden_state, weight_set, params, document_begin):
    query_key_value_weight, attention_out_weight, feedforward_in_weight, feedforward_out_weight = (
        weight_set
    )
    (
        query_value_bias,
        attention_out_bias,
        feedforward_in_bias,
        feedforward_out_bias,
        gains,
        shifts,
        down_projection,
        up_projection,
    ) = params
    model_dimension = hidden_state.shape[-1]
    normed = layer_norm(hidden_state, gains[0], shifts[0]).astype(jnp.bfloat16)
    projected_rows = jnp.einsum(
        "std,de->ste", normed, query_key_value_weight, preferred_element_type=jnp.float32
    )
    widened = normed.astype(jnp.float32)
    adapter_scale = ADAPTER_ALPHA / down_projection.shape[1]
    query_row_block = jnp.einsum(
        "nyh,lh->nyl", widened, down_projection[0], precision=EXACT_PRECISION
    )
    value_row_block = jnp.einsum(
        "nyh,lh->nyl", widened, down_projection[1], precision=EXACT_PRECISION
    )
    query_rows = (
        (
            projected_rows[..., :model_dimension]
            + query_value_bias[0]
            + adapter_scale
            * jnp.einsum(
                "wah,hp->wap", query_row_block, up_projection[0], precision=EXACT_PRECISION
            )
        )
        * HEAD_SIZE ** (-0.5)
    ).astype(jnp.bfloat16)
    key_rows = projected_rows[..., model_dimension : 2 * model_dimension].astype(jnp.bfloat16)
    value_rows = (
        projected_rows[..., 2 * model_dimension :]
        + query_value_bias[1]
        + adapter_scale
        * jnp.einsum("wah,hp->wap", value_row_block, up_projection[1], precision=EXACT_PRECISION)
    ).astype(jnp.bfloat16)
    queries_h, keys_h, values_h = lax.all_to_all(
        jnp.stack([query_rows, key_rows, value_rows]), SP, split_axis=3, concat_axis=2, tiled=True
    )
    mixture_h, log_total = lax.map(slot_forward, (queries_h, keys_h, values_h, document_begin))
    mixture = lax.all_to_all(mixture_h, SP, split_axis=1, concat_axis=2, tiled=True)
    attended = hidden_state + (
        jnp.einsum("std,de->ste", mixture, attention_out_weight, preferred_element_type=jnp.float32)
        + attention_out_bias
    )
    normed_mlp = layer_norm(attended, gains[1], shifts[1]).astype(jnp.bfloat16)
    pre_act = (
        jnp.einsum(
            "std,df->stf", normed_mlp, feedforward_in_weight, preferred_element_type=jnp.float32
        )
        + feedforward_in_bias
    )
    activation = jax.nn.gelu(pre_act, approximate=True).astype(jnp.bfloat16)
    final_result = attended + (
        jnp.einsum(
            "stf,fd->std", activation, feedforward_out_weight, preferred_element_type=jnp.float32
        )
        + feedforward_out_bias
    )
    saved_state = (
        normed,
        query_row_block,
        value_row_block,
        queries_h,
        keys_h,
        values_h,
        log_total,
        attended,
        pre_act,
    )
    return (final_result, saved_state)


def layer_backward(hidden_state, gradient, weight_set, params, document_begin, saved_state):
    query_key_value_weight, attention_out_weight, feedforward_in_weight, feedforward_out_weight = (
        weight_set
    )
    (
        query_value_bias,
        attention_out_bias,
        feedforward_in_bias,
        feedforward_out_bias,
        gains,
        shifts,
        down_projection,
        up_projection,
    ) = params
    (
        normed,
        query_row_block,
        value_row_block,
        queries_h,
        keys_h,
        values_h,
        log_total,
        attended,
        pre_act,
    ) = saved_state
    grad_act = jnp.einsum(
        "std,fd->stf",
        gradient.astype(jnp.bfloat16),
        feedforward_out_weight,
        preferred_element_type=jnp.float32,
    )
    unused_act, gelu_back = jax.vjp(partial(jax.nn.gelu, approximate=True), pre_act)
    grad_pre = gelu_back(grad_act)[0].astype(jnp.bfloat16)
    grad_normed_mlp = jnp.einsum(
        "stf,df->std", grad_pre, feedforward_in_weight, preferred_element_type=jnp.float32
    )
    unused_norm, second_back = jax.vjp(
        lambda tensor: layer_norm(tensor, gains[1], shifts[1]), attended
    )
    grad_attended = gradient + second_back(grad_normed_mlp)[0]
    grad_mixture = jnp.einsum(
        "ste,de->std",
        grad_attended.astype(jnp.bfloat16),
        attention_out_weight,
        preferred_element_type=jnp.float32,
    ).astype(jnp.bfloat16)
    grad_mixture_h = lax.all_to_all(grad_mixture, SP, split_axis=2, concat_axis=1, tiled=True)
    grad_q_h, grad_k_h, grad_v_h = lax.map(
        slot_backward, (queries_h, keys_h, values_h, document_begin, log_total, grad_mixture_h)
    )
    grad_queries, grad_keys, grad_values = lax.all_to_all(
        jnp.stack([grad_q_h, grad_k_h, grad_v_h]), SP, split_axis=2, concat_axis=3, tiled=True
    )
    grad_queries = grad_queries * jnp.asarray(HEAD_SIZE ** (-0.5), jnp.bfloat16)
    stacked = jnp.concatenate([grad_queries, grad_keys, grad_values], -1)
    grad_normed = jnp.einsum(
        "ste,de->std", stacked, query_key_value_weight, preferred_element_type=jnp.float32
    )
    adapter_scale = ADAPTER_ALPHA / down_projection.shape[1]
    widened = normed.astype(jnp.float32)
    query_widened = grad_queries.astype(jnp.float32)
    value_widened = grad_values.astype(jnp.float32)
    query_row_gradient = adapter_scale * jnp.einsum(
        "nyh,lh->nyl", query_widened, up_projection[0], precision=EXACT_PRECISION
    )
    value_row_gradient = adapter_scale * jnp.einsum(
        "nyh,lh->nyl", value_widened, up_projection[1], precision=EXACT_PRECISION
    )
    query_up_weight = adapter_scale * jnp.einsum(
        "fkp,fkz->pz", query_row_block, query_widened, precision=EXACT_PRECISION
    )
    value_up_weight = adapter_scale * jnp.einsum(
        "fkp,fkz->pz", value_row_block, value_widened, precision=EXACT_PRECISION
    )
    down_q = jnp.einsum("fkp,fkz->pz", query_row_gradient, widened, precision=EXACT_PRECISION)
    down_v = jnp.einsum("fkp,fkz->pz", value_row_gradient, widened, precision=EXACT_PRECISION)
    grad_normed = (
        grad_normed
        + jnp.einsum(
            "wah,hp->wap", query_row_gradient, down_projection[0], precision=EXACT_PRECISION
        )
        + jnp.einsum(
            "wah,hp->wap", value_row_gradient, down_projection[1], precision=EXACT_PRECISION
        )
    )
    unused_first, first_back = jax.vjp(
        lambda tensor: layer_norm(tensor, gains[0], shifts[0]), hidden_state
    )
    grad_hidden = grad_attended + first_back(grad_normed)[0]
    return (grad_hidden, jnp.stack([down_q, down_v]), jnp.stack([query_up_weight, value_up_weight]))


def body(
    first_layer_input,
    cotangent,
    document_begin,
    query_key_value_weight,
    attention_out_weight,
    feedforward_in_weight,
    feedforward_out_weight,
    query_value_bias,
    attention_out_bias,
    feedforward_in_bias,
    feedforward_out_bias,
    layernorm_gain,
    layernorm_bias,
    adapter_down_maps,
    adapter_up_maps,
):
    layers = query_key_value_weight.shape[0]

    def params_of(layer_number):
        return (
            query_value_bias[layer_number],
            attention_out_bias[layer_number],
            feedforward_in_bias[layer_number],
            feedforward_out_bias[layer_number],
            layernorm_gain[layer_number],
            layernorm_bias[layer_number],
            adapter_down_maps[layer_number],
            adapter_up_maps[layer_number],
        )

    hidden_state = first_layer_input.astype(jnp.float32)
    inputs = []
    gathered = []
    kept = []
    for layer_number in range(layers):
        weight_set = fetch_weights(
            query_key_value_weight,
            attention_out_weight,
            feedforward_in_weight,
            feedforward_out_weight,
            layer_number,
        )
        inputs.append(hidden_state)
        gathered.append(weight_set)
        hidden_state, saved_state = layer_forward(
            hidden_state, weight_set, params_of(layer_number), document_begin
        )
        kept.append(saved_state)
    gradient = cotangent.astype(jnp.float32)
    down_parts = [None] * layers
    up_parts = [None] * layers
    for layer_number in reversed(range(layers)):
        gradient, down_terms, up_terms = layer_backward(
            inputs[layer_number],
            gradient,
            gathered[layer_number],
            params_of(layer_number),
            document_begin,
            kept[layer_number],
        )
        down_parts[layer_number] = down_terms
        up_parts[layer_number] = up_terms
    grad_down = jnp.stack(down_parts)
    grad_up = jnp.stack(up_parts)
    grad_down, grad_up = sum_adapters(grad_down, grad_up)
    tokens = (
        first_layer_input.shape[0]
        * first_layer_input.shape[1]
        * lax.axis_size("dp")
        * lax.axis_size("z")
        * lax.axis_size("core")
    )
    token_scale = 1.0 / math.sqrt(tokens)
    return (hidden_state, gradient, grad_down * token_scale, grad_up * token_scale)


MESH = pl.DeviceIdType.MESH
TILE = 512
LANES = 128
DEPTH = 4
SHARED = ((), ())
VMEM_LIMIT = 60 * 1024 * 1024
LOW, FULL = jnp.bfloat16, jnp.float32


def dot_nn(left, right):
    return jnp.dot(left, right, preferred_element_type=FULL)


def dot_nt(left, right):
    return lax.dot_general(left, right, (((1,), (1,)), ((), ())), preferred_element_type=FULL)


def dot_tn(left, right):
    return lax.dot_general(left, right, (((0,), (0,)), ((), ())), preferred_element_type=FULL)


def normalize(tensor):
    centred = tensor - jnp.mean(tensor, -1, keepdims=True)
    spread = jnp.mean(centred * centred, -1, keepdims=True)
    scale = lax.rsqrt(spread + EPSILON)
    return centred * scale, scale


def norm_backward(tensor, gains, gradient):
    unit, scale = normalize(tensor)
    weighted = gradient * gains
    first = jnp.mean(weighted, -1, keepdims=True)
    second = jnp.mean(weighted * unit, -1, keepdims=True)
    return scale * (weighted - first - unit * second)


GELU_INNER = math.sqrt(2.0 / math.pi)
GELU_CUBE = 0.044715


def gelu_and_slope(value):
    square = value * value
    bend = jnp.tanh(GELU_INNER * (value + GELU_CUBE * (square * value)))
    climb = GELU_INNER * (1.0 + 3.0 * GELU_CUBE * square)
    rise = 0.5 * (1.0 + bend)
    return value * rise, rise + 0.5 * value * (1.0 - bend * bend) * climb


def split_heads(rows):
    heads = rows.shape[1] // HEAD_SIZE
    owner = lax.broadcasted_iota(jnp.int32, rows.shape, 1) // HEAD_SIZE
    return jnp.concatenate(
        [jnp.where(owner == head, rows, jnp.zeros_like(rows)) for head in range(heads)], 0
    )


def join_heads(stacked, length):
    heads = stacked.shape[0] // HEAD_SIZE
    joined = [
        stacked[head * HEAD_SIZE : (head + 1) * HEAD_SIZE, head * length : (head + 1) * length]
        for head in range(heads)
    ]
    return jnp.concatenate(joined, 0).T


def remote(source, target, send_sem, recv_sem, device):
    return pltpu.make_async_remote_copy(
        src_ref=source,
        dst_ref=target,
        send_sem=send_sem,
        recv_sem=recv_sem,
        device_id=device,
        device_id_type=MESH,
    )


def prime(count, copies):
    for index in range(min(count, DEPTH)):
        for copy in copies(index, index):
            copy.start()


def stream(count, copies, body):
    def step(index, carry):
        slot = lax.rem(index, DEPTH)
        for copy in copies(index, slot):
            copy.wait()
        body(index, slot)

        @pl.when(index + DEPTH < count)
        def _():
            for copy in copies(index + DEPTH, slot):
                copy.start()

        return carry

    lax.fori_loop(0, count, step, 0)


def at_columns(index, size):
    return pl.ds(pl.multiple_of(index * size, size), size)


class Gather:
    def __init__(self, shard, full, stride, offset, columns, shared, place, sems):
        self.shard, self.full, self.shared = shard, full, shared
        self.stride, self.offset, self.columns = stride, offset, columns
        self.rows = shard.shape[0]
        self.unit = self.rows // 16
        chips, chip, lane = place
        self.chip, self.core, self.side = chip, lax.rem(lane, 2), lax.rem(lane // 2, 2)
        self.next_x = chip + 1 - 2 * lax.rem(chip, 2)
        self.next_y = lax.rem(chip + 2, chips)
        self.far = chips - 1 - chip
        self.to_x, self.to_y = (self.next_x, lane), (self.next_y, lane)
        self.to_z = (chip, lane + 2 - 4 * self.side)
        self.to_core = (chip, lane + 1 - 2 * self.core)
        self.send_sem, self.recv_sem = sems

    def whole(self, owner, start, count):
        first = owner * self.stride + self.offset + start
        return self.full.at[pl.ds(pl.multiple_of(first, 16), count), self.columns]

    def units(self, owner, first, count, own=False):
        start = (self.core * 8 + first) * self.unit
        size = count * self.unit
        if own:
            return self.shard.at[pl.ds(pl.multiple_of(start, 16), size), self.columns]
        return self.whole(owner, start, size)

    def hop(self, index):
        side = self.side
        rest = (4 - 3 * side, 3) if self.shared else (4 - 4 * side, 4)
        owner, first, count, device = (
            (self.chip, 4 * side, 4, self.to_x),
            (self.chip, 4 * side, 4, self.to_y),
            (self.chip, *rest, self.to_x),
            (self.chip, *rest, self.to_y),
            (self.next_x, 4 * side, 2, self.to_y),
            (self.next_y, 4 * side + 2, 2, self.to_x),
            (self.far, 4 * side, 4, self.to_z),
            (self.next_x, 0, 8, self.to_core),
            (self.next_y, 0, 8, self.to_core),
            (self.far, 0, 8, self.to_core),
            (self.next_x, 7 * side, 1, self.to_z),
            (self.next_y, 7 * side, 1, self.to_z),
        )[index]
        return remote(
            self.units(owner, first, count, own=index < 4),
            self.units(owner, first, count),
            self.send_sem.at[index],
            self.recv_sem.at[index],
            device,
        )

    def own(self):
        return remote(
            self.shard.at[:, self.columns],
            self.whole(self.chip, 0, self.rows),
            self.send_sem.at[12],
            self.recv_sem.at[12],
            self.to_core,
        )

    def begin(self):
        for index in range(4):
            self.hop(index).start()
        self.own().start()

    def pass_on(self):
        for arrived, onward in ((0, 4), (1, 5)):
            self.hop(arrived).wait_recv()
            self.hop(onward).start()

    def trade(self):
        for arrived, onward in ((2, 10), (3, 11)) if self.shared else ((2, 7), (3, 8)):
            self.hop(arrived).wait_recv()
            self.hop(onward).start()
        self.hop(4).wait_recv()
        self.hop(5).wait_recv()
        self.hop(6).start()

    def cross(self):
        pairs = ((10, 7), (11, 8)) if self.shared else ()
        for arrived, onward in pairs + ((6, 9),):
            self.hop(arrived).wait_recv()
            self.hop(onward).start()

    def arrive(self):
        for index in range(7, 10):
            self.hop(index).wait_recv()
        self.own().wait_recv()

    def drain(self):
        for index in range(12 if self.shared else 10):
            self.hop(index).wait_send()
        self.own().wait_send()


def train_kernel(
    sizes,
    tokens_in,
    cotangent_in,
    begin,
    shard_qkv,
    shard_out,
    shard_in,
    shard_back,
    qv_bias,
    out_bias,
    in_bias,
    back_bias,
    gains,
    shifts,
    down_maps,
    up_maps,
    output,
    input_grad,
    grad_down,
    grad_up,
    full_qkv,
    full_out,
    full_in,
    full_back,
    hidden,
    tokens_low,
    cotangent_low,
    normed,
    low_rank,
    heads_in,
    mixed,
    log_total,
    attended,
    slope,
    tile_in,
    tile_back,
    out_weight,
    qkv_weight,
    heads_out,
    mixture,
    scores,
    activation,
    total,
    gradient,
    grad_attended,
    mix_out,
    mix_in,
    queries,
    mix_heads,
    delta,
    query_sum,
    key_sum,
    value_sum,
    grads_in,
    grads_flat,
    qkv_bias,
    up_low,
    down_low,
    return_out,
    result_low,
    terms,
    landing,
    landing_chips,
    summed,
    tile_sem,
    load_sem,
    heads_send,
    heads_recv,
    mix_send,
    mix_recv,
    move_send,
    move_recv,
    sum_send,
    sum_recv,
    gather_send,
    gather_recv,
):
    chips, lanes = sizes
    chip, lane = lax.axis_index("dp"), lax.axis_index("sp")
    slots, length, model = tokens_in.shape
    layers, rows, hidden_units = slope.shape
    ranks = down_low.shape[0]
    group = lanes // slots
    half, seat = lane // group, lax.rem(lane, group)
    side = seat // 2
    parts = model // group // LANES
    heads = LANES // HEAD_SIZE
    per_tile = TILE // LANES
    tiles_each = model // TILE
    shares = hidden_units // TILE

    def gathers_of(layer):
        model_half, unit_half = 3 * model // 2, hidden_units // 2
        back_rows = shard_back.shape[1]
        back_half = back_rows // 2
        everything = pl.ds(0, model)
        plans = (
            (shard_qkv.at[layer], full_qkv, shard_qkv.shape[1], 0, pl.ds(0, model_half)),
            (shard_qkv.at[layer], full_qkv, shard_qkv.shape[1], 0, pl.ds(model_half, model_half)),
            (shard_out.at[layer], full_out, shard_out.shape[1], 0, everything),
            (shard_in.at[layer], full_in, shard_in.shape[1], 0, pl.ds(0, unit_half)),
            (shard_in.at[layer], full_in, shard_in.shape[1], 0, pl.ds(unit_half, unit_half)),
            (shard_back.at[layer, pl.ds(0, back_half)], full_back, back_rows, 0, everything),
            (
                shard_back.at[layer, pl.ds(back_half, back_half)],
                full_back,
                back_rows,
                back_half,
                everything,
            ),
        )
        return [
            Gather(
                shard,
                full.at[layer],
                stride,
                offset,
                columns,
                index in SHARED[layer],
                (chips, chip, lane),
                (gather_send.at[layer, index], gather_recv.at[layer, index]),
            )
            for index, (shard, full, stride, offset, columns) in enumerate(plans)
        ]

    gathers = [gathers_of(layer) for layer in range(layers)]

    def mates():
        return [lax.rem(seat + 2, group), group - 1 - seat, seat + 1 - 2 * lax.rem(seat, 2)]

    def block_at(index):
        return side * index + (1 - side) * (group - 1 - index)

    def device(mate):
        return (chip, half * group + mate)

    def lane_of(slot):
        return slot * group + lane // 2

    def move_in(kind, source, target):
        def copy(slot):
            return remote(
                source.at[slot],
                target.at[pl.ds(pl.multiple_of(lax.rem(lane, 2) * length, length), length)],
                move_send.at[kind, slot],
                move_recv.at[kind, lax.rem(lane, 2)],
                (chip, lane_of(slot)),
            )

        for slot in range(slots):

            @pl.when(lane_of(slot) != lane)
            def _():
                copy(slot).start()

            @pl.when(lane_of(slot) == lane)
            def _():
                start = pl.multiple_of(lax.rem(lane, 2) * length, length)
                target[pl.ds(start, length)] = source[slot]

    def move_in_wait(kind, source, target, sent):
        for step in range(2):
            sender = 2 * seat + step
            copy = remote(
                source.at[0],
                target.at[pl.ds(step * length, length)],
                move_send.at[kind, step],
                move_recv.at[kind, step],
                (chip, lane_of(step)),
            )
            if sent:

                @pl.when(lane_of(step) != lane)
                def _():
                    copy.wait_send()

            else:

                @pl.when(sender != lane)
                def _():
                    copy.wait_recv()

    def move_out(kind, source, target):
        for step in range(2):
            owner = 2 * seat + step
            part = pl.ds(step * length, length)

            @pl.when(owner != lane)
            def _():
                remote(
                    source.at[part],
                    target.at[half],
                    move_send.at[kind, step],
                    move_recv.at[kind, half],
                    (chip, owner),
                ).start()

            @pl.when(owner == lane)
            def _():
                target[half] = source[part]

    def move_out_wait(kind, source, target, sent):
        for step in range(2):
            owner = 2 * seat + step
            copy = remote(
                source.at[pl.ds(step * length, length)],
                target.at[step],
                move_send.at[kind, step],
                move_recv.at[kind, step],
                (chip, owner),
            )
            if sent:

                @pl.when(owner != lane)
                def _():
                    copy.wait_send()

            else:

                @pl.when(lane_of(step) != lane)
                def _():
                    copy.wait_recv()

    def heads_copy(part, mate, target, owner):
        return remote(
            heads_out.at[mate, part],
            target.at[owner, part],
            heads_send.at[part, mate],
            heads_recv.at[part, owner],
            device(mate),
        )

    def mix_copy(part, mate, source, target, owner):
        return remote(
            source.at[part, mate],
            target.at[owner, part],
            mix_send.at[part, mate],
            mix_recv.at[part, owner],
            device(mate),
        )

    def allowed_pairs(key_block, query_block, diagonal):
        place = lax.broadcasted_iota(jnp.int32, (rows, heads * rows), 0)
        begin_row = begin[pl.ds(half, 1), at_columns(query_block, rows)]
        begin_row = jnp.concatenate([begin_row] * heads, 1) - key_block * rows
        allowed = place >= begin_row
        if diagonal:
            column = lax.broadcasted_iota(jnp.int32, (1, heads * rows), 1)
            allowed = allowed & (place <= lax.rem(column, rows))
        return allowed

    def load_params(layer):
        scale = ADAPTER_ALPHA / (ranks // 2)
        down = jnp.concatenate([down_maps[layer, 0], down_maps[layer, 1]], 0)
        down_low[...] = down.astype(LOW)
        blank = jnp.zeros((ranks // 2, model), FULL)
        up_query = jnp.concatenate([scale * up_maps[layer, 0], blank], 0)
        up_value = jnp.concatenate([blank, scale * up_maps[layer, 1]], 0)
        up_low[:, :model] = up_query.astype(LOW)
        up_low[:, model : 2 * model] = jnp.zeros((ranks, model), LOW)
        up_low[:, 2 * model :] = up_value.astype(LOW)

    def forward(layer, following):
        get_qkv_a, get_qkv_b, get_out, get_in_a, get_in_b, get_back_a, get_back_b = gathers[layer]
        if layer == 0:
            get_qkv_a.begin()
            move_in(0, tokens_in, tokens_low)
            get_qkv_a.pass_on()
            get_qkv_b.begin()
        load_params(layer)
        qkv_bias[0:1, :model] = qv_bias[layer, 0:1]
        qkv_bias[0:1, model : 2 * model] = jnp.zeros((1, model), FULL)
        qkv_bias[0:1, 2 * model :] = qv_bias[layer, 1:2]
        qkv_bias[1:2, :model] = jnp.full((1, model), HEAD_SIZE ** (-0.5), FULL)
        qkv_bias[1:2, model:] = jnp.ones((1, 2 * model), FULL)
        if layer == 0:
            get_qkv_a.trade()
            move_in_wait(0, tokens_in, tokens_low, False)
            hidden[0] = tokens_low[...].astype(FULL)
        unit, _ = normalize(hidden[layer])
        normed[layer] = (unit * gains[layer, 0:1] + shifts[layer, 0:1]).astype(LOW)
        low_rank[layer] = dot_nt(normed[layer], down_low[...])
        if layer > 0:
            for part in range(parts):
                for mate in mates():
                    heads_copy(part, mate, heads_in.at[layer - 1], seat).wait_send()
        get_qkv_b.pass_on()
        get_out.begin()
        get_in_a.begin()
        get_qkv_a.cross()

        def qkv_run(first_tile, count):
            def copies(index, slot):
                columns = at_columns(first_tile + index, TILE)
                return [
                    pltpu.make_async_copy(
                        full_qkv.at[layer, :, columns], tile_in.at[slot], tile_sem.at[0, slot]
                    )
                ]

            def body(index, slot):
                tile = first_tile + index
                columns = at_columns(tile, TILE)
                value = dot_nn(normed[layer], tile_in[slot])
                value += dot_nn(low_rank[layer].astype(LOW), up_low[:, columns])
                value += qkv_bias[0:1, columns]
                value = (value * qkv_bias[1:2, columns]).astype(LOW)
                kind = tile // tiles_each
                first = lax.rem(tile, tiles_each) * (per_tile // parts)
                for step in range(per_tile):
                    heads_out[first + step // parts, step % parts, kind] = value[
                        :, step * LANES : (step + 1) * LANES
                    ]

            prime(count, copies)
            stream(count, copies, body)

        tile_count = 3 * tiles_each
        get_qkv_a.arrive()
        qkv_run(0, tile_count // 2)
        get_qkv_b.trade()
        get_qkv_b.cross()
        get_qkv_b.arrive()
        qkv_run(tile_count // 2, tile_count // 2)
        arrivals = heads_in.at[layer]
        for part in range(parts):
            for mate in mates():
                heads_copy(part, mate, arrivals, seat).start()
            heads_in[layer, seat, part] = heads_out[seat, part]
        get_out.pass_on()
        get_in_a.pass_on()
        get_in_b.begin()

        def attend(part):
            def query_step(index, carry):
                query_block = block_at(index)
                query_heads = split_heads(heads_in[layer, query_block, part, 0])

                def score_step(key_block, best, diagonal=False):
                    found = dot_nt(heads_in[layer, key_block, part, 1], query_heads)
                    allowed = allowed_pairs(key_block, query_block, diagonal)
                    found = jnp.where(allowed, found, MASKED)
                    scores[key_block] = found
                    return jnp.maximum(best, jnp.max(found, 0, keepdims=True))

                lowest = jnp.full((1, heads * rows), MASKED, FULL)
                best = lax.fori_loop(0, query_block, score_step, lowest)
                best = score_step(query_block, best, True)

                def mix_step(key_block, carried):
                    sums, mix = carried
                    raised = jnp.exp(scores[key_block] - best)
                    sums = sums + jnp.sum(raised, 0, keepdims=True)
                    return sums, mix + dot_tn(heads_in[layer, key_block, part, 2], raised.astype(LOW))

                nothing = jnp.zeros((1, heads * rows), FULL), jnp.zeros((LANES, heads * rows), FULL)
                sums, mix = lax.fori_loop(0, query_block + 1, mix_step, nothing)
                log_total[layer, part, query_block] = best + jnp.log(sums)
                mixed[layer, part, query_block] = join_heads(mix * (1.0 / sums), rows).astype(LOW)

                @pl.when(query_block != seat)
                def _():
                    mix_copy(part, query_block, mixed.at[layer], mixture, seat).start()

                return carry

            lax.fori_loop(0, group, query_step, 0)
            mixture[seat, part] = mixed[layer, part, seat]

        load = pltpu.make_async_copy(full_out.at[layer], out_weight, load_sem.at[0])
        for part in range(parts):
            for mate in mates():
                heads_copy(part, mate, arrivals, mate).wait_recv()
            attend(part)
            if part == 0:
                get_out.trade()
                get_in_b.pass_on()
                get_back_a.begin()
                get_in_a.trade()
        get_back_a.pass_on()
        get_back_b.begin()
        get_out.cross()
        get_out.arrive()
        load.start()
        get_in_b.trade()
        get_in_a.cross()

        for part in range(parts):
            for mate in mates():
                mix_copy(part, mate, mixed.at[layer], mixture, mate).wait_recv()
        load.wait()
        total[...] = hidden[layer] + out_bias[layer : layer + 1]

        def out_body(index, carry):
            joined = jnp.concatenate([mixture[index, part] for part in range(parts)], 1)
            start = pl.multiple_of(index * parts * LANES, parts * LANES)
            total[...] += dot_nn(joined, out_weight[pl.ds(start, parts * LANES)])
            return carry

        lax.fori_loop(0, group, out_body, 0)
        attended[layer] = total[...]
        unit, _ = normalize(total[...])
        second = (unit * gains[layer, 1:2] + shifts[layer, 1:2]).astype(LOW)

        def in_run(first_tile, count):
            def copies(index, slot):
                columns = at_columns(first_tile + index, TILE)
                return [
                    pltpu.make_async_copy(
                        full_in.at[layer, :, columns], tile_in.at[slot], tile_sem.at[0, slot]
                    )
                ]

            def body(index, slot):
                tile = first_tile + index
                columns = at_columns(tile, TILE)
                value = dot_nn(second, tile_in[slot]) + in_bias[layer : layer + 1, columns]
                lifted, steepness = gelu_and_slope(value)
                slope[layer, :, columns] = steepness.astype(LOW)
                activation[tile] = lifted.astype(LOW)

            prime(count, copies)
            stream(count, copies, body)

        get_back_a.trade()
        get_in_a.arrive()
        in_run(0, shares // 2)
        get_back_b.pass_on()
        if following is not None:
            following[0].begin()
        get_in_b.cross()
        get_in_b.arrive()
        in_run(shares // 2, shares // 2)
        if following is not None:
            move_in(1, cotangent_in, cotangent_low)
        get_back_a.cross()
        for part in range(parts):
            for mate in mates():
                mix_copy(part, mate, mixed.at[layer], mixture, seat).wait_send()

    def back_copies(layer, first):
        def copies(index, slot):
            return [
                pltpu.make_async_copy(
                    full_back.at[layer, at_columns(grad_tile(first + index), TILE)],
                    tile_back.at[slot],
                    tile_sem.at[1, slot],
                )
            ]

        return copies

    def back_run(layer, first, count):
        def body(index, slot):
            total[...] += dot_nn(activation[grad_tile(first + index)], tile_back[slot])

        stream(count, back_copies(layer, first), body)

    def grad_tile(index):
        pairs = shares // 2
        return 2 * lax.rem(index, pairs) + index // pairs

    def grad_copies(layer, first):
        def copies(index, slot):
            columns = at_columns(grad_tile(first + index), TILE)
            return [
                pltpu.make_async_copy(
                    full_in.at[layer, :, columns], tile_in.at[slot], tile_sem.at[0, slot]
                ),
                pltpu.make_async_copy(
                    full_back.at[layer, columns], tile_back.at[slot], tile_sem.at[1, slot]
                ),
            ]

        return copies

    def grad_run(layer, low_gradient, first, count):
        def body(index, slot):
            columns = at_columns(grad_tile(first + index), TILE)
            grad_act = dot_nt(low_gradient, tile_back[slot])
            grad_pre = (slope[layer, :, columns].astype(FULL) * grad_act).astype(LOW)
            total[...] += dot_nt(grad_pre, tile_in[slot])

        stream(count, grad_copies(layer, first), body)

    def backward(layer, last):
        load_out = pltpu.make_async_copy(full_out.at[layer], out_weight, load_sem.at[0])
        load_qkv = pltpu.make_async_copy(full_qkv.at[layer], qkv_weight, load_sem.at[1])
        if last:
            load_out.start()
        load_qkv.start()
        load_params(layer)
        low_gradient = gradient[...].astype(LOW)
        total[...] = jnp.zeros_like(total)
        if last:
            get_back_a, get_back_b = gathers[layer][5:7]
            get_back_b.trade()
            get_back_a.arrive()
            prime(shares // 2, grad_copies(layer, 0))
            grad_run(layer, low_gradient, 0, shares // 2)
            get_back_b.cross()
            get_back_b.arrive()
            prime(shares // 2, grad_copies(layer, shares // 2))
            grad_run(layer, low_gradient, shares // 2, shares // 2)
        else:
            grad_run(layer, low_gradient, 0, shares)
        grad_attended[...] = gradient[...] + norm_backward(
            attended[layer], gains[layer, 1:2], total[...]
        )
        low_attended = grad_attended[...].astype(LOW)
        load_out.wait()
        if last:
            prime(shares, back_copies(layer, 0))
        else:
            for part in range(parts):
                for mate in mates():
                    mix_copy(part, mate, mix_out, mix_in, seat).wait_send()

        for mate in mates() + [seat]:
            start = pl.multiple_of(mate * parts * LANES, parts * LANES)
            value = dot_nt(low_attended, out_weight[pl.ds(start, parts * LANES)]).astype(LOW)
            for part in range(parts):
                mix_out[part, mate] = value[:, part * LANES : (part + 1) * LANES]
        for part in range(parts):
            for mate in mates():
                mix_copy(part, mate, mix_out, mix_in, seat).start()
            mix_in[seat, part] = mix_out[part, seat]
            for mate in mates():
                heads_copy(part, mate, grads_in, seat).wait_send()
        if last:
            total[...] = attended[layer] + back_bias[layer : layer + 1]
            back_run(layer, 0, shares)
            result_low[...] = total[...].astype(LOW)
        if layer > 0:
            pltpu.make_async_copy(full_out.at[layer - 1], out_weight, load_sem.at[0]).start()
            prime(shares, grad_copies(layer - 1, 0))

        def attend(part):
            def prepare(block, carry):
                queries[block] = split_heads(heads_in[layer, block, part, 0])
                grads = split_heads(mix_in[block, part])
                mix_heads[block] = grads
                mix = jnp.concatenate([mixed[layer, part, block]] * heads, 0)
                product = grads.astype(FULL) * mix.astype(FULL)
                delta[block] = jnp.sum(product.T, 0, keepdims=True)
                query_sum[block] = jnp.zeros_like(query_sum[block])
                key_sum[block] = jnp.zeros_like(key_sum[block])
                value_sum[block] = jnp.zeros_like(value_sum[block])
                return carry

            lax.fori_loop(0, group, prepare, 0)

            def pair_step(key_block, query_block, diagonal):
                keys = heads_in[layer, key_block, part, 1]
                values = heads_in[layer, key_block, part, 2]
                query_heads = queries[query_block]
                grad_heads = mix_heads[query_block]
                found = dot_nt(keys, query_heads)
                raised = jnp.exp(found - log_total[layer, part, query_block])
                allowed = allowed_pairs(key_block, query_block, diagonal)
                weights = jnp.where(allowed, raised, 0.0)
                value_sum[key_block] += dot_nn(weights.astype(LOW), grad_heads)
                grad_weights = dot_nt(values, grad_heads)
                grad_scores = weights * (grad_weights - delta[query_block])
                grad_scores = grad_scores.astype(LOW)
                key_sum[key_block] += dot_nn(grad_scores, query_heads)
                query_sum[query_block] += dot_tn(keys, grad_scores)

            def block_step(index, carry):
                block = block_at(index)
                pair_step(block, block, True)

                def inner_step(step, inner):
                    key_block = block - (1 - side) * step
                    pair_step(key_block, block + side * step, False)
                    return inner

                lax.fori_loop(1, group - index, inner_step, 0)
                out = join_heads(query_sum[block], rows).astype(LOW)
                heads_out[block, part, 0] = out * jnp.asarray(HEAD_SIZE ** (-0.5), LOW)
                heads_out[block, part, 1] = key_sum[block].astype(LOW)
                heads_out[block, part, 2] = value_sum[block].astype(LOW)

                @pl.when(block != seat)
                def _():
                    heads_copy(part, block, grads_in, seat).start()

                return carry

            lax.fori_loop(0, group, block_step, 0)
            grads_in[seat, part] = heads_out[seat, part]

        for part in range(parts):
            for mate in mates():
                mix_copy(part, mate, mix_out, mix_in, mate).wait_recv()
            attend(part)
        def part_columns(source, part, kind):
            starts = [kind * model + (owner * parts + part) * LANES for owner in range(group)]
            return jnp.concatenate([source[:, start : start + LANES] for start in starts], 1)

        load_qkv.wait()
        rank = ranks // 2
        low_values = (low_rank[layer] * (ADAPTER_ALPHA / rank)).astype(LOW)
        grad_low = jnp.zeros((rows, ranks), FULL)
        total[...] = jnp.zeros_like(total)
        for part in range(parts):
            for mate in mates():
                heads_copy(part, mate, grads_in, mate).wait_recv()
            for kind in range(3):
                joined = [grads_in[owner, part, kind] for owner in range(group)]
                grads_flat[kind] = jnp.concatenate(joined, 1)
            for entry, kind in ((2, 0), (3, 2)):
                grad_low += dot_nt(grads_flat[kind], part_columns(up_low, part, kind))
                found = dot_tn(low_values, grads_flat[kind])
                found = found[:rank] if kind == 0 else found[rank:]
                for owner in range(group):
                    start = (owner * parts + part) * LANES
                    terms[4 * layer + entry, :, start : start + LANES] = found[
                        :, owner * LANES : (owner + 1) * LANES
                    ]
            if part == parts - 1:
                grad_low = grad_low.astype(LOW)
                down_terms = dot_tn(grad_low, normed[layer])
                terms[4 * layer] = down_terms[:rank]
                terms[4 * layer + 1] = down_terms[rank:]
                if not last:
                    sum_begin()
                total[...] += dot_nn(grad_low, down_low[...])
            for kind in range(3):
                total[...] += dot_nt(grads_flat[kind], part_columns(qkv_weight, part, kind))
        if last:
            move_out(2, result_low, output)
        gradient[...] = grad_attended[...] + norm_backward(
            hidden[layer], gains[layer, 0:1], total[...]
        )

    def sum_lanes():
        return [
            remote(
                terms.at[lax.rem(lane + step, lanes)],
                landing.at[lane],
                sum_send.at[0, step],
                sum_recv.at[0, step],
                (chip, lax.rem(lane + step, lanes)),
            )
            for step in range(1, lanes)
        ]

    def sum_spread():
        return [
            remote(
                summed.at[lane],
                summed.at[lane],
                sum_send.at[1, step],
                sum_recv.at[1, step],
                (chip, lax.rem(lane + step, lanes)),
            )
            for step in range(1, lanes)
        ]

    def sum_chips():
        return [
            remote(
                summed,
                landing_chips.at[chip],
                sum_send.at[2, step],
                sum_recv.at[2, step],
                (lax.rem(chip + step, chips), lane),
            )
            for step in range(1, chips)
        ]

    def sum_begin():
        for copy in sum_lanes():
            copy.start()
        landing[lane] = terms[lane]

    def sum_lanes_finish():
        for copy in sum_lanes():
            copy.wait()
        summed[lane] = jnp.sum(landing[...], axis=0)
        for copy in sum_spread():
            copy.start()

    def sum_finish():
        for copy in sum_spread():
            copy.wait()
        for copy in sum_chips():
            copy.start()
        landing_chips[chip] = summed[...]
        for copy in sum_chips():
            copy.wait()
        scale = 1.0 / math.sqrt(slots * chips * length * lanes)
        for layer in range(layers):
            for kind in range(2):
                for grads, entry in ((grad_down, kind), (grad_up, 2 + kind)):
                    terms_of = landing_chips[:, 4 * layer + entry]
                    grads[layer, kind] = jnp.sum(terms_of, axis=0) * scale

    barrier = pltpu.get_barrier_semaphore()
    friends = [(chip, lax.rem(lane + step, lanes)) for step in range(1, lanes)]
    friends += [(lax.rem(chip + step, chips), lane) for step in range(1, chips)]
    for friend in friends:
        pl.semaphore_signal(barrier, inc=1, device_id=friend, device_id_type=MESH)
    pl.semaphore_wait(barrier, len(friends))

    for layer in range(layers):
        last = layer + 1 == layers
        forward(layer, None if last else gathers[layer + 1])
        if not last:
            total[...] = attended[layer] + back_bias[layer : layer + 1]
            get_back_a, get_back_b = gathers[layer][5:7]
            get_back_a.arrive()
            prime(shares // 2, back_copies(layer, 0))
            back_run(layer, 0, shares // 2)
            gathers[layer + 1][0].pass_on()
            gathers[layer + 1][1].begin()
            get_back_b.trade()
            get_back_b.cross()
            get_back_b.arrive()
            prime(shares // 2, back_copies(layer, shares // 2))
            back_run(layer, shares // 2, shares // 2)
            hidden[layer + 1] = total[...]
            gathers[layer + 1][0].trade()
    move_in_wait(1, cotangent_in, cotangent_low, False)
    gradient[...] = cotangent_low[...].astype(FULL)
    for layer in reversed(range(layers)):
        last = layer + 1 == layers
        backward(layer, last)
    return_out[...] = gradient[...].astype(LOW)
    sum_lanes_finish()
    move_out(3, return_out, input_grad)
    sum_finish()
    move_out_wait(2, result_low, output, False)
    move_out_wait(3, return_out, input_grad, False)

    move_in_wait(0, tokens_in, tokens_low, True)
    move_in_wait(1, cotangent_in, cotangent_low, True)
    move_out_wait(2, result_low, output, True)
    move_out_wait(3, return_out, input_grad, True)
    for layer_gathers in gathers:
        for gather in layer_gathers:
            gather.drain()
    for part in range(parts):
        for mate in mates():
            mix_copy(part, mate, mix_out, mix_in, seat).wait_send()
            heads_copy(part, mate, grads_in, seat).wait_send()


def widen_kernel(*refs):
    for source, target in zip(refs[:4], refs[4:]):
        target[...] = source[...].astype(FULL)


def fast_body(sizes, *arrays):
    chips, lanes = sizes
    tokens, _, _, *shards = arrays[:7]
    slots, length, model = tokens.shape
    layers, kinds, rank, _ = arrays[-1].shape
    hidden_units = shards[2].shape[2]
    group = lanes // slots
    rows, ranks = slots * length, kinds * rank
    parts, heads = model // group // LANES, LANES // HEAD_SIZE
    vmem = pl.BlockSpec(memory_space=pltpu.VMEM)
    anywhere = pl.BlockSpec(memory_space=pl.ANY)
    shape, dma = jax.ShapeDtypeStruct, pltpu.SemaphoreType.DMA
    scratch = [
        ((layers, rows, model), FULL),
        ((rows, model), LOW),
        ((rows, model), LOW),
        ((layers, rows, model), LOW),
        ((layers, rows, ranks), FULL),
        ((layers, group, parts, 3, rows, LANES), LOW),
        ((layers, parts, group, rows, LANES), LOW),
        ((layers, parts, group, 1, heads * rows), FULL),
        ((layers, rows, model), FULL),
        ((layers, rows, hidden_units), LOW),
        ((DEPTH, model, TILE), LOW),
        ((DEPTH, TILE, model), LOW),
        ((model, model), LOW),
        ((model, 3 * model), LOW),
        ((group, parts, 3, rows, LANES), LOW),
        ((group, parts, rows, LANES), LOW),
        ((group, rows, heads * rows), FULL),
        ((hidden_units // TILE, rows, TILE), LOW),
        ((rows, model), FULL),
        ((rows, model), FULL),
        ((rows, model), FULL),
        ((parts, group, rows, LANES), LOW),
        ((group, parts, rows, LANES), LOW),
        ((group, heads * rows, LANES), LOW),
        ((group, heads * rows, LANES), LOW),
        ((group, 1, heads * rows), FULL),
        ((group, LANES, heads * rows), FULL),
        ((group, rows, LANES), FULL),
        ((group, rows, LANES), FULL),
        ((group, parts, 3, rows, LANES), LOW),
        ((3, rows, group * LANES), LOW),
        ((2, 3 * model), FULL),
        ((ranks, 3 * model), LOW),
        ((ranks, model), LOW),
        ((rows, model), LOW),
        ((rows, model), LOW),
        ((lanes, rank, model), FULL),
        ((lanes, rank, model), FULL),
        ((chips, lanes, rank, model), FULL),
        ((lanes, rank, model), FULL),
    ]
    semaphores = [
        (2, DEPTH),
        (2,),
        (parts, group),
        (parts, group),
        (parts, group),
        (parts, group),
        (4, 2),
        (4, 2),
        (3, lanes),
        (3, lanes),
        (layers, 7, 13),
        (layers, 7, 13),
    ]
    results = pl.pallas_call(
        partial(train_kernel, sizes),
        out_shape=(
            shape((slots, length, model), LOW),
            shape((slots, length, model), LOW),
            shape((layers, kinds, rank, model), FULL),
            shape((layers, kinds, rank, model), FULL),
        )
        + tuple(shape((layers, chips * part.shape[1], part.shape[2]), LOW) for part in shards),
        in_specs=[vmem] * 3 + [anywhere] * 4 + [vmem] * 8,
        out_specs=(vmem,) * 4 + (anywhere,) * 4,
        scratch_shapes=[pltpu.VMEM(*entry) for entry in scratch]
        + [dma(entry) for entry in semaphores],
        name="train",
        compiler_params=pltpu.CompilerParams(
            collective_id=0, has_side_effects=True, vmem_limit_bytes=VMEM_LIMIT
        ),
    )(*arrays)
    return pl.pallas_call(
        widen_kernel,
        out_shape=(
            shape((slots, length, model), FULL),
            shape((slots, length, model), FULL),
            shape((layers, kinds, rank, model), FULL),
            shape((layers, kinds, rank, model), FULL),
        ),
        in_specs=[vmem] * 4,
        out_specs=(vmem,) * 4,
        name="widen",
    )(*results[:4])


def solution(mesh):
    chips, lanes = sizes = tuple(mesh.devices.shape)
    fast = sizes == (4, 8)
    token_axes = "sp" if fast else SP
    if not fast:
        mesh = Mesh(mesh.devices.reshape(chips, lanes // 2, 2), ("dp",) + SP)
    tokens = P("dp", token_axes, None)
    weights = P(None, "dp", None)
    return jax.shard_map(
        partial(fast_body, sizes) if fast else body,
        mesh=mesh,
        in_specs=(tokens, tokens, P("dp", None)) + (weights,) * 4 + (P(),) * 8,
        out_specs=(tokens, tokens, P(), P()),
        check_vma=False,
    )
```

```python
from functools import partial
import math

import jax
import jax.numpy as jnp
from jax import lax
from jax.experimental import pallas as pl
from jax.experimental.pallas import tpu as pltpu
from jax.sharding import Mesh, PartitionSpec as P

HEAD_SIZE = 64


EPSILON = 1e-05
ADAPTER_ALPHA = 32.0
EXACT_PRECISION = lax.Precision.HIGHEST
MASKED = -1e30
SP = ("z", "core")


def layer_norm(tensor, gains, shifts):
    row_mean = jnp.mean(tensor, -1, keepdims=True)
    centred = tensor - row_mean
    spread = jnp.mean(centred * centred, -1, keepdims=True)
    return centred * lax.rsqrt(spread + EPSILON) * gains + shifts


def fetch_weights(
    query_key_value_weight,
    attention_out_weight,
    feedforward_in_weight,
    feedforward_out_weight,
    layer_number,
):
    core = lax.axis_index("core")

    def fetch(shards):
        half = shards.shape[1] // 2
        part = lax.dynamic_slice_in_dim(shards[layer_number], core * half, half, 0)
        return lax.all_gather(part, ("dp", "core"), axis=0, tiled=True)

    return (
        fetch(query_key_value_weight),
        fetch(attention_out_weight),
        fetch(feedforward_in_weight),
        fetch(feedforward_out_weight),
    )


def sum_kernel(sizes, terms_ref, out_ref, landing, send_sem, recv_sem, send_sem2, recv_sem2):
    count = math.prod(sizes)
    me = [lax.axis_index(name) for name in ("dp", "z", "core")]
    mine = (me[0] * sizes[1] + me[1]) * sizes[2] + me[2]

    def place(step):
        other = lax.rem(mine + step, count)
        return other, (
            other // (sizes[1] * sizes[2]),
            lax.rem(other // sizes[2], sizes[1]),
            lax.rem(other, sizes[2]),
        )

    barrier = pltpu.get_barrier_semaphore()
    for step in range(1, count):
        pl.semaphore_signal(
            barrier, inc=1, device_id=place(step)[1], device_id_type=pl.DeviceIdType.MESH
        )
    pl.semaphore_wait(barrier, count - 1)

    def scatter(step):
        other, device = place(step)
        return pltpu.make_async_remote_copy(
            src_ref=terms_ref.at[other],
            dst_ref=landing.at[step],
            send_sem=send_sem.at[step],
            recv_sem=recv_sem.at[step],
            device_id=device,
            device_id_type=pl.DeviceIdType.MESH,
        )

    def spread(step):
        other, device = place(step)
        return pltpu.make_async_remote_copy(
            src_ref=out_ref.at[mine],
            dst_ref=out_ref.at[mine],
            send_sem=send_sem2.at[step],
            recv_sem=recv_sem2.at[step],
            device_id=device,
            device_id_type=pl.DeviceIdType.MESH,
        )

    for step in range(1, count):
        scatter(step).start()
    landing[0] = terms_ref[mine]
    for step in range(1, count):
        scatter(step).wait()
    out_ref[mine] = jnp.sum(landing[...], axis=0)
    for step in range(1, count):
        spread(step).start()
    for step in range(1, count):
        spread(step).wait()


def sum_adapters(down_terms, up_terms):
    sizes = [lax.axis_size(name) for name in ("dp", "z", "core")]
    count = math.prod(sizes)
    packed = jnp.stack([down_terms, up_terms])
    if count > 64 or packed.size % (count * 1024) != 0:
        return lax.psum((down_terms, up_terms), ("dp", "z", "core"))
    pieces = packed.reshape(count, -1, 128)
    vmem = pl.BlockSpec(memory_space=pltpu.VMEM)
    summed = pl.pallas_call(
        partial(sum_kernel, sizes),
        out_shape=jax.ShapeDtypeStruct(pieces.shape, jnp.float32),
        in_specs=[vmem],
        out_specs=vmem,
        scratch_shapes=[pltpu.VMEM(pieces.shape, jnp.float32)]
        + [pltpu.SemaphoreType.DMA((count,))] * 4,
        name="adapter_sum",
        compiler_params=pltpu.CompilerParams(collective_id=0, has_side_effects=True),
    )(pieces)
    summed = summed.reshape(packed.shape)
    return summed[0], summed[1]


def slot_scores(query_rows, key_rows, document_starts):
    length = query_rows.shape[0]
    heads_q = query_rows.reshape(length, -1, HEAD_SIZE)
    heads_k = key_rows.reshape(length, -1, HEAD_SIZE)
    scores = jnp.einsum("qhd,khd->hqk", heads_q, heads_k, preferred_element_type=jnp.float32)
    places = jnp.arange(length)
    allowed = (document_starts[:, None] == document_starts[None, :]) & (
        places[None, :] <= places[:, None]
    )
    return jnp.where(allowed[None], scores, MASKED)


def slot_forward(slot_items):
    query_rows, key_rows, value_rows, document_starts = slot_items
    length = query_rows.shape[0]
    scores = slot_scores(query_rows, key_rows, document_starts)
    row_max = jnp.max(scores, -1, keepdims=True)
    row_total = jnp.sum(jnp.exp(scores - row_max), -1, keepdims=True)
    log_total = row_max + jnp.log(row_total)
    probability = jnp.exp(scores - log_total).astype(jnp.bfloat16)
    mixture = jnp.einsum(
        "hqk,khd->qhd",
        probability,
        value_rows.reshape(length, -1, HEAD_SIZE),
        preferred_element_type=jnp.float32,
    )
    return (mixture.reshape(length, -1).astype(jnp.bfloat16), log_total[..., 0])


def slot_backward(slot_items):
    query_rows, key_rows, value_rows, document_starts, log_total, grad_mixture = slot_items
    length = query_rows.shape[0]
    scores = slot_scores(query_rows, key_rows, document_starts)
    probability = jnp.exp(scores - log_total[..., None])
    low_probability = probability.astype(jnp.bfloat16)
    grad_heads = grad_mixture.reshape(length, -1, HEAD_SIZE)
    value_heads = value_rows.reshape(length, -1, HEAD_SIZE)
    grad_values = jnp.einsum(
        "hqk,qhd->khd", low_probability, grad_heads, preferred_element_type=jnp.float32
    )
    grad_prob = jnp.einsum(
        "qhd,khd->hqk", grad_heads, value_heads, preferred_element_type=jnp.float32
    )
    grad_scores = probability * (grad_prob - jnp.sum(probability * grad_prob, -1, keepdims=True))
    low_scores = grad_scores.astype(jnp.bfloat16)
    grad_queries = jnp.einsum(
        "hqk,khd->qhd",
        low_scores,
        key_rows.reshape(length, -1, HEAD_SIZE),
        preferred_element_type=jnp.float32,
    )
    grad_keys = jnp.einsum(
        "hqk,qhd->khd",
        low_scores,
        query_rows.reshape(length, -1, HEAD_SIZE),
        preferred_element_type=jnp.float32,
    )
    return (
        grad_queries.reshape(length, -1).astype(jnp.bfloat16),
        grad_keys.reshape(length, -1).astype(jnp.bfloat16),
        grad_values.reshape(length, -1).astype(jnp.bfloat16),
    )


def layer_forward(hidden_state, weight_set, params, document_begin):
    query_key_value_weight, attention_out_weight, feedforward_in_weight, feedforward_out_weight = (
        weight_set
    )
    (
        query_value_bias,
        attention_out_bias,
        feedforward_in_bias,
        feedforward_out_bias,
        gains,
        shifts,
        down_projection,
        up_projection,
    ) = params
    model_dimension = hidden_state.shape[-1]
    normed = layer_norm(hidden_state, gains[0], shifts[0]).astype(jnp.bfloat16)
    projected_rows = jnp.einsum(
        "std,de->ste", normed, query_key_value_weight, preferred_element_type=jnp.float32
    )
    widened = normed.astype(jnp.float32)
    adapter_scale = ADAPTER_ALPHA / down_projection.shape[1]
    query_row_block = jnp.einsum(
        "nyh,lh->nyl", widened, down_projection[0], precision=EXACT_PRECISION
    )
    value_row_block = jnp.einsum(
        "nyh,lh->nyl", widened, down_projection[1], precision=EXACT_PRECISION
    )
    query_rows = (
        (
            projected_rows[..., :model_dimension]
            + query_value_bias[0]
            + adapter_scale
            * jnp.einsum(
                "wah,hp->wap", query_row_block, up_projection[0], precision=EXACT_PRECISION
            )
        )
        * HEAD_SIZE ** (-0.5)
    ).astype(jnp.bfloat16)
    key_rows = projected_rows[..., model_dimension : 2 * model_dimension].astype(jnp.bfloat16)
    value_rows = (
        projected_rows[..., 2 * model_dimension :]
        + query_value_bias[1]
        + adapter_scale
        * jnp.einsum("wah,hp->wap", value_row_block, up_projection[1], precision=EXACT_PRECISION)
    ).astype(jnp.bfloat16)
    queries_h, keys_h, values_h = lax.all_to_all(
        jnp.stack([query_rows, key_rows, value_rows]), SP, split_axis=3, concat_axis=2, tiled=True
    )
    mixture_h, log_total = lax.map(slot_forward, (queries_h, keys_h, values_h, document_begin))
    mixture = lax.all_to_all(mixture_h, SP, split_axis=1, concat_axis=2, tiled=True)
    attended = hidden_state + (
        jnp.einsum("std,de->ste", mixture, attention_out_weight, preferred_element_type=jnp.float32)
        + attention_out_bias
    )
    normed_mlp = layer_norm(attended, gains[1], shifts[1]).astype(jnp.bfloat16)
    pre_act = (
        jnp.einsum(
            "std,df->stf", normed_mlp, feedforward_in_weight, preferred_element_type=jnp.float32
        )
        + feedforward_in_bias
    )
    activation = jax.nn.gelu(pre_act, approximate=True).astype(jnp.bfloat16)
    final_result = attended + (
        jnp.einsum(
            "stf,fd->std", activation, feedforward_out_weight, preferred_element_type=jnp.float32
        )
        + feedforward_out_bias
    )
    saved_state = (
        normed,
        query_row_block,
        value_row_block,
        queries_h,
        keys_h,
        values_h,
        log_total,
        attended,
        pre_act,
    )
    return (final_result, saved_state)


def layer_backward(hidden_state, gradient, weight_set, params, document_begin, saved_state):
    query_key_value_weight, attention_out_weight, feedforward_in_weight, feedforward_out_weight = (
        weight_set
    )
    (
        query_value_bias,
        attention_out_bias,
        feedforward_in_bias,
        feedforward_out_bias,
        gains,
        shifts,
        down_projection,
        up_projection,
    ) = params
    (
        normed,
        query_row_block,
        value_row_block,
        queries_h,
        keys_h,
        values_h,
        log_total,
        attended,
        pre_act,
    ) = saved_state
    grad_act = jnp.einsum(
        "std,fd->stf",
        gradient.astype(jnp.bfloat16),
        feedforward_out_weight,
        preferred_element_type=jnp.float32,
    )
    unused_act, gelu_back = jax.vjp(partial(jax.nn.gelu, approximate=True), pre_act)
    grad_pre = gelu_back(grad_act)[0].astype(jnp.bfloat16)
    grad_normed_mlp = jnp.einsum(
        "stf,df->std", grad_pre, feedforward_in_weight, preferred_element_type=jnp.float32
    )
    unused_norm, second_back = jax.vjp(
        lambda tensor: layer_norm(tensor, gains[1], shifts[1]), attended
    )
    grad_attended = gradient + second_back(grad_normed_mlp)[0]
    grad_mixture = jnp.einsum(
        "ste,de->std",
        grad_attended.astype(jnp.bfloat16),
        attention_out_weight,
        preferred_element_type=jnp.float32,
    ).astype(jnp.bfloat16)
    grad_mixture_h = lax.all_to_all(grad_mixture, SP, split_axis=2, concat_axis=1, tiled=True)
    grad_q_h, grad_k_h, grad_v_h = lax.map(
        slot_backward, (queries_h, keys_h, values_h, document_begin, log_total, grad_mixture_h)
    )
    grad_queries, grad_keys, grad_values = lax.all_to_all(
        jnp.stack([grad_q_h, grad_k_h, grad_v_h]), SP, split_axis=2, concat_axis=3, tiled=True
    )
    grad_queries = grad_queries * jnp.asarray(HEAD_SIZE ** (-0.5), jnp.bfloat16)
    stacked = jnp.concatenate([grad_queries, grad_keys, grad_values], -1)
    grad_normed = jnp.einsum(
        "ste,de->std", stacked, query_key_value_weight, preferred_element_type=jnp.float32
    )
    adapter_scale = ADAPTER_ALPHA / down_projection.shape[1]
    widened = normed.astype(jnp.float32)
    query_widened = grad_queries.astype(jnp.float32)
    value_widened = grad_values.astype(jnp.float32)
    query_row_gradient = adapter_scale * jnp.einsum(
        "nyh,lh->nyl", query_widened, up_projection[0], precision=EXACT_PRECISION
    )
    value_row_gradient = adapter_scale * jnp.einsum(
        "nyh,lh->nyl", value_widened, up_projection[1], precision=EXACT_PRECISION
    )
    query_up_weight = adapter_scale * jnp.einsum(
        "fkp,fkz->pz", query_row_block, query_widened, precision=EXACT_PRECISION
    )
    value_up_weight = adapter_scale * jnp.einsum(
        "fkp,fkz->pz", value_row_block, value_widened, precision=EXACT_PRECISION
    )
    down_q = jnp.einsum("fkp,fkz->pz", query_row_gradient, widened, precision=EXACT_PRECISION)
    down_v = jnp.einsum("fkp,fkz->pz", value_row_gradient, widened, precision=EXACT_PRECISION)
    grad_normed = (
        grad_normed
        + jnp.einsum(
            "wah,hp->wap", query_row_gradient, down_projection[0], precision=EXACT_PRECISION
        )
        + jnp.einsum(
            "wah,hp->wap", value_row_gradient, down_projection[1], precision=EXACT_PRECISION
        )
    )
    unused_first, first_back = jax.vjp(
        lambda tensor: layer_norm(tensor, gains[0], shifts[0]), hidden_state
    )
    grad_hidden = grad_attended + first_back(grad_normed)[0]
    return (grad_hidden, jnp.stack([down_q, down_v]), jnp.stack([query_up_weight, value_up_weight]))


def body(
    first_layer_input,
    cotangent,
    document_begin,
    query_key_value_weight,
    attention_out_weight,
    feedforward_in_weight,
    feedforward_out_weight,
    query_value_bias,
    attention_out_bias,
    feedforward_in_bias,
    feedforward_out_bias,
    layernorm_gain,
    layernorm_bias,
    adapter_down_maps,
    adapter_up_maps,
):
    layers = query_key_value_weight.shape[0]

    def params_of(layer_number):
        return (
            query_value_bias[layer_number],
            attention_out_bias[layer_number],
            feedforward_in_bias[layer_number],
            feedforward_out_bias[layer_number],
            layernorm_gain[layer_number],
            layernorm_bias[layer_number],
            adapter_down_maps[layer_number],
            adapter_up_maps[layer_number],
        )

    hidden_state = first_layer_input.astype(jnp.float32)
    inputs = []
    gathered = []
    kept = []
    for layer_number in range(layers):
        weight_set = fetch_weights(
            query_key_value_weight,
            attention_out_weight,
            feedforward_in_weight,
            feedforward_out_weight,
            layer_number,
        )
        inputs.append(hidden_state)
        gathered.append(weight_set)
        hidden_state, saved_state = layer_forward(
            hidden_state, weight_set, params_of(layer_number), document_begin
        )
        kept.append(saved_state)
    gradient = cotangent.astype(jnp.float32)
    down_parts = [None] * layers
    up_parts = [None] * layers
    for layer_number in reversed(range(layers)):
        gradient, down_terms, up_terms = layer_backward(
            inputs[layer_number],
            gradient,
            gathered[layer_number],
            params_of(layer_number),
            document_begin,
            kept[layer_number],
        )
        down_parts[layer_number] = down_terms
        up_parts[layer_number] = up_terms
    grad_down = jnp.stack(down_parts)
    grad_up = jnp.stack(up_parts)
    grad_down, grad_up = sum_adapters(grad_down, grad_up)
    tokens = (
        first_layer_input.shape[0]
        * first_layer_input.shape[1]
        * lax.axis_size("dp")
        * lax.axis_size("z")
        * lax.axis_size("core")
    )
    token_scale = 1.0 / math.sqrt(tokens)
    return (hidden_state, gradient, grad_down * token_scale, grad_up * token_scale)


MESH = pl.DeviceIdType.MESH
TILE = 512
LANES = 128
DEPTH = 4
SHARED = ((), ())
VMEM_LIMIT = 60 * 1024 * 1024
LOW, FULL = jnp.bfloat16, jnp.float32


def dot_nn(left, right):
    return jnp.dot(left, right, preferred_element_type=FULL)


def dot_nt(left, right):
    return lax.dot_general(left, right, (((1,), (1,)), ((), ())), preferred_element_type=FULL)


def dot_tn(left, right):
    return lax.dot_general(left, right, (((0,), (0,)), ((), ())), preferred_element_type=FULL)


def normalize(tensor):
    centred = tensor - jnp.mean(tensor, -1, keepdims=True)
    spread = jnp.mean(centred * centred, -1, keepdims=True)
    scale = lax.rsqrt(spread + EPSILON)
    return centred * scale, scale


def norm_backward(tensor, gains, gradient):
    unit, scale = normalize(tensor)
    weighted = gradient * gains
    first = jnp.mean(weighted, -1, keepdims=True)
    second = jnp.mean(weighted * unit, -1, keepdims=True)
    return scale * (weighted - first - unit * second)


GELU_INNER = math.sqrt(2.0 / math.pi)
GELU_CUBE = 0.044715


def gelu_and_slope(value):
    square = value * value
    bend = jnp.tanh(GELU_INNER * (value + GELU_CUBE * (square * value)))
    climb = GELU_INNER * (1.0 + 3.0 * GELU_CUBE * square)
    rise = 0.5 * (1.0 + bend)
    return value * rise, rise + 0.5 * value * (1.0 - bend * bend) * climb


def split_heads(rows):
    heads = rows.shape[1] // HEAD_SIZE
    owner = lax.broadcasted_iota(jnp.int32, rows.shape, 1) // HEAD_SIZE
    return jnp.concatenate(
        [jnp.where(owner == head, rows, jnp.zeros_like(rows)) for head in range(heads)], 0
    )


def join_heads(stacked, length):
    heads = stacked.shape[0] // HEAD_SIZE
    joined = [
        stacked[head * HEAD_SIZE : (head + 1) * HEAD_SIZE, head * length : (head + 1) * length]
        for head in range(heads)
    ]
    return jnp.concatenate(joined, 0).T


def remote(source, target, send_sem, recv_sem, device):
    return pltpu.make_async_remote_copy(
        src_ref=source,
        dst_ref=target,
        send_sem=send_sem,
        recv_sem=recv_sem,
        device_id=device,
        device_id_type=MESH,
    )


def prime(count, copies):
    for index in range(min(count, DEPTH)):
        for copy in copies(index, index):
            copy.start()


def stream(count, copies, body):
    def step(index, carry):
        slot = lax.rem(index, DEPTH)
        for copy in copies(index, slot):
            copy.wait()
        body(index, slot)

        @pl.when(index + DEPTH < count)
        def _():
            for copy in copies(index + DEPTH, slot):
                copy.start()

        return carry

    lax.fori_loop(0, count, step, 0)


def at_columns(index, size):
    return pl.ds(pl.multiple_of(index * size, size), size)


class Gather:
    def __init__(self, shard, full, stride, offset, columns, shared, place, sems):
        self.shard, self.full, self.shared = shard, full, shared
        self.stride, self.offset, self.columns = stride, offset, columns
        self.rows = shard.shape[0]
        self.unit = self.rows // 16
        chips, chip, lane = place
        self.chip, self.core, self.side = chip, lax.rem(lane, 2), lax.rem(lane // 2, 2)
        self.next_x = chip + 1 - 2 * lax.rem(chip, 2)
        self.next_y = lax.rem(chip + 2, chips)
        self.far = chips - 1 - chip
        self.to_x, self.to_y = (self.next_x, lane), (self.next_y, lane)
        self.to_z = (chip, lane + 2 - 4 * self.side)
        self.to_core = (chip, lane + 1 - 2 * self.core)
        self.send_sem, self.recv_sem = sems

    def whole(self, owner, start, count):
        first = owner * self.stride + self.offset + start
        return self.full.at[pl.ds(pl.multiple_of(first, 16), count), self.columns]

    def units(self, owner, first, count, own=False):
        start = (self.core * 8 + first) * self.unit
        size = count * self.unit
        if own:
            return self.shard.at[pl.ds(pl.multiple_of(start, 16), size), self.columns]
        return self.whole(owner, start, size)

    def hop(self, index):
        side = self.side
        rest = (4 - 3 * side, 3) if self.shared else (4 - 4 * side, 4)
        owner, first, count, device = (
            (self.chip, 4 * side, 4, self.to_x),
            (self.chip, 4 * side, 4, self.to_y),
            (self.chip, *rest, self.to_x),
            (self.chip, *rest, self.to_y),
            (self.next_x, 4 * side, 2, self.to_y),
            (self.next_y, 4 * side + 2, 2, self.to_x),
            (self.far, 4 * side, 4, self.to_z),
            (self.next_x, 0, 8, self.to_core),
            (self.next_y, 0, 8, self.to_core),
            (self.far, 0, 8, self.to_core),
            (self.next_x, 7 * side, 1, self.to_z),
            (self.next_y, 7 * side, 1, self.to_z),
        )[index]
        return remote(
            self.units(owner, first, count, own=index < 4),
            self.units(owner, first, count),
            self.send_sem.at[index],
            self.recv_sem.at[index],
            device,
        )

    def own(self):
        return remote(
            self.shard.at[:, self.columns],
            self.whole(self.chip, 0, self.rows),
            self.send_sem.at[12],
            self.recv_sem.at[12],
            self.to_core,
        )

    def begin(self):
        for index in range(4):
            self.hop(index).start()
        self.own().start()

    def pass_on(self):
        for arrived, onward in ((0, 4), (1, 5)):
            self.hop(arrived).wait_recv()
            self.hop(onward).start()

    def trade(self):
        for arrived, onward in ((2, 10), (3, 11)) if self.shared else ((2, 7), (3, 8)):
            self.hop(arrived).wait_recv()
            self.hop(onward).start()
        self.hop(4).wait_recv()
        self.hop(5).wait_recv()
        self.hop(6).start()

    def cross(self):
        pairs = ((10, 7), (11, 8)) if self.shared else ()
        for arrived, onward in pairs + ((6, 9),):
            self.hop(arrived).wait_recv()
            self.hop(onward).start()

    def arrive(self):
        for index in range(7, 10):
            self.hop(index).wait_recv()
        self.own().wait_recv()

    def drain(self):
        for index in range(12 if self.shared else 10):
            self.hop(index).wait_send()
        self.own().wait_send()


def train_kernel(
    sizes,
    tokens_in,
    cotangent_in,
    begin,
    shard_qkv,
    shard_out,
    shard_in,
    shard_back,
    qv_bias,
    out_bias,
    in_bias,
    back_bias,
    gains,
    shifts,
    down_maps,
    up_maps,
    output,
    input_grad,
    grad_down,
    grad_up,
    full_qkv,
    full_out,
    full_in,
    full_back,
    hidden,
    tokens_low,
    cotangent_low,
    normed,
    low_rank,
    heads_in,
    mixed,
    log_total,
    attended,
    slope,
    tile_in,
    tile_back,
    out_weight,
    qkv_weight,
    heads_out,
    mixture,
    scores,
    activation,
    total,
    gradient,
    grad_attended,
    mix_out,
    mix_in,
    queries,
    mix_heads,
    delta,
    query_sum,
    key_sum,
    value_sum,
    grads_in,
    grads_flat,
    qkv_bias,
    up_low,
    down_low,
    return_out,
    result_low,
    terms,
    landing,
    landing_chips,
    summed,
    tile_sem,
    load_sem,
    heads_send,
    heads_recv,
    mix_send,
    mix_recv,
    move_send,
    move_recv,
    sum_send,
    sum_recv,
    gather_send,
    gather_recv,
):
    chips, lanes = sizes
    chip, lane = lax.axis_index("dp"), lax.axis_index("sp")
    slots, length, model = tokens_in.shape
    layers, rows, hidden_units = slope.shape
    ranks = down_low.shape[0]
    group = lanes // slots
    half, seat = lane // group, lax.rem(lane, group)
    side = seat // 2
    parts = model // group // LANES
    heads = LANES // HEAD_SIZE
    per_tile = TILE // LANES
    tiles_each = model // TILE
    shares = hidden_units // TILE

    def gathers_of(layer):
        model_half, unit_half = 3 * model // 2, hidden_units // 2
        back_rows = shard_back.shape[1]
        back_half = back_rows // 2
        everything = pl.ds(0, model)
        plans = (
            (shard_qkv.at[layer], full_qkv, shard_qkv.shape[1], 0, pl.ds(0, model_half)),
            (shard_qkv.at[layer], full_qkv, shard_qkv.shape[1], 0, pl.ds(model_half, model_half)),
            (shard_out.at[layer], full_out, shard_out.shape[1], 0, everything),
            (shard_in.at[layer], full_in, shard_in.shape[1], 0, pl.ds(0, unit_half)),
            (shard_in.at[layer], full_in, shard_in.shape[1], 0, pl.ds(unit_half, unit_half)),
            (shard_back.at[layer, pl.ds(0, back_half)], full_back, back_rows, 0, everything),
            (
                shard_back.at[layer, pl.ds(back_half, back_half)],
                full_back,
                back_rows,
                back_half,
                everything,
            ),
        )
        return [
            Gather(
                shard,
                full.at[layer],
                stride,
                offset,
                columns,
                index in SHARED[layer],
                (chips, chip, lane),
                (gather_send.at[layer, index], gather_recv.at[layer, index]),
            )
            for index, (shard, full, stride, offset, columns) in enumerate(plans)
        ]

    gathers = [gathers_of(layer) for layer in range(layers)]

    def mates():
        return [lax.rem(seat + 2, group), group - 1 - seat, seat + 1 - 2 * lax.rem(seat, 2)]

    def block_at(index):
        return side * index + (1 - side) * (group - 1 - index)

    def device(mate):
        return (chip, half * group + mate)

    def lane_of(slot):
        return slot * group + lane // 2

    def move_in(kind, source, target):
        def copy(slot):
            return remote(
                source.at[slot],
                target.at[pl.ds(pl.multiple_of(lax.rem(lane, 2) * length, length), length)],
                move_send.at[kind, slot],
                move_recv.at[kind, lax.rem(lane, 2)],
                (chip, lane_of(slot)),
            )

        for slot in range(slots):

            @pl.when(lane_of(slot) != lane)
            def _():
                copy(slot).start()

            @pl.when(lane_of(slot) == lane)
            def _():
                start = pl.multiple_of(lax.rem(lane, 2) * length, length)
                target[pl.ds(start, length)] = source[slot]

    def move_in_wait(kind, source, target, sent):
        for step in range(2):
            sender = 2 * seat + step
            copy = remote(
                source.at[0],
                target.at[pl.ds(step * length, length)],
                move_send.at[kind, step],
                move_recv.at[kind, step],
                (chip, lane_of(step)),
            )
            if sent:

                @pl.when(lane_of(step) != lane)
                def _():
                    copy.wait_send()

            else:

                @pl.when(sender != lane)
                def _():
                    copy.wait_recv()

    def move_out(kind, source, target):
        for step in range(2):
            owner = 2 * seat + step
            part = pl.ds(step * length, length)

            @pl.when(owner != lane)
            def _():
                remote(
                    source.at[part],
                    target.at[half],
                    move_send.at[kind, step],
                    move_recv.at[kind, half],
                    (chip, owner),
                ).start()

            @pl.when(owner == lane)
            def _():
                target[half] = source[part]

    def move_out_wait(kind, source, target, sent):
        for step in range(2):
            owner = 2 * seat + step
            copy = remote(
                source.at[pl.ds(step * length, length)],
                target.at[step],
                move_send.at[kind, step],
                move_recv.at[kind, step],
                (chip, owner),
            )
            if sent:

                @pl.when(owner != lane)
                def _():
                    copy.wait_send()

            else:

                @pl.when(lane_of(step) != lane)
                def _():
                    copy.wait_recv()

    def heads_copy(part, mate, target, owner):
        return remote(
            heads_out.at[mate, part],
            target.at[owner, part],
            heads_send.at[part, mate],
            heads_recv.at[part, owner],
            device(mate),
        )

    def mix_copy(part, mate, source, target, owner):
        return remote(
            source.at[part, mate],
            target.at[owner, part],
            mix_send.at[part, mate],
            mix_recv.at[part, owner],
            device(mate),
        )

    def allowed_pairs(key_block, query_block, diagonal):
        place = lax.broadcasted_iota(jnp.int32, (rows, heads * rows), 0)
        begin_row = begin[pl.ds(half, 1), at_columns(query_block, rows)]
        begin_row = jnp.concatenate([begin_row] * heads, 1) - key_block * rows
        allowed = place >= begin_row
        if diagonal:
            column = lax.broadcasted_iota(jnp.int32, (1, heads * rows), 1)
            allowed = allowed & (place <= lax.rem(column, rows))
        return allowed

    def load_params(layer):
        scale = ADAPTER_ALPHA / (ranks // 2)
        down = jnp.concatenate([down_maps[layer, 0], down_maps[layer, 1]], 0)
        down_low[...] = down.astype(LOW)
        blank = jnp.zeros((ranks // 2, model), FULL)
        up_query = jnp.concatenate([scale * up_maps[layer, 0], blank], 0)
        up_value = jnp.concatenate([blank, scale * up_maps[layer, 1]], 0)
        up_low[:, :model] = up_query.astype(LOW)
        up_low[:, model : 2 * model] = jnp.zeros((ranks, model), LOW)
        up_low[:, 2 * model :] = up_value.astype(LOW)

    def forward(layer, following):
        get_qkv_a, get_qkv_b, get_out, get_in_a, get_in_b, get_back_a, get_back_b = gathers[layer]
        if layer == 0:
            get_qkv_a.begin()
            move_in(0, tokens_in, tokens_low)
            get_qkv_a.pass_on()
            get_qkv_b.begin()
        load_params(layer)
        qkv_bias[0:1, :model] = qv_bias[layer, 0:1]
        qkv_bias[0:1, model : 2 * model] = jnp.zeros((1, model), FULL)
        qkv_bias[0:1, 2 * model :] = qv_bias[layer, 1:2]
        qkv_bias[1:2, :model] = jnp.full((1, model), HEAD_SIZE ** (-0.5), FULL)
        qkv_bias[1:2, model:] = jnp.ones((1, 2 * model), FULL)
        if layer == 0:
            get_qkv_a.trade()
            move_in_wait(0, tokens_in, tokens_low, False)
            hidden[0] = tokens_low[...].astype(FULL)
        unit, _ = normalize(hidden[layer])
        normed[layer] = (unit * gains[layer, 0:1] + shifts[layer, 0:1]).astype(LOW)
        low_rank[layer] = dot_nt(normed[layer], down_low[...])
        if layer > 0:
            for part in range(parts):
                for mate in mates():
                    heads_copy(part, mate, heads_in.at[layer - 1], seat).wait_send()
        get_qkv_b.pass_on()
        get_out.begin()
        get_in_a.begin()
        get_qkv_a.cross()

        def qkv_run(first_tile, count):
            def copies(index, slot):
                columns = at_columns(first_tile + index, TILE)
                return [
                    pltpu.make_async_copy(
                        full_qkv.at[layer, :, columns], tile_in.at[slot], tile_sem.at[0, slot]
                    )
                ]

            def body(index, slot):
                tile = first_tile + index
                columns = at_columns(tile, TILE)
                value = dot_nn(normed[layer], tile_in[slot])
                value += dot_nn(low_rank[layer].astype(LOW), up_low[:, columns])
                value += qkv_bias[0:1, columns]
                value = (value * qkv_bias[1:2, columns]).astype(LOW)
                kind = tile // tiles_each
                first = lax.rem(tile, tiles_each) * (per_tile // parts)
                for step in range(per_tile):
                    heads_out[first + step // parts, step % parts, kind] = value[
                        :, step * LANES : (step + 1) * LANES
                    ]

            prime(count, copies)
            stream(count, copies, body)

        tile_count = 3 * tiles_each
        get_qkv_a.arrive()
        qkv_run(0, tile_count // 2)
        get_qkv_b.trade()
        get_qkv_b.cross()
        get_qkv_b.arrive()
        qkv_run(tile_count // 2, tile_count // 2)
        arrivals = heads_in.at[layer]
        for part in range(parts):
            for mate in mates():
                heads_copy(part, mate, arrivals, seat).start()
            heads_in[layer, seat, part] = heads_out[seat, part]
        get_out.pass_on()
        get_in_a.pass_on()
        get_in_b.begin()

        def attend(part):
            def query_step(index, carry):
                query_block = block_at(index)
                query_heads = split_heads(heads_in[layer, query_block, part, 0])

                def score_step(key_block, best, diagonal=False):
                    found = dot_nt(heads_in[layer, key_block, part, 1], query_heads)
                    allowed = allowed_pairs(key_block, query_block, diagonal)
                    found = jnp.where(allowed, found, MASKED)
                    scores[key_block] = found
                    return jnp.maximum(best, jnp.max(found, 0, keepdims=True))

                lowest = jnp.full((1, heads * rows), MASKED, FULL)
                best = lax.fori_loop(0, query_block, score_step, lowest)
                best = score_step(query_block, best, True)

                def mix_step(key_block, carried):
                    sums, mix = carried
                    raised = jnp.exp(scores[key_block] - best)
                    sums = sums + jnp.sum(raised, 0, keepdims=True)
                    return sums, mix + dot_tn(heads_in[layer, key_block, part, 2], raised.astype(LOW))

                nothing = jnp.zeros((1, heads * rows), FULL), jnp.zeros((LANES, heads * rows), FULL)
                sums, mix = lax.fori_loop(0, query_block + 1, mix_step, nothing)
                log_total[layer, part, query_block] = best + jnp.log(sums)
                mixed[layer, part, query_block] = join_heads(mix * (1.0 / sums), rows).astype(LOW)

                @pl.when(query_block != seat)
                def _():
                    mix_copy(part, query_block, mixed.at[layer], mixture, seat).start()

                return carry

            lax.fori_loop(0, group, query_step, 0)
            mixture[seat, part] = mixed[layer, part, seat]

        load = pltpu.make_async_copy(full_out.at[layer], out_weight, load_sem.at[0])
        for part in range(parts):
            for mate in mates():
                heads_copy(part, mate, arrivals, mate).wait_recv()
            attend(part)
            if part == 0:
                get_out.trade()
                get_in_b.pass_on()
                get_back_a.begin()
                get_in_a.trade()
        get_out.cross()
        get_back_a.pass_on()
        get_back_b.begin()
        get_in_b.trade()
        get_in_a.cross()
        get_out.arrive()
        load.start()

        for part in range(parts):
            for mate in mates():
                mix_copy(part, mate, mixed.at[layer], mixture, mate).wait_recv()
        load.wait()
        total[...] = hidden[layer] + out_bias[layer : layer + 1]

        def out_body(index, carry):
            joined = jnp.concatenate([mixture[index, part] for part in range(parts)], 1)
            start = pl.multiple_of(index * parts * LANES, parts * LANES)
            total[...] += dot_nn(joined, out_weight[pl.ds(start, parts * LANES)])
            return carry

        lax.fori_loop(0, group, out_body, 0)
        attended[layer] = total[...]
        unit, _ = normalize(total[...])
        second = (unit * gains[layer, 1:2] + shifts[layer, 1:2]).astype(LOW)

        def in_run(first_tile, count):
            def copies(index, slot):
                columns = at_columns(first_tile + index, TILE)
                return [
                    pltpu.make_async_copy(
                        full_in.at[layer, :, columns], tile_in.at[slot], tile_sem.at[0, slot]
                    )
                ]

            def body(index, slot):
                tile = first_tile + index
                columns = at_columns(tile, TILE)
                value = dot_nn(second, tile_in[slot]) + in_bias[layer : layer + 1, columns]
                lifted, steepness = gelu_and_slope(value)
                slope[layer, :, columns] = steepness.astype(LOW)
                activation[tile] = lifted.astype(LOW)

            prime(count, copies)
            stream(count, copies, body)

        get_back_a.trade()
        get_in_a.arrive()
        in_run(0, shares // 2)
        get_back_b.pass_on()
        if following is not None:
            following[0].begin()
        get_in_b.cross()
        get_in_b.arrive()
        in_run(shares // 2, shares // 2)
        if following is not None:
            move_in(1, cotangent_in, cotangent_low)
        get_back_a.cross()
        for part in range(parts):
            for mate in mates():
                mix_copy(part, mate, mixed.at[layer], mixture, seat).wait_send()

    def back_copies(layer, first):
        def copies(index, slot):
            return [
                pltpu.make_async_copy(
                    full_back.at[layer, at_columns(grad_tile(first + index), TILE)],
                    tile_back.at[slot],
                    tile_sem.at[1, slot],
                )
            ]

        return copies

    def back_run(layer, first, count):
        def body(index, slot):
            total[...] += dot_nn(activation[grad_tile(first + index)], tile_back[slot])

        stream(count, back_copies(layer, first), body)

    def grad_tile(index):
        pairs = shares // 2
        return 2 * lax.rem(index, pairs) + index // pairs

    def grad_copies(layer, first):
        def copies(index, slot):
            columns = at_columns(grad_tile(first + index), TILE)
            return [
                pltpu.make_async_copy(
                    full_in.at[layer, :, columns], tile_in.at[slot], tile_sem.at[0, slot]
                ),
                pltpu.make_async_copy(
                    full_back.at[layer, columns], tile_back.at[slot], tile_sem.at[1, slot]
                ),
            ]

        return copies

    def grad_run(layer, low_gradient, first, count):
        def body(index, slot):
            columns = at_columns(grad_tile(first + index), TILE)
            grad_act = dot_nt(low_gradient, tile_back[slot])
            grad_pre = (slope[layer, :, columns].astype(FULL) * grad_act).astype(LOW)
            total[...] += dot_nt(grad_pre, tile_in[slot])

        stream(count, grad_copies(layer, first), body)

    def backward(layer, last):
        load_out = pltpu.make_async_copy(full_out.at[layer], out_weight, load_sem.at[0])
        load_qkv = pltpu.make_async_copy(full_qkv.at[layer], qkv_weight, load_sem.at[1])
        if last:
            load_out.start()
        load_qkv.start()
        load_params(layer)
        low_gradient = gradient[...].astype(LOW)
        total[...] = jnp.zeros_like(total)
        if last:
            get_back_a, get_back_b = gathers[layer][5:7]
            get_back_b.trade()
            get_back_a.arrive()
            prime(shares // 2, grad_copies(layer, 0))
            grad_run(layer, low_gradient, 0, shares // 2)
            get_back_b.cross()
            get_back_b.arrive()
            prime(shares // 2, grad_copies(layer, shares // 2))
            grad_run(layer, low_gradient, shares // 2, shares // 2)
        else:
            grad_run(layer, low_gradient, 0, shares)
        grad_attended[...] = gradient[...] + norm_backward(
            attended[layer], gains[layer, 1:2], total[...]
        )
        low_attended = grad_attended[...].astype(LOW)
        load_out.wait()
        if last:
            prime(shares, back_copies(layer, 0))
        else:
            for part in range(parts):
                for mate in mates():
                    mix_copy(part, mate, mix_out, mix_in, seat).wait_send()

        for mate in mates() + [seat]:
            start = pl.multiple_of(mate * parts * LANES, parts * LANES)
            value = dot_nt(low_attended, out_weight[pl.ds(start, parts * LANES)]).astype(LOW)
            for part in range(parts):
                mix_out[part, mate] = value[:, part * LANES : (part + 1) * LANES]
        for part in range(parts):
            for mate in mates():
                mix_copy(part, mate, mix_out, mix_in, seat).start()
            mix_in[seat, part] = mix_out[part, seat]
            for mate in mates():
                heads_copy(part, mate, grads_in, seat).wait_send()
        if last:
            total[...] = attended[layer] + back_bias[layer : layer + 1]
            back_run(layer, 0, shares)
            result_low[...] = total[...].astype(LOW)
        if layer > 0:
            pltpu.make_async_copy(full_out.at[layer - 1], out_weight, load_sem.at[0]).start()
            prime(shares, grad_copies(layer - 1, 0))

        def attend(part):
            def prepare(block, carry):
                queries[block] = split_heads(heads_in[layer, block, part, 0])
                grads = split_heads(mix_in[block, part])
                mix_heads[block] = grads
                mix = jnp.concatenate([mixed[layer, part, block]] * heads, 0)
                product = grads.astype(FULL) * mix.astype(FULL)
                delta[block] = jnp.sum(product.T, 0, keepdims=True)
                query_sum[block] = jnp.zeros_like(query_sum[block])
                key_sum[block] = jnp.zeros_like(key_sum[block])
                value_sum[block] = jnp.zeros_like(value_sum[block])
                return carry

            lax.fori_loop(0, group, prepare, 0)

            def pair_step(key_block, query_block, diagonal):
                keys = heads_in[layer, key_block, part, 1]
                values = heads_in[layer, key_block, part, 2]
                query_heads = queries[query_block]
                grad_heads = mix_heads[query_block]
                found = dot_nt(keys, query_heads)
                raised = jnp.exp(found - log_total[layer, part, query_block])
                allowed = allowed_pairs(key_block, query_block, diagonal)
                weights = jnp.where(allowed, raised, 0.0)
                value_sum[key_block] += dot_nn(weights.astype(LOW), grad_heads)
                grad_weights = dot_nt(values, grad_heads)
                grad_scores = weights * (grad_weights - delta[query_block])
                grad_scores = grad_scores.astype(LOW)
                key_sum[key_block] += dot_nn(grad_scores, query_heads)
                query_sum[query_block] += dot_tn(keys, grad_scores)

            def block_step(index, carry):
                block = block_at(index)
                pair_step(block, block, True)

                def inner_step(step, inner):
                    key_block = block - (1 - side) * step
                    pair_step(key_block, block + side * step, False)
                    return inner

                lax.fori_loop(1, group - index, inner_step, 0)
                out = join_heads(query_sum[block], rows).astype(LOW)
                heads_out[block, part, 0] = out * jnp.asarray(HEAD_SIZE ** (-0.5), LOW)
                heads_out[block, part, 1] = key_sum[block].astype(LOW)
                heads_out[block, part, 2] = value_sum[block].astype(LOW)

                @pl.when(block != seat)
                def _():
                    heads_copy(part, block, grads_in, seat).start()

                return carry

            lax.fori_loop(0, group, block_step, 0)
            grads_in[seat, part] = heads_out[seat, part]

        for part in range(parts):
            for mate in mates():
                mix_copy(part, mate, mix_out, mix_in, mate).wait_recv()
            attend(part)
        def part_columns(source, part, kind):
            starts = [kind * model + (owner * parts + part) * LANES for owner in range(group)]
            return jnp.concatenate([source[:, start : start + LANES] for start in starts], 1)

        load_qkv.wait()
        rank = ranks // 2
        low_values = (low_rank[layer] * (ADAPTER_ALPHA / rank)).astype(LOW)
        grad_low = jnp.zeros((rows, ranks), FULL)
        total[...] = jnp.zeros_like(total)
        for part in range(parts):
            for mate in mates():
                heads_copy(part, mate, grads_in, mate).wait_recv()
            for kind in range(3):
                joined = [grads_in[owner, part, kind] for owner in range(group)]
                grads_flat[kind] = jnp.concatenate(joined, 1)
            for entry, kind in ((2, 0), (3, 2)):
                grad_low += dot_nt(grads_flat[kind], part_columns(up_low, part, kind))
                found = dot_tn(low_values, grads_flat[kind])
                found = found[:rank] if kind == 0 else found[rank:]
                for owner in range(group):
                    start = (owner * parts + part) * LANES
                    terms[4 * layer + entry, :, start : start + LANES] = found[
                        :, owner * LANES : (owner + 1) * LANES
                    ]
            if part == parts - 1:
                grad_low = grad_low.astype(LOW)
                down_terms = dot_tn(grad_low, normed[layer])
                terms[4 * layer] = down_terms[:rank]
                terms[4 * layer + 1] = down_terms[rank:]
                if not last:
                    sum_begin()
                total[...] += dot_nn(grad_low, down_low[...])
            for kind in range(3):
                total[...] += dot_nt(grads_flat[kind], part_columns(qkv_weight, part, kind))
        if last:
            move_out(2, result_low, output)
        gradient[...] = grad_attended[...] + norm_backward(
            hidden[layer], gains[layer, 0:1], total[...]
        )

    def sum_lanes():
        return [
            remote(
                terms.at[lax.rem(lane + step, lanes)],
                landing.at[lane],
                sum_send.at[0, step],
                sum_recv.at[0, step],
                (chip, lax.rem(lane + step, lanes)),
            )
            for step in range(1, lanes)
        ]

    def sum_spread():
        return [
            remote(
                summed.at[lane],
                summed.at[lane],
                sum_send.at[1, step],
                sum_recv.at[1, step],
                (chip, lax.rem(lane + step, lanes)),
            )
            for step in range(1, lanes)
        ]

    def sum_chips():
        return [
            remote(
                summed,
                landing_chips.at[chip],
                sum_send.at[2, step],
                sum_recv.at[2, step],
                (lax.rem(chip + step, chips), lane),
            )
            for step in range(1, chips)
        ]

    def sum_begin():
        for copy in sum_lanes():
            copy.start()
        landing[lane] = terms[lane]

    def sum_lanes_finish():
        for copy in sum_lanes():
            copy.wait()
        summed[lane] = jnp.sum(landing[...], axis=0)
        for copy in sum_spread():
            copy.start()

    def sum_finish():
        for copy in sum_spread():
            copy.wait()
        for copy in sum_chips():
            copy.start()
        landing_chips[chip] = summed[...]
        for copy in sum_chips():
            copy.wait()
        scale = 1.0 / math.sqrt(slots * chips * length * lanes)
        for layer in range(layers):
            for kind in range(2):
                for grads, entry in ((grad_down, kind), (grad_up, 2 + kind)):
                    terms_of = landing_chips[:, 4 * layer + entry]
                    grads[layer, kind] = jnp.sum(terms_of, axis=0) * scale

    barrier = pltpu.get_barrier_semaphore()
    friends = [(chip, lax.rem(lane + step, lanes)) for step in range(1, lanes)]
    friends += [(lax.rem(chip + step, chips), lane) for step in range(1, chips)]
    for friend in friends:
        pl.semaphore_signal(barrier, inc=1, device_id=friend, device_id_type=MESH)
    pl.semaphore_wait(barrier, len(friends))

    for layer in range(layers):
        last = layer + 1 == layers
        forward(layer, None if last else gathers[layer + 1])
        if not last:
            total[...] = attended[layer] + back_bias[layer : layer + 1]
            get_back_a, get_back_b = gathers[layer][5:7]
            get_back_a.arrive()
            prime(shares // 2, back_copies(layer, 0))
            back_run(layer, 0, shares // 2)
            gathers[layer + 1][0].pass_on()
            gathers[layer + 1][1].begin()
            get_back_b.trade()
            get_back_b.cross()
            get_back_b.arrive()
            prime(shares // 2, back_copies(layer, shares // 2))
            back_run(layer, shares // 2, shares // 2)
            hidden[layer + 1] = total[...]
            gathers[layer + 1][0].trade()
    move_in_wait(1, cotangent_in, cotangent_low, False)
    gradient[...] = cotangent_low[...].astype(FULL)
    for layer in reversed(range(layers)):
        last = layer + 1 == layers
        backward(layer, last)
    return_out[...] = gradient[...].astype(LOW)
    sum_lanes_finish()
    move_out(3, return_out, input_grad)
    sum_finish()
    move_out_wait(2, result_low, output, False)
    move_out_wait(3, return_out, input_grad, False)

    move_in_wait(0, tokens_in, tokens_low, True)
    move_in_wait(1, cotangent_in, cotangent_low, True)
    move_out_wait(2, result_low, output, True)
    move_out_wait(3, return_out, input_grad, True)
    for layer_gathers in gathers:
        for gather in layer_gathers:
            gather.drain()
    for part in range(parts):
        for mate in mates():
            mix_copy(part, mate, mix_out, mix_in, seat).wait_send()
            heads_copy(part, mate, grads_in, seat).wait_send()


def widen_kernel(*refs):
    for source, target in zip(refs[:4], refs[4:]):
        target[...] = source[...].astype(FULL)


def fast_body(sizes, *arrays):
    chips, lanes = sizes
    tokens, _, _, *shards = arrays[:7]
    slots, length, model = tokens.shape
    layers, kinds, rank, _ = arrays[-1].shape
    hidden_units = shards[2].shape[2]
    group = lanes // slots
    rows, ranks = slots * length, kinds * rank
    parts, heads = model // group // LANES, LANES // HEAD_SIZE
    vmem = pl.BlockSpec(memory_space=pltpu.VMEM)
    anywhere = pl.BlockSpec(memory_space=pl.ANY)
    shape, dma = jax.ShapeDtypeStruct, pltpu.SemaphoreType.DMA
    scratch = [
        ((layers, rows, model), FULL),
        ((rows, model), LOW),
        ((rows, model), LOW),
        ((layers, rows, model), LOW),
        ((layers, rows, ranks), FULL),
        ((layers, group, parts, 3, rows, LANES), LOW),
        ((layers, parts, group, rows, LANES), LOW),
        ((layers, parts, group, 1, heads * rows), FULL),
        ((layers, rows, model), FULL),
        ((layers, rows, hidden_units), LOW),
        ((DEPTH, model, TILE), LOW),
        ((DEPTH, TILE, model), LOW),
        ((model, model), LOW),
        ((model, 3 * model), LOW),
        ((group, parts, 3, rows, LANES), LOW),
        ((group, parts, rows, LANES), LOW),
        ((group, rows, heads * rows), FULL),
        ((hidden_units // TILE, rows, TILE), LOW),
        ((rows, model), FULL),
        ((rows, model), FULL),
        ((rows, model), FULL),
        ((parts, group, rows, LANES), LOW),
        ((group, parts, rows, LANES), LOW),
        ((group, heads * rows, LANES), LOW),
        ((group, heads * rows, LANES), LOW),
        ((group, 1, heads * rows), FULL),
        ((group, LANES, heads * rows), FULL),
        ((group, rows, LANES), FULL),
        ((group, rows, LANES), FULL),
        ((group, parts, 3, rows, LANES), LOW),
        ((3, rows, group * LANES), LOW),
        ((2, 3 * model), FULL),
        ((ranks, 3 * model), LOW),
        ((ranks, model), LOW),
        ((rows, model), LOW),
        ((rows, model), LOW),
        ((lanes, rank, model), FULL),
        ((lanes, rank, model), FULL),
        ((chips, lanes, rank, model), FULL),
        ((lanes, rank, model), FULL),
    ]
    semaphores = [
        (2, DEPTH),
        (2,),
        (parts, group),
        (parts, group),
        (parts, group),
        (parts, group),
        (4, 2),
        (4, 2),
        (3, lanes),
        (3, lanes),
        (layers, 7, 13),
        (layers, 7, 13),
    ]
    results = pl.pallas_call(
        partial(train_kernel, sizes),
        out_shape=(
            shape((slots, length, model), LOW),
            shape((slots, length, model), LOW),
            shape((layers, kinds, rank, model), FULL),
            shape((layers, kinds, rank, model), FULL),
        )
        + tuple(shape((layers, chips * part.shape[1], part.shape[2]), LOW) for part in shards),
        in_specs=[vmem] * 3 + [anywhere] * 4 + [vmem] * 8,
        out_specs=(vmem,) * 4 + (anywhere,) * 4,
        scratch_shapes=[pltpu.VMEM(*entry) for entry in scratch]
        + [dma(entry) for entry in semaphores],
        name="train",
        compiler_params=pltpu.CompilerParams(
            collective_id=0, has_side_effects=True, vmem_limit_bytes=VMEM_LIMIT
        ),
    )(*arrays)
    return pl.pallas_call(
        widen_kernel,
        out_shape=(
            shape((slots, length, model), FULL),
            shape((slots, length, model), FULL),
            shape((layers, kinds, rank, model), FULL),
            shape((layers, kinds, rank, model), FULL),
        ),
        in_specs=[vmem] * 4,
        out_specs=(vmem,) * 4,
        name="widen",
    )(*results[:4])


def solution(mesh):
    chips, lanes = sizes = tuple(mesh.devices.shape)
    fast = sizes == (4, 8)
    token_axes = "sp" if fast else SP
    if not fast:
        mesh = Mesh(mesh.devices.reshape(chips, lanes // 2, 2), ("dp",) + SP)
    tokens = P("dp", token_axes, None)
    weights = P(None, "dp", None)
    return jax.shard_map(
        partial(fast_body, sizes) if fast else body,
        mesh=mesh,
        in_specs=(tokens, tokens, P("dp", None)) + (weights,) * 4 + (P(),) * 8,
        out_specs=(tokens, tokens, P(), P()),
        check_vma=False,
    )
```
